32 devices in a mesh: seq: 4 (over x, core), fsdp: 8 (over z, y).
Axes of the slice: x: 2, y: 2, z: 4, core: 2. Of those that a mesh axis runs over, the one named last changes fastest.
Arguments:
- tokens: bfloat16 [64, 256, 512], P('fsdp', 'seq'), may hold values from -6 to 6
- pad_mask: int32 [64, 256], P('fsdp', 'seq'), may hold values from 0 to 1, as said below
- routes: int32 [64, 256, 2], P('fsdp', 'seq'), may hold values from 0 to 3, all different within a row
- ln1_gain: float32 [512], P('fsdp'), may hold values from 0.5 to 1.5
- w_qkv: float32 [512, 1536], P('fsdp'), may hold values from -0.25 to 0.25
- w_proj: float32 [512, 512], P('fsdp'), may hold values from -1 to 1
- ln2_gain: float32 [512], P('fsdp'), may hold values from 0.5 to 1.5
- w_router: float32 [512, 4], P('fsdp'), may hold values from -0.1875 to 0.1875
- exp_in: float32 [2048, 4, 512], P('fsdp'), may hold values from -0.25 to 0.25
- exp_out: float32 [2048, 4, 512], P('fsdp'), may hold values from -0.375 to 0.375
- cotangent: bfloat16 [64, 256, 512], P('fsdp', 'seq'), may hold values from -6 to 6
Outputs:
- block_out: bfloat16 [64, 256, 512], P('fsdp', 'seq')
- grad_tokens: float32 [64, 256, 512], P('fsdp', 'seq')
- grad_ln1_gain: float32 [512], P('fsdp')
- grad_w_qkv: float32 [512, 1536], P('fsdp')
- grad_w_proj: float32 [512, 512], P('fsdp')
- grad_ln2_gain: float32 [512], P('fsdp')
- grad_w_router: float32 [512, 4], P('fsdp')
- grad_exp_in: float32 [2048, 4, 512], P('fsdp')
- grad_exp_out: float32 [2048, 4, 512], P('fsdp')
The draws below stay inside these ranges and needn't reach their ends.
Inputs may be any that keep to these rules, and one draw needn't show every extreme that they name: pad_mask is 1 on the first tokens of each image and 0 after them; at least 192 tokens of every image are real, and image 0 has all 256. `routes`: the two experts of a token differ.
All inputs are finite; a program needn't handle non-finite values.
Results may differ from the reference program's by a relative error of at most 0.014.
Values may be sent and summed in bfloat16 or wider, within the bound.
No kernel may reach another device: no remote copies, remote signals or barrier semaphores. Data moves between devices by JAX's collectives and lax.ppermute only.
A program may use at most 320 MiB of HBM per device.

```python
import jax
import jax.numpy as jnp
from jax import lax

D = 512
HEADS = 8
FF = 2048
EXPERTS = 4
TOP = 2
LEN = 256
IMAGES = 64


def draw_pad_mask(key, part):
    lengths = jax.random.randint(key, (IMAGES,), LEN - LEN // 4, LEN + 1)
    image_ids = jnp.arange(IMAGES, dtype=jnp.int32)
    lengths = jnp.where(image_ids == 0, LEN, lengths)
    places = jnp.arange(LEN, dtype=jnp.int32)
    return (places[None, :] < lengths[:, None]).astype(jnp.int32)


def level_of(stream_key, extent, cuts, least, top_value):
    loudness = 1.0
    for dim, shards_of in cuts:
        draws = jax.random.uniform(jax.random.fold_in(jax.random.fold_in(stream_key, 6), dim), (shards_of,), jnp.float32, least / len(cuts), top_value / len(cuts))
        loudness = loudness * jnp.repeat(jnp.exp(draws), extent[dim] // shards_of).reshape((-1,) + (1,) * (len(extent) - 1 - dim))
    return loudness


def distinct(key, rows, number_of, top, lift):
    order = jax.random.permutation(jax.random.fold_in(key, 1), number_of)
    favour = order
    for power in range(3):
        favour = favour * favour // number_of
    favour = favour * lift // number_of
    chance = jax.random.randint(jax.random.fold_in(key, 2), (rows, number_of), 0, 4096) + favour
    sure = jax.random.permutation(jax.random.fold_in(key, 3), rows)[jnp.arange(number_of) % rows]
    chance = jnp.where(jnp.arange(rows)[:, None] == sure[None, :], 1 << 14, chance)
    merit = chance * number_of + jnp.arange(number_of)
    return lax.top_k(merit.astype(jnp.int32), top)[1].astype(jnp.int32)


def normal_values(own_key, shape, deviation, most, split=(), kind=jnp.bfloat16):
    array = jax.random.normal(own_key, shape, jnp.float32) * deviation
    if len(split) > 0:
        array = level_of(own_key, shape, split, -0.22, 0.18) * array
    return jnp.clip(array, min=-most, max=most).astype(kind)


def setup_inputs(seed: int = 0) -> dict:
    key_of = jax.random.split(jax.random.key(seed), 12)
    return {
        "tokens": normal_values(key_of[0], (IMAGES, LEN, D), 1.0, 6.0, ((0, 8), (1, 4))),
        "pad_mask": draw_pad_mask(jax.random.fold_in(key_of[11], 71), 0),
        "routes": distinct(key_of[2], IMAGES * LEN, EXPERTS, TOP, 4096).reshape((IMAGES, LEN, TOP)),
        "ln1_gain": jnp.clip(1.0 + 0.1 * jax.random.normal(key_of[3], (D,), jnp.float32), 0.5, 1.5),
        "w_qkv": normal_values(key_of[4], (D, 3 * D), D ** -0.5, 0.25, ((0, 8),), jnp.float32),
        "w_proj": normal_values(key_of[5], (D, D), (D // 16) ** -0.5, 1.0, ((0, 8),), jnp.float32),
        "ln2_gain": jnp.clip(1.0 + 0.1 * jax.random.normal(key_of[6], (D,), jnp.float32), 0.5, 1.5),
        "w_router": normal_values(key_of[7], (D, EXPERTS), (2 * D) ** -0.5, 0.1875, ((0, 8),), jnp.float32),
        "exp_in": normal_values(key_of[8], (FF, EXPERTS, D), D ** -0.5, 0.25, ((0, 8),), jnp.float32),
        "exp_out": normal_values(key_of[9], (FF, EXPERTS, D), (FF // 8) ** -0.5, 0.375, ((0, 8),), jnp.float32),
        "cotangent": normal_values(key_of[10], (IMAGES, LEN, D), 1.0, 6.0, ((0, 8), (1, 4))),
    }


@jax.custom_vjp
def low(v):
    return lax.optimization_barrier(v.astype(jnp.bfloat16)).astype(jnp.float32)

@jax.custom_vjp
def low_back(v):
    return v

def low_keep(v):
    return (low(v), None)

def low_pass(kept, grad):
    return (grad,)

def back_keep(v):
    return (v, None)

def back_low(kept, grad):
    return (low(grad),)
low.defvjp(low_keep, low_pass)
low_back.defvjp(back_keep, back_low)
HIGHEST_PREC = lax.Precision.HIGHEST
epsilon = 1e-06

def layer_norm(values, gain_vec):
    average = lax.optimization_barrier(jnp.mean(values, axis=-1, keepdims=True))
    centred = values - average
    variance = lax.optimization_barrier(jnp.mean(centred * centred, axis=-1, keepdims=True))
    return centred * lax.rsqrt(variance + epsilon) * gain_vec

def group_block(rounded, group_tokens, group_keep, group_chosen):
    gain_one, qkv_weight, proj_weight, gain_two, router_weight, in_weight, out_weight = rounded
    images, full_len, width = group_tokens.shape
    head_size = width // HEADS
    score_scale = 1.0 / jnp.sqrt(jnp.float32(head_size))
    keep_col = group_keep[..., None]
    start = group_tokens * keep_col
    normed_one = low(layer_norm(start, gain_one))
    qkv_proj = jnp.einsum('bsd,de->bse', normed_one, qkv_weight, precision=HIGHEST_PREC)
    qkv_proj = low(low_back(qkv_proj)).reshape(images, full_len, 3, HEADS, head_size)
    queries = qkv_proj[:, :, 0]
    keys_here = qkv_proj[:, :, 1]
    values_here = qkv_proj[:, :, 2]
    scores = low_back(jnp.einsum('bqhc,bkhc->bhqk', queries, keys_here, precision=HIGHEST_PREC) * score_scale)
    scores = jnp.where(group_keep[:, None, None, :] > 0.5, scores, jnp.float32(-1e+30))
    attn_weights = low(jax.nn.softmax(scores, axis=-1))
    context = jnp.einsum('bhqk,bkhc->bqhc', attn_weights, values_here, precision=HIGHEST_PREC)
    context = low(low_back(context.reshape(images, full_len, width)))
    attn_out = low_back(jnp.einsum('bsd,de->bse', context, proj_weight, precision=HIGHEST_PREC))
    residual = start + attn_out * keep_col
    normed_two = low(layer_norm(residual, gain_two))
    logits = jnp.einsum('bsd,de->bse', normed_two, router_weight, precision=HIGHEST_PREC)
    gate_vals = jax.nn.softmax(logits, axis=-1) * group_chosen
    hidden = low_back(jnp.einsum('bsd,fed->bsef', normed_two, in_weight, precision=HIGHEST_PREC))
    active = low(jax.nn.gelu(hidden, approximate=False))
    expert_outs = low_back(jnp.einsum('bsef,fed->bsed', active, out_weight, precision=HIGHEST_PREC))
    moe_out = lax.optimization_barrier(jnp.sum(gate_vals[..., None] * expert_outs, axis=2))
    return residual + moe_out * keep_col

def reference(tokens, pad_mask, routes, ln1_gain, w_qkv, w_proj, ln2_gain, w_router, exp_in, exp_out, cotangent):
    keep_rows = pad_mask.astype(jnp.float32)
    expert_ids = jnp.arange(EXPERTS, dtype=jnp.int32)
    chosen = (routes[..., 0:1] == expert_ids).astype(jnp.float32) + (routes[..., 1:2] == expert_ids).astype(jnp.float32)
    group_size = max(1, min(IMAGES, 4096 // LEN))
    while IMAGES % group_size != 0:
        group_size = group_size - 1
    groups = IMAGES // group_size
    keep_groups = keep_rows.reshape(groups, group_size, LEN)
    chosen_groups = chosen.reshape(groups, group_size, LEN, EXPERTS)

    def forward(inputs, params):
        rounded = tuple((low(member) for member in params))

        def one_group(group_parts):
            return group_block(rounded, group_parts[0], group_parts[1], group_parts[2])
        outputs = lax.map(jax.checkpoint(one_group), (inputs.reshape(groups, group_size, LEN, D), keep_groups, chosen_groups))
        return outputs.reshape(IMAGES, LEN, D)
    params = (ln1_gain, w_qkv, w_proj, ln2_gain, w_router, exp_in, exp_out)
    result, pullback = jax.vjp(forward, tokens.astype(jnp.float32), params)
    grad_tokens, weight_grads = pullback(cotangent.astype(jnp.float32))
    return (result.astype(jnp.bfloat16), grad_tokens, weight_grads[0], weight_grads[1], weight_grads[2], weight_grads[3], weight_grads[4], weight_grads[5], weight_grads[6])
```

```python
import jax
import jax.numpy as jnp
from jax import lax
from jax.experimental import pallas as pl
from jax.experimental.pallas import tpu as pltpu
from jax.sharding import PartitionSpec as P

BF = jnp.bfloat16
F32 = jnp.float32
HEADS = 8
HEAD = 64
EPS = 1e-06
SQRT_HALF = 0.7071067811865476
INV_ROOT_TWO_PI = 0.3989422804014327
SMALL = 128
CODE_ROWS = 16
NT = (((1,), (1,)), ((), ()))
TN = (((0,), (0,)), ((), ()))
MIB = 1 << 20


def dot(a, b, dims=(((1,), (0,)), ((), ()))):
    return lax.dot_general(a, b, dims, preferred_element_type=F32)


def ring_order(n):
    return [2 * i for i in range(n // 2)] + [2 * i + 1 for i in reversed(range(n // 2))]


def ring_pairs(orders):
    fw = []
    for order in orders:
        n = len(order)
        fw += [(order[i], order[(i + 1) % n]) for i in range(n)]
    return fw, [(b, a) for a, b in fw]


def send(x, axis, pairs):
    return lax.ppermute(x, axis, pairs)


def add_low(a, b):
    return (a.astype(F32) + b.astype(F32)).astype(BF)


def norm(v):
    c = v - jnp.mean(v, axis=-1, keepdims=True)
    inv = lax.rsqrt(jnp.mean(c * c, axis=-1, keepdims=True) + EPS)
    return c * inv, inv


def norm_back(u, hat, inv):
    return inv * (
        u
        - jnp.mean(u, axis=-1, keepdims=True)
        - hat * jnp.mean(u * hat, axis=-1, keepdims=True)
    )


def attn_fwd_kernel(n_pieces, cuts, offs, lens, tok_ref, *refs):
    pieces = refs[:n_pieces]
    n2_ref, res_ref, qkv_ref, ctx_ref, w_ref, gain_ref, wr_ref, sems = refs[n_pieces:]
    img = pl.program_id(0)
    seq_len, width = tok_ref.shape[1:]

    @pl.when(img == 0)
    def _():
        copies = []
        for i, piece in enumerate(pieces):
            rows = piece.shape[0]
            off = pl.multiple_of(offs[i], rows)
            lo, hi = cuts[i]
            copies.append(
                pltpu.make_async_copy(piece, w_ref.at[pl.ds(off, rows), lo:hi], sems.at[i])
            )
        for copy in copies:
            copy.start()
        for copy in copies:
            copy.wait()
        small = w_ref[:, 4 * width :].astype(F32).T
        gain_ref[...] = small[0:8]
        wr_ref[...] = small[8:16].astype(BF)

    length = lens[img]
    x = tok_ref[0].astype(F32)
    hat, _ = norm(x)
    n1 = (hat * gain_ref[0:1]).astype(BF)
    qkv_ref[0] = dot(n1, w_ref[:, : 3 * width]).astype(BF)
    key_ok = lax.broadcasted_iota(jnp.int32, (1, seq_len), 1) < length
    parts = []
    for h in range(HEADS):
        q = qkv_ref[0, :, h * HEAD : (h + 1) * HEAD]
        k = qkv_ref[0, :, width + h * HEAD : width + (h + 1) * HEAD]
        v = qkv_ref[0, :, 2 * width + h * HEAD : 2 * width + (h + 1) * HEAD]
        s = jnp.where(key_ok, dot(q, k, NT) * 0.125, -1e30)
        e = jnp.exp(s - jnp.max(s, axis=-1, keepdims=True))
        p = (e * (1.0 / jnp.sum(e, axis=-1, keepdims=True))).astype(BF)
        parts.append(dot(p, v))
    ctx = jnp.concatenate(parts, axis=1).astype(BF)
    ctx_ref[0] = ctx
    keep = lax.broadcasted_iota(jnp.int32, (seq_len, 1), 0) < length
    res = x + jnp.where(keep, dot(ctx, w_ref[:, 3 * width : 4 * width]), 0.0)
    res_ref[0] = res
    hat2, _ = norm(res)
    n2_ref[0] = (hat2 * gain_ref[1:2]).astype(BF)


def attn_fwd(tok, pieces, offs, cuts, lens):
    images, seq_len, width = tok.shape
    n = len(pieces)
    row = lambda w: pl.BlockSpec((1, seq_len, w), lambda i, *_: (i, 0, 0))
    whole = lambda s: pl.BlockSpec(s, lambda i, *_: (0,) * len(s))
    cols = 4 * width + SMALL
    return pl.pallas_call(
        lambda *a: attn_fwd_kernel(n, cuts, *a),
        grid_spec=pltpu.PrefetchScalarGridSpec(
            num_scalar_prefetch=2,
            grid=(images,),
            in_specs=[row(width)] + [pl.BlockSpec(memory_space=pl.ANY)] * n,
            out_specs=[
                row(width),
                row(width),
                row(3 * width),
                row(width),
                whole((width, cols)),
                whole((8, width)),
                whole((8, width)),
            ],
            scratch_shapes=[pltpu.SemaphoreType.DMA((n,))],
        ),
        out_shape=[
            jax.ShapeDtypeStruct((images, seq_len, width), BF),
            jax.ShapeDtypeStruct((images, seq_len, width), F32),
            jax.ShapeDtypeStruct((images, seq_len, 3 * width), BF),
            jax.ShapeDtypeStruct((images, seq_len, width), BF),
            jax.ShapeDtypeStruct((width, cols), BF),
            jax.ShapeDtypeStruct((8, width), F32),
            jax.ShapeDtypeStruct((8, width), BF),
        ],
        compiler_params=pltpu.CompilerParams(vmem_limit_bytes=40 * MIB),
        cost_estimate=pl.CostEstimate(
            flops=20 * 10**9, bytes_accessed=10 * MIB, transcendentals=1 << 20
        ),
    )(offs, lens, tok, *pieces)


def router(n2, wr, code):
    ids = lax.broadcasted_iota(jnp.int32, (8, n2.shape[0]), 0)
    logits = jnp.where(ids < 4, dot(wr, n2, NT), -1e30)
    e = jnp.exp(logits - jnp.max(logits, axis=0, keepdims=True))
    probs = e * (1.0 / jnp.sum(e, axis=0, keepdims=True))
    route = code.astype(F32).astype(jnp.int32)
    first = (route >> 1) & 3
    second = route >> 3
    chosen = ((ids == first) | (ids == second)).astype(F32)
    return probs, chosen


def moe_kernel(starts, n_aliased, wr_ref, win_ref, wout_ref, wint_ref, *refs):
    n = len(starts)
    xs, gs = refs[:n], refs[n : 2 * n]
    refs = refs[2 * n + n_aliased :]
    dx_ref, ga_ref, hg_ref, xo_ref, go_ref = refs
    step = pl.program_id(0)
    seq_len, width = xo_ref.shape[1:]
    rows = win_ref.shape[0] // 8
    for j in range(n):
        end = starts[j + 1] if j + 1 < n else None

        @pl.when((step >= starts[j]) if end is None else ((step >= starts[j]) & (step < end)))
        def _():
            xo_ref[0] = xs[j][0]
            go_ref[0] = gs[j][0]

    x = xo_ref[0]
    g = go_ref[0, :seq_len]
    probs, chosen = router(x, wr_ref[...], go_ref[0, seq_len : seq_len + 1, :seq_len])
    gate = probs * chosen
    sums = [None] * 4
    for b in range(8):
        e = b % 4
        sl = slice(b * rows, (b + 1) * rows)
        h = dot(win_ref[sl], x, NT)
        u = dot(wout_ref[sl], g, NT)
        cumul = 0.5 * (1.0 + lax.erf(h * SQRT_HALF))
        slope = cumul + h * (INV_ROOT_TWO_PI * jnp.exp(-0.5 * h * h))
        act = h * cumul
        row = gate[e : e + 1]
        ga_ref[0, sl] = (act * row).astype(BF)
        hg_ref[0, sl] = (u * row * slope).astype(BF)
        part = jnp.sum(act * u, axis=0, keepdims=True)
        sums[e] = part if sums[e] is None else sums[e] + part
    dx_ref[0, :width] = dot(wint_ref[...], hg_ref[0]).astype(BF)
    pad = jnp.zeros((CODE_ROWS - 4, seq_len), F32)
    dx_ref[0, width:] = jnp.concatenate(sums + [pad], axis=0).astype(BF)


def moe_call(xs, gs, wr, win, wout, wint, first, units, bufs):
    n = len(xs)
    counts = [x.shape[0] for x in xs]
    starts = [sum(counts[:j]) for j in range(n)]
    total = sum(counts)
    seq_len, width = xs[0].shape[1:]
    f = win.shape[0]
    g_rows = gs[0].shape[1]

    def item(rows, j):
        lo, c = starts[j], counts[j]
        return pl.BlockSpec(
            (1, rows, width), lambda i: (jnp.clip(i - lo, 0, c - 1), 0, 0)
        )

    whole = lambda s: pl.BlockSpec(s, lambda i: (0, 0), pipeline_mode=pl.Buffered(1))
    buf = lambda r, w: pl.BlockSpec((1, r, w), lambda i: (first + i, 0, 0))
    aliased = [] if bufs is None else list(bufs)
    base = 4 + 2 * n
    return pl.pallas_call(
        lambda *a: moe_kernel(starts, len(aliased), *a),
        grid=(total,),
        in_specs=[whole(wr.shape), whole(win.shape), whole(wout.shape), whole(wint.shape)]
        + [item(seq_len, j) for j in range(n)]
        + [item(g_rows, j) for j in range(n)]
        + [pl.BlockSpec(memory_space=pl.ANY)] * len(aliased),
        out_specs=[
            pl.BlockSpec((1, width + CODE_ROWS, seq_len), lambda i: (i, 0, 0)),
            buf(f, seq_len),
            buf(f, seq_len),
            buf(seq_len, width),
            buf(g_rows, width),
        ],
        out_shape=[
            jax.ShapeDtypeStruct((total, width + CODE_ROWS, seq_len), BF),
            jax.ShapeDtypeStruct((units, f, seq_len), BF),
            jax.ShapeDtypeStruct((units, f, seq_len), BF),
            jax.ShapeDtypeStruct((units, seq_len, width), BF),
            jax.ShapeDtypeStruct((units, g_rows, width), BF),
        ],
        input_output_aliases={base + k: 1 + k for k in range(len(aliased))},
        compiler_params=pltpu.CompilerParams(vmem_limit_bytes=40 * MIB),
        cost_estimate=pl.CostEstimate(
            flops=total * 6 * f * seq_len * width,
            bytes_accessed=total * 4 * f * seq_len + 6 * f * width,
            transcendentals=total * 2 * f * seq_len,
        ),
    )(wr, win, wout, wint, *xs, *gs, *aliased)


def moe_out_kernel(woutt_ref, ga_ref, out_ref):
    out_ref[0] = dot(woutt_ref[...], ga_ref[0]).astype(BF)


def moe_out(woutt, ga):
    units, f, seq_len = ga.shape
    width = woutt.shape[0]
    return pl.pallas_call(
        moe_out_kernel,
        grid=(units,),
        in_specs=[
            pl.BlockSpec((width, f), lambda i: (0, 0), pipeline_mode=pl.Buffered(1)),
            pl.BlockSpec((1, f, seq_len), lambda i: (i, 0, 0)),
        ],
        out_specs=pl.BlockSpec((1, width, seq_len), lambda i: (i, 0, 0)),
        out_shape=jax.ShapeDtypeStruct((units, width, seq_len), BF),
        compiler_params=pltpu.CompilerParams(vmem_limit_bytes=32 * MIB),
        cost_estimate=pl.CostEstimate(
            flops=units * 2 * f * seq_len * width,
            bytes_accessed=units * 2 * f * seq_len,
            transcendentals=0,
        ),
    )(woutt, ga)


def moe_grad_kernel(groups, ga_ref, hg_ref, x_ref, g_ref, din_ref, dout_ref, acc_in, acc_out):
    seq_len = x_ref.shape[1]
    part = pl.program_id(1)
    a_in = a_out = None
    for u in range(x_ref.shape[0]):
        t_in = dot(hg_ref[u], x_ref[u])
        t_out = dot(ga_ref[u], g_ref[u, :seq_len])
        a_in = t_in if a_in is None else a_in + t_in
        a_out = t_out if a_out is None else a_out + t_out
    if groups == 1:
        din_ref[0, 0, 0] = a_in.astype(BF)
        dout_ref[0, 0, 0] = a_out.astype(BF)
        return

    @pl.when(part == 0)
    def _():
        acc_in[...] = jnp.zeros_like(acc_in)
        acc_out[...] = jnp.zeros_like(acc_out)

    acc_in[...] += a_in
    acc_out[...] += a_out

    @pl.when(part == groups - 1)
    def _():
        din_ref[0, 0, 0] = acc_in[...].astype(BF)
        dout_ref[0, 0, 0] = acc_out[...].astype(BF)


def moe_grad(ga, hg, xb, gb):
    units, f, seq_len = ga.shape
    width = xb.shape[2]
    rows = f // 8
    per = min(units, 8)
    groups = units // per
    act = pl.BlockSpec((per, rows, seq_len), lambda b, p: (p, b, 0))
    out = pl.BlockSpec(
        (1, 1, 1, rows, width), lambda b, p: ((b % 4) // 2, b // 4, b % 2, 0, 0)
    )
    shape = jax.ShapeDtypeStruct((2, 2, 2, rows, width), BF)
    return pl.pallas_call(
        lambda *a: moe_grad_kernel(groups, *a),
        grid=(8, groups),
        in_specs=[
            act,
            act,
            pl.BlockSpec((per, seq_len, width), lambda b, p: (p, 0, 0)),
            pl.BlockSpec((per, gb.shape[1], width), lambda b, p: (p, 0, 0)),
        ],
        out_specs=[out, out],
        out_shape=[shape, shape],
        scratch_shapes=[pltpu.VMEM((rows, width), F32)] * 2,
        compiler_params=pltpu.CompilerParams(vmem_limit_bytes=40 * MIB),
        cost_estimate=pl.CostEstimate(
            flops=units * 4 * f * seq_len * width,
            bytes_accessed=units * 4 * f * seq_len,
            transcendentals=0,
        ),
    )(ga, hg, xb, gb)


def attn_bwd_kernel(
    lens,
    d0_ref,
    d1_ref,
    d2_ref,
    n2_ref,
    cot_ref,
    res_ref,
    ctx_ref,
    qkv_ref,
    tok_ref,
    w_ref,
    gain_ref,
    wr_ref,
    gtok_ref,
    dw_ref,
    acc,
    rows_acc,
):
    img = pl.program_id(0)
    seq_len, width = tok_ref.shape[1:]

    @pl.when(img == 0)
    def _():
        acc[...] = jnp.zeros_like(acc)
        rows_acc[...] = jnp.zeros_like(rows_acc)

    length = lens[img]
    keep = lax.broadcasted_iota(jnp.int32, (seq_len, 1), 0) < length
    total = d0_ref[0].astype(F32) + d1_ref[0].astype(F32) + d2_ref[0].astype(F32)
    n2 = n2_ref[0]
    probs, chosen = router(n2, wr_ref[...], cot_ref[0, seq_len : seq_len + 1, :seq_len])
    gate_grad = chosen * total[width : width + 8]
    logit_grad = probs * (gate_grad - jnp.sum(probs * gate_grad, axis=0, keepdims=True))
    high = logit_grad.astype(BF)
    low = (logit_grad - high.astype(F32)).astype(BF)
    rows_acc[8:16] += dot(high, n2) + dot(low, n2)
    dn2t = total[:width]
    w_small = w_ref[:, 4 * width :].astype(F32)
    for e in range(4):
        dn2t = dn2t + w_small[:, 8 + e : 9 + e] * logit_grad[e : e + 1]
    dn2 = dn2t.T
    hat2, inv2 = norm(res_ref[0])
    rows_acc[1:2] += jnp.sum(dn2 * hat2, axis=0, keepdims=True)
    res_grad = cot_ref[0, :seq_len].astype(F32) + norm_back(dn2 * gain_ref[1:2], hat2, inv2)
    pg = jnp.where(keep, res_grad, 0.0).astype(BF)
    acc[:, 3 * width :] += dot(ctx_ref[0], pg, TN)
    dctx = dot(pg, w_ref[:, 3 * width : 4 * width], NT).astype(BF)
    dqs, dks, dvs = [], [], []
    for h in range(HEADS):
        q = qkv_ref[0, :, h * HEAD : (h + 1) * HEAD]
        k = qkv_ref[0, :, width + h * HEAD : width + (h + 1) * HEAD]
        v = qkv_ref[0, :, 2 * width + h * HEAD : 2 * width + (h + 1) * HEAD]
        do = dctx[:, h * HEAD : (h + 1) * HEAD]
        s = jnp.where(keep, dot(k, q, NT) * 0.125, -1e30)
        e = jnp.exp(s - jnp.max(s, axis=0, keepdims=True))
        p = e * (1.0 / jnp.sum(e, axis=0, keepdims=True))
        dvs.append(dot(p.astype(BF), do))
        wg = dot(v, do, NT)
        sg = (p * (wg - jnp.sum(p * wg, axis=0, keepdims=True))).astype(BF)
        dqs.append(dot(sg, k, TN) * 0.125)
        dks.append(dot(sg, q) * 0.125)
    dqkv = jnp.concatenate(dqs + dks + dvs, axis=1).astype(BF)
    hat, inv = norm(tok_ref[0].astype(F32))
    n1 = (hat * gain_ref[0:1]).astype(BF)
    acc[:, : 3 * width] += dot(n1, dqkv, TN)
    dn1 = dot(dqkv, w_ref[:, : 3 * width], NT)
    rows_acc[0:1] += jnp.sum(dn1 * hat, axis=0, keepdims=True)
    gtok = res_grad + norm_back(dn1 * gain_ref[0:1], hat, inv)
    gtok_ref[0] = jnp.where(keep, gtok, 0.0).astype(BF)

    @pl.when(img == pl.num_programs(0) - 1)
    def _():
        dw_ref[:, : 4 * width] = acc[...].astype(BF)
        dw_ref[:, 4 * width :] = rows_acc[...].T.astype(BF)


def attn_bwd(lens, d0, d1, d2, n2, cot, res, ctx, qkv, tok, w, gains, wr):
    images, seq_len, width = tok.shape
    item = lambda a: pl.BlockSpec((1,) + a.shape[1:], lambda i, *_: (i, 0, 0))
    whole = lambda a: pl.BlockSpec(a.shape, lambda i, *_: (0, 0))
    cols = 4 * width + SMALL
    return pl.pallas_call(
        attn_bwd_kernel,
        grid_spec=pltpu.PrefetchScalarGridSpec(
            num_scalar_prefetch=1,
            grid=(images,),
            in_specs=[item(a) for a in (d0, d1, d2, n2, cot, res, ctx, qkv, tok)]
            + [whole(a) for a in (w, gains, wr)],
            out_specs=[
                pl.BlockSpec((1, seq_len, width), lambda i, *_: (i, 0, 0)),
                pl.BlockSpec((width, cols), lambda i, *_: (0, 0)),
            ],
            scratch_shapes=[
                pltpu.VMEM((width, 4 * width), F32),
                pltpu.VMEM((SMALL, width), F32),
            ],
        ),
        out_shape=[
            jax.ShapeDtypeStruct((images, seq_len, width), BF),
            jax.ShapeDtypeStruct((width, cols), BF),
        ],
        compiler_params=pltpu.CompilerParams(vmem_limit_bytes=48 * MIB),
        cost_estimate=pl.CostEstimate(
            flops=40 * 10**9, bytes_accessed=12 * MIB, transcendentals=1 << 20
        ),
    )(lens, d0, d1, d2, n2, cot, res, ctx, qkv, tok, w, gains, wr)


def ring_gather(x, m, fw, bw, cut):
    ahead, behind = [], []
    a = b = x
    for _ in range(m // 2 - 1):
        a, b = send(a, "fsdp", fw), send(b, "fsdp", bw)
        ahead.append(a)
        behind.append(b)
    top, bottom = cut(a)[0], cut(b)[1]
    return ahead, behind, send(top, "fsdp", fw), send(bottom, "fsdp", bw)


def ring_scatter(ahead, behind, top, bottom, fw, bw, put):
    a, b = send(top, "fsdp", fw), send(bottom, "fsdp", bw)
    first = True
    for to_fw, to_bw in zip(reversed(ahead), reversed(behind)):
        if first:
            a, b = put(to_fw, a, 0), put(to_bw, b, 1)
            first = False
        else:
            a, b = add_low(to_fw, a), add_low(to_bw, b)
        a, b = send(a, "fsdp", fw), send(b, "fsdp", bw)
    return a, b


def per_device(
    tokens, pad_mask, routes, ln1_gain, w_qkv, w_proj, ln2_gain, w_router, exp_in, exp_out, cotangent
):
    n = lax.axis_size("fsdp")
    width = tokens.shape[2]
    seq_idx = lax.axis_index("seq")
    core, half = seq_idx & 1, seq_idx >> 1
    idx = lax.axis_index("fsdp")
    m = n // 2
    fw8, bw8 = ring_pairs([ring_order(n)])
    low_ring = ring_order(m)
    fw4, bw4 = ring_pairs([low_ring, [m + i for i in low_ring]])
    pair = [(i, (i + m) % n) for i in range(n)]
    by_core = [(i, i ^ 1) for i in range(4)]
    by_half = [(i, i ^ 2) for i in range(4)]

    rows = w_qkv.shape[0]
    lead = lambda a: a.astype(BF).reshape(rows, -1)
    block = jnp.concatenate(
        [
            lead(w_qkv),
            lead(w_proj),
            lead(ln1_gain),
            lead(ln2_gain),
            jnp.zeros((rows, 6), BF),
            lead(w_router),
            jnp.zeros((rows, SMALL - 12), BF),
        ],
        axis=1,
    )
    cols = block.shape[1]
    mid = 9 * 128
    ahead, behind, top, bottom = ring_gather(
        block, n, fw8, bw8, lambda a: (a[:, :mid], a[:, mid:])
    )
    place = jnp.where(idx % 2 == 0, idx // 2, n - 1 - idx // 2)

    def at_place(p):
        p = p % n
        return jnp.where(p < m, 2 * p, 2 * (n - 1 - p) + 1)

    pieces, offs, cuts = [block], [idx], [(0, cols)]
    for d in range(1, m):
        pieces += [ahead[d - 1], behind[d - 1]]
        offs += [at_place(place - d + n), at_place(place + d)]
        cuts += [(0, cols)] * 2
    pieces += [top, bottom]
    offs += [at_place(place + m)] * 2
    cuts += [(0, mid), (mid, cols)]
    offs = jnp.stack(offs).astype(jnp.int32) * rows

    keep = pad_mask.astype(BF)[..., None]
    tok = lax.all_to_all(tokens * keep, "seq", split_axis=0, concat_axis=1, tiled=True)
    code = pad_mask + 2 * routes[..., 0] + 8 * routes[..., 1]
    code = jnp.pad(code.astype(BF)[..., None], ((0, 0), (0, 0), (0, 127)))
    cot = lax.all_to_all(
        jnp.concatenate([cotangent * keep, code], axis=2),
        "seq",
        split_axis=0,
        concat_axis=1,
        tiled=True,
    )
    images, seq_len = tok.shape[:2]
    code = cot[:, :, width]
    lens = jnp.sum(code.astype(jnp.int32) & 1, axis=1)
    code = jnp.pad(code[:, None, :], ((0, 0), (0, CODE_ROWS - 1), (0, width - seq_len)))
    cot = jnp.concatenate([cot[:, :, :width], code], axis=1)

    by_image = lambda a: (a[: images // 2], a[images // 2 :])
    g_ahead, g_behind, g_top, g_bottom = ring_gather(cot, m, fw4, bw4, by_image)

    fr = exp_in.shape[0]
    win = exp_in.transpose(1, 0, 2).astype(BF)
    wout = exp_out.transpose(1, 0, 2).astype(BF)
    quarters = jnp.stack([win, wout]).reshape(4, 2, fr, width)
    mine = lax.dynamic_index_in_dim(quarters, seq_idx, 0, False)
    qa = send(mine, "fsdp", pair)
    qb = send(qa, "seq", by_half)
    qc = send(jnp.stack([qa, qb]), "seq", by_core)
    rel = jnp.stack([qa, qc[0], qb, qc[1]])
    other = jnp.stack(
        [lax.dynamic_index_in_dim(rel, seq_idx ^ q, 0, False) for q in range(4)]
    ).reshape(2, 4 * fr, width)
    win = jnp.concatenate([win.reshape(4 * fr, width), other[0]], axis=0)
    wout = jnp.concatenate([wout.reshape(4 * fr, width), other[1]], axis=0)
    wint, woutt = win.T, wout.T

    n2, res, qkv, ctx, w, gains, wr = attn_fwd(tok, pieces, offs, cuts, lens)

    x_ahead, x_behind, x_top, x_bottom = ring_gather(n2, m, fw4, bw4, by_image)
    units = images * m
    half_img = images // 2
    d_own, *bufs = moe_call([n2], [cot], wr, win, wout, wint, 0, units, None)
    at = images
    dx_ahead, dx_behind = [None] * (m // 2 - 1), [None] * (m // 2 - 1)
    where = {}
    for d in range(m // 2 - 1):
        dd, *bufs = moe_call(
            [x_ahead[d], x_behind[d]],
            [g_ahead[d], g_behind[d]],
            wr,
            win,
            wout,
            wint,
            at,
            units,
            bufs,
        )
        where[d] = at
        at += 2 * images
        dx_behind[d], dx_ahead[d] = dd[:images], dd[images:]
    dd, *bufs = moe_call(
        [x_top, x_bottom], [g_top, g_bottom], wr, win, wout, wint, at, units, bufs
    )

    def put(term, part, side):
        if side == 0:
            return jnp.concatenate([add_low(term[:half_img], part), term[half_img:]])
        return jnp.concatenate([term[:half_img], add_low(term[half_img:], part)])

    d1, d2 = ring_scatter(dx_ahead, dx_behind, dd[:half_img], dd[half_img:], fw4, bw4, put)

    ga, hg, xb, gb = bufs
    din, dout = moe_grad(ga, hg, xb, gb)
    outs = moe_out(woutt, ga)
    o_ahead = [outs[where[d] + images : where[d] + 2 * images] for d in range(m // 2 - 1)]
    o_behind = [outs[where[d] : where[d] + images] for d in range(m // 2 - 1)]
    o1, o2 = ring_scatter(
        o_ahead, o_behind, outs[at : at + half_img], outs[at + half_img :], fw4, bw4, put
    )
    moe = outs[:images].astype(F32) + o1.astype(F32) + o2.astype(F32)
    real = jnp.arange(seq_len)[None, :] < lens[:, None]
    block_out = res + moe.transpose(0, 2, 1) * real[..., None].astype(F32)
    block_out = lax.all_to_all(
        block_out.astype(BF), "seq", split_axis=1, concat_axis=0, tiled=True
    )

    gtok, dw = attn_bwd(lens, d_own, d1, d2, n2, cot, res, ctx, qkv, tok, w, gains, wr)
    grad_tokens = lax.all_to_all(gtok, "seq", split_axis=1, concat_axis=0, tiled=True).astype(F32)

    def term(p):
        return lax.dynamic_slice_in_dim(dw, at_place(p) * rows, rows, 0)

    far = term(place + m)

    def put_cols(t, part, side):
        if side == 0:
            return jnp.concatenate([add_low(t[:, :mid], part), t[:, mid:]], axis=1)
        return jnp.concatenate([t[:, :mid], add_low(t[:, mid:], part)], axis=1)

    s1, s2 = ring_scatter(
        [term(place + d) for d in range(1, m)],
        [term(place - d + n) for d in range(1, m)],
        far[:, :mid],
        far[:, mid:],
        fw8,
        bw8,
        put_cols,
    )
    dense = (term(place).astype(F32) + s1.astype(F32) + s2.astype(F32)).astype(BF)
    dense = add_low(dense, send(dense, "seq", by_core))
    dense = dense.astype(F32) + send(dense, "seq", by_half).astype(F32)

    pick = lambda a, i: lax.dynamic_index_in_dim(a, i, 0, False)
    got = send(jnp.stack([pick(din, 1 - core), pick(dout, 1 - core)]), "seq", by_core)
    kept = add_low(jnp.stack([pick(din, core), pick(dout, core)]), got)
    kept = add_low(pick(kept, half), send(pick(kept, 1 - half), "seq", by_half))
    quarter = add_low(kept[0], send(kept[1], "fsdp", pair))
    from_half = send(quarter, "seq", by_half)
    from_core = send(jnp.stack([quarter, from_half]), "seq", by_core)
    rel = jnp.stack([quarter, from_core[0], from_half, from_core[1]])
    grads = [pick(rel, seq_idx ^ q) for q in range(4)]
    grad_in = jnp.concatenate(grads[:2], axis=0).astype(F32).transpose(1, 0, 2)
    grad_out = jnp.concatenate(grads[2:], axis=0).astype(F32).transpose(1, 0, 2)

    small = dense[:, 4 * width :]
    return (
        block_out,
        grad_tokens,
        small[:, 0],
        dense[:, : 3 * width],
        dense[:, 3 * width : 4 * width],
        small[:, 1],
        small[:, 8:12],
        grad_in,
        grad_out,
    )


def solution(mesh):
    row = P("fsdp", None)
    cube = P("fsdp", None, None)
    split = P("fsdp", "seq", None)
    return jax.shard_map(
        per_device,
        mesh=mesh,
        in_specs=(
            split,
            P("fsdp", "seq"),
            split,
            P("fsdp"),
            row,
            row,
            P("fsdp"),
            row,
            cube,
            cube,
            split,
        ),
        out_specs=(split, split, P("fsdp"), row, row, P("fsdp"), row, cube, cube),
        check_vma=False,
    )
```

```python
import jax
import jax.numpy as jnp
from jax import lax
from jax.experimental import pallas as pl
from jax.experimental.pallas import tpu as pltpu
from jax.sharding import PartitionSpec as P

BF = jnp.bfloat16
F32 = jnp.float32
HEADS = 8
HEAD = 64
EPS = 1e-06
SQRT_HALF = 0.7071067811865476
INV_ROOT_TWO_PI = 0.3989422804014327
SMALL = 256
CODE_ROWS = 16
NT = (((1,), (1,)), ((), ()))
TN = (((0,), (0,)), ((), ()))
MIB = 1 << 20
PACE = 0.0001


def cost(us):
    return pl.CostEstimate(
        flops=int(us * 1.15e9 * PACE) + 1, bytes_accessed=int(us * 1e5 * PACE) + 1, transcendentals=0
    )


def dot(a, b, dims=(((1,), (0,)), ((), ()))):
    return lax.dot_general(a, b, dims, preferred_element_type=F32)


def ring_order(n):
    return [2 * i for i in range(n // 2)] + [2 * i + 1 for i in reversed(range(n // 2))]


def ring_pairs(orders):
    fw = []
    for order in orders:
        n = len(order)
        fw += [(order[i], order[(i + 1) % n]) for i in range(n)]
    return fw, [(b, a) for a, b in fw]


def send(x, axis, pairs):
    return lax.ppermute(x, axis, pairs)


def add_low(a, b):
    return (a.astype(F32) + b.astype(F32)).astype(BF)


def norm(v):
    c = v - jnp.mean(v, axis=-1, keepdims=True)
    inv = lax.rsqrt(jnp.mean(c * c, axis=-1, keepdims=True) + EPS)
    return c * inv, inv


def norm_back(u, hat, inv):
    return inv * (
        u
        - jnp.mean(u, axis=-1, keepdims=True)
        - hat * jnp.mean(u * hat, axis=-1, keepdims=True)
    )


def block_kernel(own_ref, qkv_ref, proj_ref, small_ref, out_ref):
    mid = out_ref.shape[1]
    rest = qkv_ref.shape[1] - mid
    width = proj_ref.shape[1]

    @pl.when((own_ref[0] & 1) == 0)
    def _():
        out_ref[...] = qkv_ref[:, :mid].astype(BF)

    @pl.when((own_ref[0] & 1) == 1)
    def _():
        out_ref[:, :rest] = qkv_ref[:, mid:].astype(BF)
        out_ref[:, rest : rest + width] = proj_ref[...].astype(BF)
        out_ref[:, rest + width :] = small_ref[...].astype(BF)


def block_of(own, w_qkv, w_proj, small):
    rows = w_qkv.shape[0]
    mid = (w_qkv.shape[1] + w_proj.shape[1] + SMALL) // 2
    whole = pl.BlockSpec(memory_space=pltpu.VMEM)
    return pl.pallas_call(
        block_kernel,
        in_specs=[pl.BlockSpec(memory_space=pltpu.SMEM)] + [whole] * 3,
        out_specs=whole,
        out_shape=jax.ShapeDtypeStruct((rows, mid), BF),
        compiler_params=pltpu.CompilerParams(vmem_limit_bytes=8 * MIB),
        cost_estimate=cost(1),
    )(own, w_qkv, w_proj, small)


def unpack_kernel(c0_ref, c1_ref, code_ref, a_ref, b_ref):
    img = pl.program_id(0)
    half = pl.num_programs(0) // 2
    for k, ref in ((0, a_ref), (1, b_ref)):

        @pl.when((img >= k * half) & (img < (k + 1) * half))
        def _():
            seq_len = ref.shape[1] - CODE_ROWS
            lanes = ref.shape[2] // 2
            ref[0, :seq_len, :lanes] = c0_ref[:, 0].reshape(seq_len, lanes)
            ref[0, :seq_len, lanes:] = c1_ref[:, 0].reshape(seq_len, lanes)
            code = code_ref[:, 0].astype(F32).reshape(seq_len, 128).T
            ref[0, seq_len:, :seq_len] = code[:CODE_ROWS].astype(BF)
            ref[0, seq_len:, seq_len:] = jnp.zeros((CODE_ROWS, ref.shape[2] - seq_len), BF)


def unpack(fused, width):
    parts, images, seg, _ = fused.shape
    half = images // 2
    col = lambda w, c: pl.BlockSpec((parts, 1, seg, w), lambda i: (0, i, 0, c))
    rows = parts * seg + CODE_ROWS
    out = lambda k: pl.BlockSpec(
        (1, rows, width), lambda i: (jnp.clip(i - k * half, 0, half - 1), 0, 0)
    )
    shape = jax.ShapeDtypeStruct((half, rows, width), BF)
    return pl.pallas_call(
        unpack_kernel,
        grid=(images,),
        in_specs=[col(width // 2, 2), col(width // 2, 3), col(128, 2 * width // 128)],
        out_specs=[out(0), out(1)],
        out_shape=[shape, shape],
        compiler_params=pltpu.CompilerParams(vmem_limit_bytes=8 * MIB),
        cost_estimate=cost(1.5),
    )(fused, fused, fused)


def gather_kernel(n_pieces, cuts, offs, *refs):
    pieces, out_ref, sems = refs[:n_pieces], refs[n_pieces], refs[n_pieces + 1]
    copies = []
    for i, piece in enumerate(pieces):
        rows = piece.shape[0]
        off = pl.multiple_of(offs[i], rows)
        lo, hi = cuts[i]
        copies.append(
            pltpu.make_async_copy(piece, out_ref.at[pl.ds(off, rows), lo:hi], sems.at[i])
        )
    for copy in copies:
        copy.start()
    for copy in copies:
        copy.wait()


def gather_rows(pieces, offs, cuts, shape):
    n = len(pieces)
    anywhere = pl.BlockSpec(memory_space=pl.ANY)
    return pl.pallas_call(
        lambda *a: gather_kernel(n, cuts, *a),
        in_specs=[pl.BlockSpec(memory_space=pltpu.SMEM)] + [anywhere] * n,
        out_specs=pl.BlockSpec(memory_space=pltpu.VMEM),
        out_shape=jax.ShapeDtypeStruct(shape, BF),
        scratch_shapes=[pltpu.SemaphoreType.DMA((n,))],
        compiler_params=pltpu.CompilerParams(vmem_limit_bytes=8 * MIB),
        cost_estimate=cost(2),
    )(offs, *pieces)


def attn_fwd_kernel(own_ref, tok_ref, code_ref, mine_ref, other_ref, *refs):
    n2a_ref, n2b_ref, res_ref, qkv_ref, ctx_ref, w_ref, gain_ref, wr_ref = refs
    img = pl.program_id(0)
    seq_len, width = res_ref.shape[1:]
    mid = mine_ref.shape[1]
    own = own_ref[0]

    @pl.when(img == 0)
    def _():
        for core, left, right in ((0, mine_ref, other_ref), (1, other_ref, mine_ref)):

            @pl.when((own & 1) == core)
            def _():
                w_ref[:, :mid] = left[...]
                w_ref[:, mid:] = right[...]

        small = w_ref[:, 4 * width : 4 * width + 128].astype(F32).T
        gain_ref[...] = small[0:16]
        for r in range(4):
            wr_ref[r : r + 1] = gain_ref[pl.ds(8 + (own ^ r), 1)]
        wr_ref[4:8] = jnp.zeros((4, width), F32)

    code = code_ref[:, 0].reshape(seq_len, 128).astype(F32)
    keep = (code[:, 0:1].astype(jnp.int32) & 1) > 0
    key_ok = (code.T[0:1].astype(jnp.int32) & 1) > 0
    x = tok_ref[:, 0].reshape(seq_len, width).astype(F32)
    hat, _ = norm(x)
    n1 = (hat * gain_ref[0:1]).astype(BF)
    qkv_ref[0] = dot(n1, w_ref[:, : 3 * width]).astype(BF)
    parts = []
    for h in range(HEADS):
        q = qkv_ref[0, :, h * HEAD : (h + 1) * HEAD]
        k = qkv_ref[0, :, width + h * HEAD : width + (h + 1) * HEAD]
        v = qkv_ref[0, :, 2 * width + h * HEAD : 2 * width + (h + 1) * HEAD]
        s = jnp.where(key_ok, dot(q, k, NT) * 0.125, -1e30)
        e = jnp.exp(s - jnp.max(s, axis=-1, keepdims=True))
        p = (e * (1.0 / jnp.sum(e, axis=-1, keepdims=True))).astype(BF)
        parts.append(dot(p, v))
    ctx = jnp.concatenate(parts, axis=1).astype(BF)
    ctx_ref[0] = ctx
    res = x + jnp.where(keep, dot(ctx, w_ref[:, 3 * width : 4 * width]), 0.0)
    res_ref[0] = res
    hat2, _ = norm(res)
    n2 = (hat2 * gain_ref[1:2]).astype(BF)
    half = pl.num_programs(0) // 2
    for k, ref in ((0, n2a_ref), (1, n2b_ref)):

        @pl.when((img >= k * half) & (img < (k + 1) * half))
        def _():
            ref[0] = n2


def attn_fwd(own, fused, mine, other, width):
    parts, images, seg, _ = fused.shape
    seq_len, half = parts * seg, images // 2
    row = lambda w: pl.BlockSpec((1, seq_len, w), lambda i, *_: (i, 0, 0))
    whole = lambda s: pl.BlockSpec(s, lambda i, *_: (0,) * len(s))
    side = lambda k: pl.BlockSpec(
        (1, seq_len, width), lambda i, *_: (jnp.clip(i - k * half, 0, half - 1), 0, 0)
    )
    cols = 4 * width + SMALL
    return pl.pallas_call(
        attn_fwd_kernel,
        grid_spec=pltpu.PrefetchScalarGridSpec(
            num_scalar_prefetch=1,
            grid=(images,),
            in_specs=[
                pl.BlockSpec((parts, 1, seg, width), lambda i, *_: (0, i, 0, 0)),
                pl.BlockSpec((parts, 1, seg, 128), lambda i, *_: (0, i, 0, 2 * width // 128)),
                whole(mine.shape),
                whole(other.shape),
            ],
            out_specs=[
                side(0),
                side(1),
                row(width),
                row(3 * width),
                row(width),
                whole((width, cols)),
                whole((16, width)),
                whole((8, width)),
            ],
        ),
        out_shape=[
            jax.ShapeDtypeStruct((half, seq_len, width), BF),
            jax.ShapeDtypeStruct((half, seq_len, width), BF),
            jax.ShapeDtypeStruct((images, seq_len, width), F32),
            jax.ShapeDtypeStruct((images, seq_len, 3 * width), BF),
            jax.ShapeDtypeStruct((images, seq_len, width), BF),
            jax.ShapeDtypeStruct((width, cols), BF),
            jax.ShapeDtypeStruct((16, width), F32),
            jax.ShapeDtypeStruct((8, width), F32),
        ],
        compiler_params=pltpu.CompilerParams(vmem_limit_bytes=20 * MIB),
        cost_estimate=cost(8),
    )(own, fused, fused, mine, other)


def router(own, n2, wr, code):
    ids = lax.broadcasted_iota(jnp.int32, (8, n2.shape[0]), 0)
    logits = jnp.where(ids < 4, dot(wr.astype(BF), n2, NT), -1e30)
    e = jnp.exp(logits - jnp.max(logits, axis=0, keepdims=True))
    probs = e * (1.0 / jnp.sum(e, axis=0, keepdims=True))
    route = code.astype(F32).astype(jnp.int32)
    first = (route >> 1) & 3
    second = route >> 3
    ids = ids ^ own
    chosen = ((ids == first) | (ids == second)).astype(F32)
    return probs, chosen


def weights_kernel(own_ref, *refs):
    win_ref, wout_ref = refs[:2]
    pieces = refs[2:-4]
    parts = len(pieces) // 4
    all_in, all_out, in_t, out_t = refs[-4:]
    own = own_ref[0]
    rows = win_ref.shape[1]
    for b in range(8):
        sl = slice(b * rows, (b + 1) * rows)
        if b < 4:
            a, c = win_ref[own ^ b], wout_ref[own ^ b]
        else:
            mine = pieces[(b - 4) * parts : (b - 3) * parts]
            a, c = (jnp.concatenate([p[k] for p in mine], axis=0) for k in range(2))
        all_in[sl] = a
        all_out[sl] = c
        in_t[:, sl] = a.T
        out_t[:, sl] = c.T


def weights(own, win, wout, pieces):
    rows, width = win.shape[1:]
    whole = pl.BlockSpec(memory_space=pltpu.VMEM)
    flat = jax.ShapeDtypeStruct((8 * rows, width), BF)
    turned = jax.ShapeDtypeStruct((width, 8 * rows), BF)
    return pl.pallas_call(
        weights_kernel,
        in_specs=[pl.BlockSpec(memory_space=pltpu.SMEM)] + [whole] * (2 + len(pieces)),
        out_specs=[whole] * 4,
        out_shape=[flat, flat, turned, turned],
        compiler_params=pltpu.CompilerParams(vmem_limit_bytes=16 * MIB),
        cost_estimate=cost(3),
    )(own, win, wout, *pieces)


def moe_kernel(starts, n_aliased, own_ref, wr_ref, win_ref, wout_ref, wint_ref, *refs):
    n = len(starts)
    xs, gs = refs[:n], refs[n : 2 * n]
    refs = refs[2 * n + n_aliased :]
    dx_refs = refs[:n]
    ga_ref, hg_ref, xo_ref, go_ref = refs[n:]
    step = pl.program_id(0)
    seq_len, width = xo_ref.shape[1:]
    rows = win_ref.shape[0] // 8
    within = []
    for j in range(n):
        low, high = starts[j], starts[j + 1] if j + 1 < n else None
        within.append((step >= low) if high is None else ((step >= low) & (step < high)))

        @pl.when(within[j])
        def _():
            xo_ref[0] = xs[j][0]
            go_ref[0] = gs[j][0]

    x = xo_ref[0]
    g = go_ref[0, :seq_len]
    probs, chosen = router(own_ref[0], x, wr_ref[...], go_ref[0, seq_len : seq_len + 1, :seq_len])
    gate = probs * chosen
    sums = [None] * 4
    for b in range(8):
        e = b % 4
        sl = slice(b * rows, (b + 1) * rows)
        h = dot(win_ref[sl], x, NT)
        u = dot(wout_ref[sl], g, NT)
        cumul = 0.5 * (1.0 + lax.erf(h * SQRT_HALF))
        slope = cumul + h * (INV_ROOT_TWO_PI * jnp.exp(-0.5 * h * h))
        act = h * cumul
        row = gate[e : e + 1]
        ga_ref[0, sl] = (act * row).astype(BF)
        hg_ref[0, sl] = (u * row * slope).astype(BF)
        part = jnp.sum(act * u, axis=0, keepdims=True)
        sums[e] = part if sums[e] is None else sums[e] + part
    dx = dot(wint_ref[...], hg_ref[0]).astype(BF)
    pad = jnp.zeros((CODE_ROWS - 4, seq_len), F32)
    tail = jnp.concatenate(sums + [pad], axis=0).astype(BF)
    for j in range(n):

        @pl.when(within[j])
        def _():
            dx_refs[j][0, :width] = dx
            dx_refs[j][0, width:] = tail


def moe_call(xs, gs, own, wr, win, wout, wint, first, units, bufs):
    n = len(xs)
    counts = [x.shape[0] for x in xs]
    starts = [sum(counts[:j]) for j in range(n)]
    total = sum(counts)
    seq_len, width = xs[0].shape[1:]
    f = win.shape[0]
    g_rows = gs[0].shape[1]

    def item(rows, j):
        lo, c = starts[j], counts[j]
        return pl.BlockSpec(
            (1, rows, width), lambda i: (jnp.clip(i - lo, 0, c - 1), 0, 0)
        )

    def out_item(j):
        lo, c = starts[j], counts[j]
        return pl.BlockSpec(
            (1, width + CODE_ROWS, seq_len), lambda i: (jnp.clip(i - lo, 0, c - 1), 0, 0)
        )

    whole = lambda s: pl.BlockSpec(s, lambda i: (0, 0), pipeline_mode=pl.Buffered(1))
    buf = lambda r, w: pl.BlockSpec((1, r, w), lambda i: (first + i, 0, 0))
    aliased = [] if bufs is None else list(bufs)
    base = 5 + 2 * n
    return pl.pallas_call(
        lambda *a: moe_kernel(starts, len(aliased), *a),
        grid=(total,),
        in_specs=[pl.BlockSpec(memory_space=pltpu.SMEM)]
        + [whole(wr.shape), whole(win.shape), whole(wout.shape), whole(wint.shape)]
        + [item(seq_len, j) for j in range(n)]
        + [item(g_rows, j) for j in range(n)]
        + [pl.BlockSpec(memory_space=pl.ANY)] * len(aliased),
        out_specs=[out_item(j) for j in range(n)]
        + [
            buf(f, seq_len),
            buf(f, seq_len),
            buf(seq_len, width),
            buf(g_rows, width),
        ],
        out_shape=[
            jax.ShapeDtypeStruct((c, width + CODE_ROWS, seq_len), BF) for c in counts
        ]
        + [
            jax.ShapeDtypeStruct((units, f, seq_len), BF),
            jax.ShapeDtypeStruct((units, f, seq_len), BF),
            jax.ShapeDtypeStruct((units, seq_len, width), BF),
            jax.ShapeDtypeStruct((units, g_rows, width), BF),
        ],
        input_output_aliases={base + k: n + k for k in range(len(aliased))},
        compiler_params=pltpu.CompilerParams(vmem_limit_bytes=16 * MIB),
        cost_estimate=cost(2.6 * total),
    )(own, wr, win, wout, wint, *xs, *gs, *aliased)


def moe_out_kernel(woutt_ref, ga_ref, out_ref):
    out_ref[0] = dot(woutt_ref[...], ga_ref[0]).astype(BF)


def moe_out(woutt, ga):
    units, f, seq_len = ga.shape
    width = woutt.shape[0]
    return pl.pallas_call(
        moe_out_kernel,
        grid=(units,),
        in_specs=[
            pl.BlockSpec((width, f), lambda i: (0, 0), pipeline_mode=pl.Buffered(1)),
            pl.BlockSpec((1, f, seq_len), lambda i: (i, 0, 0)),
        ],
        out_specs=pl.BlockSpec((1, width, seq_len), lambda i: (i, 0, 0)),
        out_shape=jax.ShapeDtypeStruct((units, width, seq_len), BF),
        compiler_params=pltpu.CompilerParams(vmem_limit_bytes=8 * MIB),
        cost_estimate=cost(0.7 * units),
    )(woutt, ga)


def moe_grad_kernel(groups, ga_ref, hg_ref, x_ref, g_ref, out_ref, acc_in, acc_out):
    seq_len = x_ref.shape[1]
    part = pl.program_id(1)
    a_in = a_out = None
    for u in range(x_ref.shape[0]):
        t_in = dot(hg_ref[u], x_ref[u])
        t_out = dot(ga_ref[u], g_ref[u, :seq_len])
        a_in = t_in if a_in is None else a_in + t_in
        a_out = t_out if a_out is None else a_out + t_out
    if groups == 1:
        out_ref[0, 0] = a_in.astype(BF)
        out_ref[0, 1] = a_out.astype(BF)
        return

    @pl.when(part == 0)
    def _():
        acc_in[...] = jnp.zeros_like(acc_in)
        acc_out[...] = jnp.zeros_like(acc_out)

    acc_in[...] += a_in
    acc_out[...] += a_out

    @pl.when(part == groups - 1)
    def _():
        out_ref[0, 0] = acc_in[...].astype(BF)
        out_ref[0, 1] = acc_out[...].astype(BF)


def moe_grad(ga, hg, xb, gb, r):
    units, f, seq_len = ga.shape
    width = xb.shape[2]
    rows = f // 8
    per = min(units, 8)
    groups = units // per
    act = pl.BlockSpec((per, rows, seq_len), lambda b, p: (p, 4 * b + r, 0))
    return pl.pallas_call(
        lambda *a: moe_grad_kernel(groups, *a),
        grid=(2, groups),
        in_specs=[
            act,
            act,
            pl.BlockSpec((per, seq_len, width), lambda b, p: (p, 0, 0)),
            pl.BlockSpec((per, gb.shape[1], width), lambda b, p: (p, 0, 0)),
        ],
        out_specs=pl.BlockSpec((1, 2, rows, width), lambda b, p: (b, 0, 0, 0)),
        out_shape=jax.ShapeDtypeStruct((2, 2, rows, width), BF),
        scratch_shapes=[pltpu.VMEM((rows, width), F32)] * 2,
        compiler_params=pltpu.CompilerParams(vmem_limit_bytes=18 * MIB),
        cost_estimate=cost(0.47 * units),
    )(ga, hg, xb, gb)


def pack_kernel(own_ref, *refs):
    pieces = refs[:4]
    in_ref, out_ref = refs[4:]
    own = own_ref[0]
    for k in range(4):

        @pl.when(own == k)
        def _():
            for e in range(4):
                in_ref[:, e, :] = pieces[k ^ e][0].astype(F32)
                out_ref[:, e, :] = pieces[k ^ e][1].astype(F32)


def pack(own, pieces):
    rows, width = pieces[0].shape[1:]
    tile = min(rows, 64)
    piece = pl.BlockSpec((2, tile, width), lambda i: (0, i, 0))
    out = pl.BlockSpec((tile, 4, width), lambda i: (i, 0, 0))
    shape = jax.ShapeDtypeStruct((rows, 4, width), F32)
    return pl.pallas_call(
        pack_kernel,
        grid=(rows // tile,),
        in_specs=[pl.BlockSpec(memory_space=pltpu.SMEM)] + [piece] * 4,
        out_specs=[out, out],
        out_shape=[shape, shape],
        compiler_params=pltpu.CompilerParams(vmem_limit_bytes=24 * MIB),
        cost_estimate=cost(3),
    )(own, *pieces)


def attn_bwd_kernel(
    own_ref,
    *refs,
):
    items, refs = refs[:10], refs[10:]
    (
    res_ref,
    ctx_ref,
    qkv_ref,
    tok_ref,
    code_ref,
    w_ref,
    gain_ref,
    wr_ref,
    gtok_ref,
    keep_ref,
    give_ref,
    acc,
    rows_acc,
    sums,
    n2_ref,
    cot_ref,
    ) = refs
    own = own_ref[0]
    img = pl.program_id(0)
    seq_len, width = n2_ref.shape

    @pl.when(img == 0)
    def _():
        acc[...] = jnp.zeros_like(acc)
        rows_acc[...] = jnp.zeros_like(rows_acc)

    half = pl.num_programs(0) // 2
    for side in range(2):

        @pl.when((img >= side * half) & (img < (side + 1) * half))
        def _():
            d0, d1, d2, n2, cot = (items[2 * t + side] for t in range(5))
            sums[...] = d0[0].astype(F32) + d1[0].astype(F32) + d2[0].astype(F32)
            n2_ref[...] = n2[0]
            cot_ref[...] = cot[0]

    code = code_ref[:, 0].reshape(seq_len, 128)[:, 0:1].astype(F32)
    keep = (code.astype(jnp.int32) & 1) > 0
    total = sums[...]
    n2 = n2_ref[...]
    probs, chosen = router(own, n2, wr_ref[...], cot_ref[seq_len : seq_len + 1, :seq_len])
    gate_grad = chosen * total[width : width + 8]
    logit_grad = probs * (gate_grad - jnp.sum(probs * gate_grad, axis=0, keepdims=True))
    high = logit_grad.astype(BF)
    low = (logit_grad - high.astype(F32)).astype(BF)
    rows_acc[16:24] += dot(high, n2) + dot(low, n2)
    wr = wr_ref[...].astype(BF)
    dn2 = (total[:width] + dot(wr, high, TN) + dot(wr, low, TN)).T
    hat2, inv2 = norm(res_ref[0])
    rows_acc[1:2] += jnp.sum(dn2 * hat2, axis=0, keepdims=True)
    res_grad = cot_ref[:seq_len].astype(F32) + norm_back(dn2 * gain_ref[1:2], hat2, inv2)
    pg = jnp.where(keep, res_grad, 0.0).astype(BF)
    acc[:, 3 * width :] += dot(ctx_ref[0], pg, TN)
    dctx = dot(pg, w_ref[:, 3 * width : 4 * width], NT).astype(BF)
    dqs, dks, dvs = [], [], []
    for h in range(HEADS):
        q = qkv_ref[0, :, h * HEAD : (h + 1) * HEAD]
        k = qkv_ref[0, :, width + h * HEAD : width + (h + 1) * HEAD]
        v = qkv_ref[0, :, 2 * width + h * HEAD : 2 * width + (h + 1) * HEAD]
        do = dctx[:, h * HEAD : (h + 1) * HEAD]
        s = jnp.where(keep, dot(k, q, NT) * 0.125, -1e30)
        e = jnp.exp(s - jnp.max(s, axis=0, keepdims=True))
        p = e * (1.0 / jnp.sum(e, axis=0, keepdims=True))
        dvs.append(dot(p.astype(BF), do))
        wg = dot(v, do, NT)
        sg = (p * (wg - jnp.sum(p * wg, axis=0, keepdims=True))).astype(BF)
        dqs.append(dot(sg, k, TN) * 0.125)
        dks.append(dot(sg, q) * 0.125)
    dqkv = jnp.concatenate(dqs + dks + dvs, axis=1).astype(BF)
    hat, inv = norm(tok_ref[:, 0].reshape(seq_len, width).astype(F32))
    n1 = (hat * gain_ref[0:1]).astype(BF)
    acc[:, : 3 * width] += dot(n1, dqkv, TN)
    dn1 = dot(dqkv, w_ref[:, : 3 * width], NT)
    rows_acc[0:1] += jnp.sum(dn1 * hat, axis=0, keepdims=True)
    gtok = res_grad + norm_back(dn1 * gain_ref[0:1], hat, inv)
    gtok = jnp.where(keep, gtok, 0.0).astype(BF)
    gtok_ref[:, 0] = gtok.reshape(gtok_ref.shape[0], gtok_ref.shape[2], width)

    @pl.when(img == pl.num_programs(0) - 1)
    def _():
        for r in range(4):
            rows_acc[pl.ds(8 + (own ^ r), 1)] = rows_acc[16 + r : 17 + r]
        tail = rows_acc[...].T.astype(BF)
        mid = keep_ref.shape[1]
        for core, left, right in ((0, keep_ref, give_ref), (1, give_ref, keep_ref)):

            @pl.when((own & 1) == core)
            def _():
                left[...] = acc[:, :mid].astype(BF)
                right[:, : 4 * width - mid] = acc[:, mid:].astype(BF)
                right[:, 4 * width - mid :] = tail


def attn_bwd(own, d0, d1, d2, n2, cot, res, ctx, qkv, fused, w, gains, wr):
    images, seq_len, width = res.shape
    parts, _, seg, _ = fused.shape
    half = images // 2
    item = lambda a: pl.BlockSpec((1,) + a.shape[1:], lambda i, *_: (i, 0, 0))
    whole = lambda a: pl.BlockSpec(a.shape, lambda i, *_: (0, 0))
    cols = 4 * width + SMALL

    def side(a, k):
        return pl.BlockSpec(
            (1,) + a.shape[1:], lambda i, *_: (jnp.clip(i - k * half, 0, half - 1), 0, 0)
        )

    halves = [*d0, *d1, *d2, *n2, *cot]
    return pl.pallas_call(
        attn_bwd_kernel,
        grid_spec=pltpu.PrefetchScalarGridSpec(
            num_scalar_prefetch=1,
            grid=(images,),
            in_specs=[side(a, k % 2) for k, a in enumerate(halves)]
            + [item(a) for a in (res, ctx, qkv)]
            + [
                pl.BlockSpec((parts, 1, seg, width), lambda i, *_: (0, i, 0, 0)),
                pl.BlockSpec((parts, 1, seg, 128), lambda i, *_: (0, i, 0, 2 * width // 128)),
            ]
            + [whole(a) for a in (w, gains, wr)],
            out_specs=[
                pl.BlockSpec((parts, 1, seg, width), lambda i, *_: (0, i, 0, 0)),
                pl.BlockSpec((width, cols // 2), lambda i, *_: (0, 0)),
                pl.BlockSpec((width, cols // 2), lambda i, *_: (0, 0)),
            ],
            scratch_shapes=[
                pltpu.VMEM((width, 4 * width), F32),
                pltpu.VMEM((SMALL, width), F32),
                pltpu.VMEM(d0[0].shape[1:], F32),
                pltpu.VMEM((seq_len, width), BF),
                pltpu.VMEM(cot[0].shape[1:], BF),
            ],
        ),
        out_shape=[
            jax.ShapeDtypeStruct((parts, images, seg, width), BF),
            jax.ShapeDtypeStruct((width, cols // 2), BF),
            jax.ShapeDtypeStruct((width, cols // 2), BF),
        ],
        compiler_params=pltpu.CompilerParams(vmem_limit_bytes=30 * MIB),
        cost_estimate=cost(17),
    )(own, *halves, res, ctx, qkv, fused, fused, w, gains, wr)


def result_kernel(*refs):
    outs, res_ref, code_ref, gtok_ref, out_ref, sums = refs[:5], *refs[5:]
    img = pl.program_id(0)
    half = pl.num_programs(0) // 2
    seq_len, width = res_ref.shape[1:]
    for side in range(2):

        @pl.when((img >= side * half) & (img < (side + 1) * half))
        def _():
            one, two = outs[1 + side], outs[3 + side]
            sums[...] = outs[0][0].astype(F32) + one[0].astype(F32) + two[0].astype(F32)

    code = code_ref[:, 0].reshape(seq_len, 128)[:, 0:1].astype(F32)
    keep = (code.astype(jnp.int32) & 1) > 0
    out = (res_ref[0] + jnp.where(keep, sums[...].T, 0.0)).astype(BF)
    out_ref[:, 0, :, :width] = out.reshape(out_ref.shape[0], out_ref.shape[2], width)
    out_ref[:, 0, :, width:] = gtok_ref[:, 0]


def result(outs, o1, o2, res, fused, gtok):
    images, seq_len, width = res.shape
    parts, _, seg, _ = fused.shape
    half = images // 2

    def side(k):
        return pl.BlockSpec(
            (1, width, seq_len), lambda i: (jnp.clip(i - k * half, 0, half - 1), 0, 0)
        )

    return pl.pallas_call(
        result_kernel,
        grid=(images,),
        in_specs=[
            pl.BlockSpec((1, width, seq_len), lambda i: (i, 0, 0)),
            side(0),
            side(1),
            side(0),
            side(1),
            pl.BlockSpec((1, seq_len, width), lambda i: (i, 0, 0)),
            pl.BlockSpec((parts, 1, seg, 128), lambda i: (0, i, 0, 2 * width // 128)),
            pl.BlockSpec((parts, 1, seg, width), lambda i: (0, i, 0, 0)),
        ],
        out_specs=pl.BlockSpec((parts, 1, seg, 2 * width), lambda i: (0, i, 0, 0)),
        out_shape=jax.ShapeDtypeStruct((parts, images, seg, 2 * width), BF),
        scratch_shapes=[pltpu.VMEM((width, seq_len), F32)],
        compiler_params=pltpu.CompilerParams(vmem_limit_bytes=12 * MIB),
        cost_estimate=cost(2),
    )(outs, *o1, *o2, res, fused, gtok)


def finish_kernel(own_ref, mine_ref, other_ref, qkv_ref, proj_ref, small_ref):
    mid = mine_ref.shape[1]
    rest = qkv_ref.shape[1] - mid
    width = proj_ref.shape[1]
    for core, left, right in ((0, mine_ref, other_ref), (1, other_ref, mine_ref)):

        @pl.when((own_ref[0] & 1) == core)
        def _():
            qkv_ref[:, :mid] = left[...].astype(F32)
            qkv_ref[:, mid:] = right[:, :rest].astype(F32)
            proj_ref[...] = right[:, rest : rest + width].astype(F32)
            small_ref[...] = right[:, rest + width : rest + width + 128].astype(F32)


def finish(own, mine, other, width):
    rows = mine.shape[0]
    whole = pl.BlockSpec(memory_space=pltpu.VMEM)
    shape = lambda w: jax.ShapeDtypeStruct((rows, w), F32)
    return pl.pallas_call(
        finish_kernel,
        in_specs=[pl.BlockSpec(memory_space=pltpu.SMEM), whole, whole],
        out_specs=[whole] * 3,
        out_shape=[shape(3 * width), shape(width), shape(128)],
        compiler_params=pltpu.CompilerParams(vmem_limit_bytes=8 * MIB),
        cost_estimate=cost(1),
    )(own, mine, other)


def ring_gather(x, m, fw, bw, cut, hook):
    ahead, behind = [], []
    a = b = x
    for step in range(m // 2 - 1):
        a, b = send(a, "fsdp", fw), send(b, "fsdp", bw)
        ahead.append(a)
        behind.append(b)
        a, b = hook(step, a, b)
    top, bottom = cut(a)[0], cut(b)[1]
    return ahead, behind, send(top, "fsdp", fw), send(bottom, "fsdp", bw)


def halves_gather(parts, m, fw, bw, last=lambda a: a):
    ahead, behind = [], []
    f, b = list(parts), list(parts)
    for _ in range(m // 2 - 1):
        first, second = send(f[0], "fsdp", fw), send(b[1], "fsdp", bw)
        f, b = [first, send(f[1], "fsdp", fw)], [send(b[0], "fsdp", bw), second]
        ahead.append(f)
        behind.append(b)
    return ahead, behind, send(last(f[0]), "fsdp", fw), send(last(b[1]), "fsdp", bw)


def halves_scatter(ahead, behind, far, fw, bw, wait=lambda a: a, seen=None):
    out = []
    for terms, pairs, whole in ((ahead, fw, 0), (behind, bw, 1)):
        got = [None, None]
        for half in (whole, 1 - whole):
            acc = far[half] if half == whole else None
            for term in reversed(terms):
                acc = term[half] if acc is None else add_low(term[half], wait(send(acc, "fsdp", pairs)))
                if seen is not None and half == whole:
                    seen.append(acc)
            got[half] = send(acc, "fsdp", pairs)
        out.append(got)
    return out


def ring_scatter(ahead, behind, top, bottom, fw, bw, put):
    a, b = send(top, "fsdp", fw), send(bottom, "fsdp", bw)
    first = True
    for to_fw, to_bw in zip(reversed(ahead), reversed(behind)):
        if first:
            a, b = put(to_fw, a, 0), put(to_bw, b, 1)
            first = False
        else:
            a, b = add_low(to_fw, a), add_low(to_bw, b)
        a, b = send(a, "fsdp", fw), send(b, "fsdp", bw)
    return a, b


def after(x, *done):
    return lax.optimization_barrier((x,) + done)[0]


def per_device(
    tokens, pad_mask, routes, ln1_gain, w_qkv, w_proj, ln2_gain, w_router, exp_in, exp_out, cotangent
):
    n = lax.axis_size("fsdp")
    per_device_images, seg, width = tokens.shape
    seq_idx = lax.axis_index("seq")
    own = seq_idx.astype(jnp.int32).reshape(1)
    idx = lax.axis_index("fsdp")
    m = n // 2
    fw8, bw8 = ring_pairs([ring_order(n)])
    low_ring = ring_order(m)
    fw4, bw4 = ring_pairs([low_ring, [m + i for i in low_ring]])
    pair = [(i, (i + m) % n) for i in range(n)]
    by_core = [(i, i ^ 1) for i in range(4)]
    by_half = [(i, i ^ 2) for i in range(4)]

    rows = w_qkv.shape[0]
    small = jnp.concatenate([ln1_gain[:, None], ln2_gain[:, None]], axis=1)
    small = jnp.pad(small, ((0, 0), (0, SMALL - 2))) + jnp.pad(
        w_router, ((0, 0), (8, SMALL - 12))
    )
    block = block_of(own, w_qkv, w_proj, small)
    mid, cut = block.shape[1], 5 * 128

    fr = exp_in.shape[0]
    pick = lambda a: lax.dynamic_index_in_dim(a, seq_idx, 1, False)
    mine = jnp.stack([pick(exp_in), pick(exp_out)]).astype(BF)
    part = lambda k: mine[:, k * fr // 2 : (k + 1) * fr // 2]

    keep = pad_mask.astype(BF)[..., None]
    code = pad_mask + 2 * routes[..., 0] + 8 * routes[..., 1]
    code = jnp.pad(code.astype(BF)[..., None], ((0, 0), (0, 0), (0, 127)))
    fused = jnp.concatenate([tokens * keep, cotangent * keep, code], axis=2)
    images = per_device_images // 4
    half_img = images // 2
    fused = lax.all_to_all(
        fused.reshape(4, images, seg, 2 * width + 128),
        "seq",
        split_axis=0,
        concat_axis=0,
        tiled=True,
    )
    cot = unpack(fused, width)

    fw = lambda a: send(a, "fsdp", fw8)
    bw = lambda a: send(a, "fsdp", bw8)
    steps = [(block, block)]
    q0, g0 = [], None
    for d in range(1, m):
        a, b = steps[-1]
        if d == m - 1 and m > 2:
            a, b = after((a, b), *q0)
        steps.append((fw(a), bw(b)))
        if d == 1:
            q0.append(send(after(part(0), *steps[-1]), "fsdp", pair))
    a, b = steps[-1]
    top, bottom = fw(a[:, :cut]), bw(b[:, cut:])
    q0.append(send(after(part(1), a, b), "fsdp", pair))

    place = jnp.where(idx % 2 == 0, idx // 2, n - 1 - idx // 2)

    def at_place(p):
        p = p % n
        return jnp.where(p < m, 2 * p, 2 * (n - 1 - p) + 1)

    pieces, offs, cuts = [block], [idx], [(0, mid)]
    for d in range(1, m):
        pieces += steps[d]
        offs += [at_place(place - d + n), at_place(place + d)]
        cuts += [(0, mid)] * 2
    pieces += [top, bottom]
    offs += [at_place(place + m)] * 2
    cuts += [(0, cut), (cut, mid)]
    offs = jnp.stack(offs).astype(jnp.int32) * rows
    w_mine = gather_rows(pieces, offs, cuts, (n * rows, mid))
    w_other = send(w_mine, "seq", by_core)

    g_ahead, g_behind, g_top, g_bottom = halves_gather(
        [after(c, top, bottom) for c in cot], m, fw4, bw4
    )
    g_near = sum(g_ahead + g_behind, [])

    win = exp_in.transpose(1, 0, 2).astype(BF)
    wout = exp_out.transpose(1, 0, 2).astype(BF)
    q2 = [send(after(q0[0], w_mine), "seq", by_half)]
    *n2, res, qkv, ctx, w, gains, wr = attn_fwd(
        own, after(fused, *q2), w_mine, w_other, width
    )
    q2.append(send(after(q0[1], *n2), "seq", by_half))
    n2 = after(tuple(n2), *g_near)
    quarters = [
        q0,
        [send(q, "seq", by_core) for q in q0],
        q2,
        [send(q, "seq", by_core) for q in q2],
    ]

    win, wout, wint, woutt = weights(own, win, wout, sum(quarters, []))
    units = images * m
    bufs, at = None, 0

    def experts(xs, gs):
        nonlocal at, bufs
        *dd, b0, b1, b2, b3 = moe_call(
            xs, gs, own, wr, win, wout, wint, at, units, bufs
        )
        bufs = [b0, b1, b2, b3]
        at += images
        return dd

    d_own = experts(n2, cot)
    x_ahead, x_behind, x_top, x_bottom = halves_gather(
        n2, m, fw4, bw4, lambda a: after(a, *d_own)
    )
    dx_ahead, dx_behind, where = [], [], []
    for d in range(m // 2 - 1):
        (xa, xb), (ga, gb) = (x_ahead[d], x_behind[d]), (g_ahead[d], g_behind[d])
        where.append(at)
        back0, on1 = experts([xa[0], xb[1]], [ga[0], gb[1]])
        back1, on0 = experts([xa[1], xb[0]], [ga[1], gb[0]])
        dx_ahead.append([on0, on1])
        dx_behind.append([back0, back1])
    far_at = at
    far = experts([x_top, x_bottom], [g_top, g_bottom])
    ga, hg, xb, gb = bufs

    grad3 = moe_grad(ga, hg, xb, gb, 3)
    grad2 = moe_grad(after(ga, grad3), hg, xb, gb, 2)
    grad1 = moe_grad(after(ga, grad2), hg, xb, gb, 1)
    seen = []
    d1, d2 = halves_scatter(
        dx_ahead, dx_behind, far, fw4, bw4, lambda a: after(a, grad1), seen
    )
    grad0 = moe_grad(after(ga, *seen), hg, xb, gb, 0)
    kept2 = add_low(grad2, send(grad3, "seq", by_core))
    kept0 = add_low(grad0, send(grad1, "seq", by_core))
    outs = moe_out(woutt, after(ga, grad0))
    first_half = send(kept2[1], "seq", by_half)
    kept_pair = add_low(kept0[1], first_half)
    d_own = [after(d_own[0], outs, kept_pair), d_own[1]]

    gtok, dw_keep, dw_give = attn_bwd(
        own, d_own, d1, d2, n2, cot, res, ctx, qkv, fused, w, gains, wr
    )

    outs = after(outs, *d1, *d2)
    out_at = lambda k: outs[k : k + half_img]
    o_ahead = [[out_at(k + 3 * half_img), out_at(k + half_img)] for k in where]
    o_behind = [[out_at(k), out_at(k + 2 * half_img)] for k in where]
    firsts = []

    def hold(a):
        firsts.append(a)
        return after(a, dw_keep)

    o1, o2 = halves_scatter(
        o_ahead, o_behind, (out_at(far_at), out_at(far_at + half_img)), fw4, bw4, hold
    )
    from_pair = [send(kept_pair[k], "fsdp", pair) for k in range(2)]

    dw_give = after(dw_give, from_pair[0], *firsts[: 2 if m == 4 else 0])
    dw = add_low(dw_keep, send(dw_give, "seq", by_core))

    def term(p):
        return lax.dynamic_slice_in_dim(dw, at_place(p) * rows, rows, 0)

    def put_cols(t, part, side):
        if side == 0:
            return jnp.concatenate([add_low(t[:, :cut], part), t[:, cut:]], axis=1)
        return jnp.concatenate([t[:, :cut], add_low(t[:, cut:], part)], axis=1)

    last = term(place + m)
    s1, s2 = ring_scatter(
        [term(place + d) for d in range(1, m)],
        [term(place - d + n) for d in range(1, m)],
        last[:, :cut],
        last[:, cut:],
        fw8,
        bw8,
        put_cols,
    )
    dense = (term(place).astype(F32) + s1.astype(F32) + s2.astype(F32)).astype(BF)
    dense = add_low(dense, send(dense, "seq", by_half))
    g_qkv, g_proj, g_small = finish(own, dense, send(dense, "seq", by_core), width)

    back = lax.all_to_all(
        result(outs, o1, o2, res, fused, gtok), "seq", split_axis=0, concat_axis=0, tiled=True
    ).reshape(per_device_images, seg, 2 * width)

    from_half = after(send(kept2[0], "seq", by_half), dw_keep)
    quarter = add_low(add_low(kept0[0], from_half), jnp.stack(from_pair))
    from_half = send(quarter, "seq", by_half)
    grad_in, grad_out = pack(
        own,
        [quarter, send(quarter, "seq", by_core), from_half, send(from_half, "seq", by_core)],
    )

    return (
        back[:, :, :width],
        back[:, :, width:].astype(F32),
        g_small[:, 0],
        g_qkv,
        g_proj,
        g_small[:, 1],
        g_small[:, 8:12],
        grad_in,
        grad_out,
    )


def solution(mesh):
    row = P("fsdp", None)
    cube = P("fsdp", None, None)
    split = P("fsdp", "seq", None)
    return jax.shard_map(
        per_device,
        mesh=mesh,
        in_specs=(
            split,
            P("fsdp", "seq"),
            split,
            P("fsdp"),
            row,
            row,
            P("fsdp"),
            row,
            cube,
            cube,
            split,
        ),
        out_specs=(split, split, P("fsdp"), row, row, P("fsdp"), row, cube, cube),
        check_vma=False,
    )
```

```python
import jax
import jax.numpy as jnp
from jax import lax
from jax.experimental import pallas as pl
from jax.experimental.pallas import tpu as pltpu
from jax.sharding import PartitionSpec as P

BF = jnp.bfloat16
F32 = jnp.float32
HEADS = 8
HEAD = 64
EPS = 1e-06
SQRT_HALF = 0.7071067811865476
INV_ROOT_TWO_PI = 0.3989422804014327
SMALL = 256
CODE_ROWS = 16
NT = (((1,), (1,)), ((), ()))
TN = (((0,), (0,)), ((), ()))
MIB = 1 << 20
PACE = 0.0001


def cost(us):
    return pl.CostEstimate(
        flops=int(us * 1.15e9 * PACE) + 1, bytes_accessed=int(us * 1e5 * PACE) + 1, transcendentals=0
    )


def dot(a, b, dims=(((1,), (0,)), ((), ()))):
    return lax.dot_general(a, b, dims, preferred_element_type=F32)


def ring_order(n):
    return [2 * i for i in range(n // 2)] + [2 * i + 1 for i in reversed(range(n // 2))]


def ring_pairs(orders):
    fw = []
    for order in orders:
        n = len(order)
        fw += [(order[i], order[(i + 1) % n]) for i in range(n)]
    return fw, [(b, a) for a, b in fw]


def send(x, axis, pairs):
    return lax.ppermute(x, axis, pairs)


def add_low(a, b):
    return (a.astype(F32) + b.astype(F32)).astype(BF)


def norm(v):
    c = v - jnp.mean(v, axis=-1, keepdims=True)
    inv = lax.rsqrt(jnp.mean(c * c, axis=-1, keepdims=True) + EPS)
    return c * inv, inv


def norm_back(u, hat, inv):
    return inv * (
        u
        - jnp.mean(u, axis=-1, keepdims=True)
        - hat * jnp.mean(u * hat, axis=-1, keepdims=True)
    )


def block_kernel(own_ref, qkv_ref, proj_ref, small_ref, out_ref):
    mid = out_ref.shape[1]
    rest = qkv_ref.shape[1] - mid
    width = proj_ref.shape[1]

    @pl.when((own_ref[0] & 1) == 0)
    def _():
        out_ref[...] = qkv_ref[:, :mid].astype(BF)

    @pl.when((own_ref[0] & 1) == 1)
    def _():
        out_ref[:, :rest] = qkv_ref[:, mid:].astype(BF)
        out_ref[:, rest : rest + width] = proj_ref[...].astype(BF)
        out_ref[:, rest + width :] = small_ref[...].astype(BF)


def block_of(own, w_qkv, w_proj, small):
    rows = w_qkv.shape[0]
    mid = (w_qkv.shape[1] + w_proj.shape[1] + SMALL) // 2
    whole = pl.BlockSpec(memory_space=pltpu.VMEM)
    return pl.pallas_call(
        block_kernel,
        in_specs=[pl.BlockSpec(memory_space=pltpu.SMEM)] + [whole] * 3,
        out_specs=whole,
        out_shape=jax.ShapeDtypeStruct((rows, mid), BF),
        compiler_params=pltpu.CompilerParams(vmem_limit_bytes=8 * MIB),
        cost_estimate=cost(1),
    )(own, w_qkv, w_proj, small)


def unpack_kernel(own_ref, p0, p1, p2, p3, tok_ref, code_ref, cot_ref):
    own = own_ref[0]
    seg, width = tok_ref.shape[2:]
    for r, piece in enumerate((p0, p1, p2, p3)):
        at = own ^ r
        tok_ref[at, 0] = piece[0, :, :width]
        code_ref[at, 0] = piece[0, :, 2 * width :]
        cot_ref[0, pl.ds(pl.multiple_of(at * seg, seg), seg)] = piece[0, :, width : 2 * width]

    seq_len = 4 * seg
    code = code_ref[:, 0].astype(F32).reshape(seq_len, 128).T
    cot_ref[0, seq_len:, :seq_len] = code[:CODE_ROWS].astype(BF)
    cot_ref[0, seq_len:, seq_len:] = jnp.zeros((CODE_ROWS, width - seq_len), BF)


def unpack(own, pieces, width):
    images, seg, cols = pieces[0].shape
    rows = 4 * seg + CODE_ROWS
    piece = pl.BlockSpec((1, seg, cols), lambda i: (i, 0, 0))
    nat = lambda w: pl.BlockSpec((4, 1, seg, w), lambda i: (0, i, 0, 0))
    shape = lambda *d: jax.ShapeDtypeStruct(d, BF)
    return pl.pallas_call(
        unpack_kernel,
        grid=(images,),
        in_specs=[pl.BlockSpec(memory_space=pltpu.SMEM)] + [piece] * 4,
        out_specs=[nat(width), nat(128), pl.BlockSpec((1, rows, width), lambda i: (i, 0, 0))],
        out_shape=[
            shape(4, images, seg, width),
            shape(4, images, seg, 128),
            shape(images, rows, width),
        ],
        compiler_params=pltpu.CompilerParams(vmem_limit_bytes=8 * MIB),
        cost_estimate=cost(1.5),
    )(own, *pieces)


def gather_kernel(n_pieces, offs, *refs):
    pieces, out_ref, sems = refs[:n_pieces], refs[n_pieces], refs[n_pieces + 1]
    copies, k = [], 0
    for piece in pieces:
        for part in range(piece.shape[0]):
            rows = piece.shape[1]
            off = pl.multiple_of(offs[k], rows)
            copies.append(
                pltpu.make_async_copy(piece.at[part], out_ref.at[pl.ds(off, rows)], sems.at[k])
            )
            k += 1
    for copy in copies:
        copy.start()
    for copy in copies:
        copy.wait()


def gather_rows(pieces, offs, shape):
    n = len(pieces)
    anywhere = pl.BlockSpec(memory_space=pl.ANY)
    return pl.pallas_call(
        lambda *a: gather_kernel(n, *a),
        in_specs=[pl.BlockSpec(memory_space=pltpu.SMEM)] + [anywhere] * n,
        out_specs=pl.BlockSpec(memory_space=pltpu.VMEM),
        out_shape=jax.ShapeDtypeStruct(shape, BF),
        scratch_shapes=[pltpu.SemaphoreType.DMA((sum(p.shape[0] for p in pieces),))],
        compiler_params=pltpu.CompilerParams(vmem_limit_bytes=8 * MIB),
        cost_estimate=cost(2),
    )(offs, *pieces)


def attn_fwd_kernel(own_ref, tok_ref, code_ref, mine_ref, other_ref, *refs):
    n2a_ref, n2b_ref, res_ref, qkv_ref, ctx_ref, w_ref, gain_ref, wr_ref = refs
    img = pl.program_id(0)
    seq_len, width = res_ref.shape[1:]
    mid = mine_ref.shape[1]
    own = own_ref[0]

    @pl.when(img == 0)
    def _():
        for core, left, right in ((0, mine_ref, other_ref), (1, other_ref, mine_ref)):

            @pl.when((own & 1) == core)
            def _():
                w_ref[:, :mid] = left[...]
                w_ref[:, mid:] = right[...]

        small = w_ref[:, 4 * width : 4 * width + 128].astype(F32).T
        gain_ref[...] = small[0:16]
        for r in range(4):
            wr_ref[r : r + 1] = gain_ref[pl.ds(8 + (own ^ r), 1)]
        wr_ref[4:8] = jnp.zeros((4, width), F32)

    code = code_ref[:, 0].reshape(seq_len, 128).astype(F32)
    keep = (code[:, 0:1].astype(jnp.int32) & 1) > 0
    key_ok = (code.T[0:1].astype(jnp.int32) & 1) > 0
    x = tok_ref[:, 0].reshape(seq_len, width).astype(F32)
    hat, _ = norm(x)
    n1 = (hat * gain_ref[0:1]).astype(BF)
    qkv_ref[0] = dot(n1, w_ref[:, : 3 * width]).astype(BF)
    parts = []
    for h in range(HEADS):
        q = qkv_ref[0, :, h * HEAD : (h + 1) * HEAD]
        k = qkv_ref[0, :, width + h * HEAD : width + (h + 1) * HEAD]
        v = qkv_ref[0, :, 2 * width + h * HEAD : 2 * width + (h + 1) * HEAD]
        s = jnp.where(key_ok, dot(q, k, NT) * 0.125, -1e30)
        e = jnp.exp(s - jnp.max(s, axis=-1, keepdims=True))
        p = (e * (1.0 / jnp.sum(e, axis=-1, keepdims=True))).astype(BF)
        parts.append(dot(p, v))
    ctx = jnp.concatenate(parts, axis=1).astype(BF)
    ctx_ref[0] = ctx
    res = x + jnp.where(keep, dot(ctx, w_ref[:, 3 * width : 4 * width]), 0.0)
    res_ref[0] = res
    hat2, _ = norm(res)
    n2 = (hat2 * gain_ref[1:2]).astype(BF)
    half = pl.num_programs(0) // 2
    for k, ref in ((0, n2a_ref), (1, n2b_ref)):

        @pl.when((img >= k * half) & (img < (k + 1) * half))
        def _():
            ref[0] = n2


def attn_fwd(own, tok, code, mine, other):
    parts, images, seg, width = tok.shape
    seq_len, half = parts * seg, images // 2
    row = lambda w: pl.BlockSpec((1, seq_len, w), lambda i, *_: (i, 0, 0))
    whole = lambda s: pl.BlockSpec(s, lambda i, *_: (0,) * len(s))
    side = lambda k: pl.BlockSpec(
        (1, seq_len, width), lambda i, *_: (jnp.clip(i - k * half, 0, half - 1), 0, 0)
    )
    cols = 4 * width + SMALL
    return pl.pallas_call(
        attn_fwd_kernel,
        grid_spec=pltpu.PrefetchScalarGridSpec(
            num_scalar_prefetch=1,
            grid=(images,),
            in_specs=[
                pl.BlockSpec((parts, 1, seg, width), lambda i, *_: (0, i, 0, 0)),
                pl.BlockSpec((parts, 1, seg, 128), lambda i, *_: (0, i, 0, 0)),
                whole(mine.shape),
                whole(other.shape),
            ],
            out_specs=[
                side(0),
                side(1),
                row(width),
                row(3 * width),
                row(width),
                whole((width, cols)),
                whole((16, width)),
                whole((8, width)),
            ],
        ),
        out_shape=[
            jax.ShapeDtypeStruct((half, seq_len, width), BF),
            jax.ShapeDtypeStruct((half, seq_len, width), BF),
            jax.ShapeDtypeStruct((images, seq_len, width), F32),
            jax.ShapeDtypeStruct((images, seq_len, 3 * width), BF),
            jax.ShapeDtypeStruct((images, seq_len, width), BF),
            jax.ShapeDtypeStruct((width, cols), BF),
            jax.ShapeDtypeStruct((16, width), F32),
            jax.ShapeDtypeStruct((8, width), F32),
        ],
        compiler_params=pltpu.CompilerParams(vmem_limit_bytes=20 * MIB),
        cost_estimate=cost(8),
    )(own, tok, code, mine, other)


def router(own, n2, wr, code):
    ids = lax.broadcasted_iota(jnp.int32, (8, n2.shape[0]), 0)
    logits = jnp.where(ids < 4, dot(wr.astype(BF), n2, NT), -1e30)
    e = jnp.exp(logits - jnp.max(logits, axis=0, keepdims=True))
    probs = e * (1.0 / jnp.sum(e, axis=0, keepdims=True))
    route = code.astype(F32).astype(jnp.int32)
    first = (route >> 1) & 3
    second = route >> 3
    ids = ids ^ own
    chosen = ((ids == first) | (ids == second)).astype(F32)
    return probs, chosen


def weights_kernel(own_ref, *refs):
    win_ref, wout_ref = refs[:2]
    pieces = refs[2:-4]
    parts = len(pieces) // 4
    all_in, all_out, in_t, out_t = refs[-4:]
    own = own_ref[0]
    rows = win_ref.shape[1]
    for b in range(8):
        sl = slice(b * rows, (b + 1) * rows)
        if b < 4:
            a, c = win_ref[own ^ b], wout_ref[own ^ b]
        else:
            mine = pieces[(b - 4) * parts : (b - 3) * parts]
            a, c = (jnp.concatenate([p[k] for p in mine], axis=0) for k in range(2))
        all_in[sl] = a
        all_out[sl] = c
        in_t[:, sl] = a.T
        out_t[:, sl] = c.T


def weights(own, win, wout, pieces):
    rows, width = win.shape[1:]
    whole = pl.BlockSpec(memory_space=pltpu.VMEM)
    flat = jax.ShapeDtypeStruct((8 * rows, width), BF)
    turned = jax.ShapeDtypeStruct((width, 8 * rows), BF)
    return pl.pallas_call(
        weights_kernel,
        in_specs=[pl.BlockSpec(memory_space=pltpu.SMEM)] + [whole] * (2 + len(pieces)),
        out_specs=[whole] * 4,
        out_shape=[flat, flat, turned, turned],
        compiler_params=pltpu.CompilerParams(vmem_limit_bytes=16 * MIB),
        cost_estimate=cost(3),
    )(own, win, wout, *pieces)


def moe_kernel(starts, n_aliased, own_ref, wr_ref, win_ref, wout_ref, wint_ref, *refs):
    n = len(starts)
    xs, gs = refs[:n], refs[n : 2 * n]
    refs = refs[2 * n + n_aliased :]
    dx_refs = refs[:n]
    ga_ref, hg_ref, xo_ref, go_ref = refs[n:]
    step = pl.program_id(0)
    seq_len, width = xo_ref.shape[1:]
    rows = win_ref.shape[0] // 8
    within = []
    for j in range(n):
        low, high = starts[j], starts[j + 1] if j + 1 < n else None
        within.append((step >= low) if high is None else ((step >= low) & (step < high)))

        @pl.when(within[j])
        def _():
            xo_ref[0] = xs[j][0]
            go_ref[0] = gs[j][0]

    x = xo_ref[0]
    g = go_ref[0, :seq_len]
    probs, chosen = router(own_ref[0], x, wr_ref[...], go_ref[0, seq_len : seq_len + 1, :seq_len])
    gate = probs * chosen
    sums = [None] * 4
    for b in range(8):
        e = b % 4
        sl = slice(b * rows, (b + 1) * rows)
        h = dot(win_ref[sl], x, NT)
        u = dot(wout_ref[sl], g, NT)
        cumul = 0.5 * (1.0 + lax.erf(h * SQRT_HALF))
        slope = cumul + h * (INV_ROOT_TWO_PI * jnp.exp(-0.5 * h * h))
        act = h * cumul
        row = gate[e : e + 1]
        ga_ref[0, sl] = (act * row).astype(BF)
        hg_ref[0, sl] = (u * row * slope).astype(BF)
        part = jnp.sum(act * u, axis=0, keepdims=True)
        sums[e] = part if sums[e] is None else sums[e] + part
    dx = dot(wint_ref[...], hg_ref[0]).astype(BF)
    pad = jnp.zeros((CODE_ROWS - 4, seq_len), F32)
    tail = jnp.concatenate(sums + [pad], axis=0).astype(BF)
    for j in range(n):

        @pl.when(within[j])
        def _():
            dx_refs[j][0, :width] = dx
            dx_refs[j][0, width:] = tail


def moe_call(xs, gs, own, wr, win, wout, wint, first, units, bufs):
    n = len(xs)
    counts = [x.shape[0] for x in xs]
    starts = [sum(counts[:j]) for j in range(n)]
    total = sum(counts)
    seq_len, width = xs[0].shape[1:]
    f = win.shape[0]
    g_rows = gs[0][0].shape[1]

    def item(rows, j, at=0):
        lo, c = starts[j], counts[j]
        return pl.BlockSpec(
            (1, rows, width), lambda i: (at + jnp.clip(i - lo, 0, c - 1), 0, 0)
        )

    def out_item(j):
        lo, c = starts[j], counts[j]
        return pl.BlockSpec(
            (1, width + CODE_ROWS, seq_len), lambda i: (jnp.clip(i - lo, 0, c - 1), 0, 0)
        )

    whole = lambda s: pl.BlockSpec(s, lambda i: (0, 0), pipeline_mode=pl.Buffered(1))
    buf = lambda r, w: pl.BlockSpec((1, r, w), lambda i: (first + i, 0, 0))
    aliased = [] if bufs is None else list(bufs)
    base = 5 + 2 * n
    return pl.pallas_call(
        lambda *a: moe_kernel(starts, len(aliased), *a),
        grid=(total,),
        in_specs=[pl.BlockSpec(memory_space=pltpu.SMEM)]
        + [whole(wr.shape), whole(win.shape), whole(wout.shape), whole(wint.shape)]
        + [item(seq_len, j) for j in range(n)]
        + [item(g_rows, j, gs[j][1]) for j in range(n)]
        + [pl.BlockSpec(memory_space=pl.ANY)] * len(aliased),
        out_specs=[out_item(j) for j in range(n)]
        + [
            buf(f, seq_len),
            buf(f, seq_len),
            buf(seq_len, width),
            buf(g_rows, width),
        ],
        out_shape=[
            jax.ShapeDtypeStruct((c, width + CODE_ROWS, seq_len), BF) for c in counts
        ]
        + [
            jax.ShapeDtypeStruct((units, f, seq_len), BF),
            jax.ShapeDtypeStruct((units, f, seq_len), BF),
            jax.ShapeDtypeStruct((units, seq_len, width), BF),
            jax.ShapeDtypeStruct((units, g_rows, width), BF),
        ],
        input_output_aliases={base + k: n + k for k in range(len(aliased))},
        compiler_params=pltpu.CompilerParams(vmem_limit_bytes=16 * MIB),
        cost_estimate=cost(2.6 * total),
    )(own, wr, win, wout, wint, *xs, *[g for g, _ in gs], *aliased)


def moe_out_kernel(woutt_ref, ga_ref, out_ref):
    out_ref[0] = dot(woutt_ref[...], ga_ref[0]).astype(BF)


def moe_out(woutt, ga):
    units, f, seq_len = ga.shape
    width = woutt.shape[0]
    return pl.pallas_call(
        moe_out_kernel,
        grid=(units,),
        in_specs=[
            pl.BlockSpec((width, f), lambda i: (0, 0), pipeline_mode=pl.Buffered(1)),
            pl.BlockSpec((1, f, seq_len), lambda i: (i, 0, 0)),
        ],
        out_specs=pl.BlockSpec((1, width, seq_len), lambda i: (i, 0, 0)),
        out_shape=jax.ShapeDtypeStruct((units, width, seq_len), BF),
        compiler_params=pltpu.CompilerParams(vmem_limit_bytes=8 * MIB),
        cost_estimate=cost(0.7 * units),
    )(woutt, ga)


def moe_grad_kernel(groups, ga_ref, hg_ref, x_ref, g_ref, out_ref, acc_in, acc_out):
    seq_len = x_ref.shape[1]
    part = pl.program_id(1)
    a_in = a_out = None
    for u in range(x_ref.shape[0]):
        t_in = dot(hg_ref[u], x_ref[u])
        t_out = dot(ga_ref[u], g_ref[u, :seq_len])
        a_in = t_in if a_in is None else a_in + t_in
        a_out = t_out if a_out is None else a_out + t_out
    if groups == 1:
        out_ref[0, 0] = a_in.astype(BF)
        out_ref[0, 1] = a_out.astype(BF)
        return

    @pl.when(part == 0)
    def _():
        acc_in[...] = jnp.zeros_like(acc_in)
        acc_out[...] = jnp.zeros_like(acc_out)

    acc_in[...] += a_in
    acc_out[...] += a_out

    @pl.when(part == groups - 1)
    def _():
        out_ref[0, 0] = acc_in[...].astype(BF)
        out_ref[0, 1] = acc_out[...].astype(BF)


def moe_grad(ga, hg, xb, gb, r):
    units, f, seq_len = ga.shape
    width = xb.shape[2]
    rows = f // 8
    per = min(units, 8)
    groups = units // per
    act = pl.BlockSpec((per, rows, seq_len), lambda b, p: (p, 4 * b + r, 0))
    return pl.pallas_call(
        lambda *a: moe_grad_kernel(groups, *a),
        grid=(2, groups),
        in_specs=[
            act,
            act,
            pl.BlockSpec((per, seq_len, width), lambda b, p: (p, 0, 0)),
            pl.BlockSpec((per, gb.shape[1], width), lambda b, p: (p, 0, 0)),
        ],
        out_specs=pl.BlockSpec((1, 2, rows, width), lambda b, p: (b, 0, 0, 0)),
        out_shape=jax.ShapeDtypeStruct((2, 2, rows, width), BF),
        scratch_shapes=[pltpu.VMEM((rows, width), F32)] * 2,
        compiler_params=pltpu.CompilerParams(vmem_limit_bytes=18 * MIB),
        cost_estimate=cost(0.47 * units),
    )(ga, hg, xb, gb)


def pack_kernel(own_ref, *refs):
    pieces = refs[:4]
    in_ref, out_ref = refs[4:]
    own = own_ref[0]
    for k in range(4):

        @pl.when(own == k)
        def _():
            for e in range(4):
                in_ref[:, e, :] = pieces[k ^ e][0].astype(F32)
                out_ref[:, e, :] = pieces[k ^ e][1].astype(F32)


def pack(own, pieces):
    rows, width = pieces[0].shape[1:]
    tile = min(rows, 64)
    piece = pl.BlockSpec((2, tile, width), lambda i: (0, i, 0))
    out = pl.BlockSpec((tile, 4, width), lambda i: (i, 0, 0))
    shape = jax.ShapeDtypeStruct((rows, 4, width), F32)
    return pl.pallas_call(
        pack_kernel,
        grid=(rows // tile,),
        in_specs=[pl.BlockSpec(memory_space=pltpu.SMEM)] + [piece] * 4,
        out_specs=[out, out],
        out_shape=[shape, shape],
        compiler_params=pltpu.CompilerParams(vmem_limit_bytes=24 * MIB),
        cost_estimate=cost(3),
    )(own, *pieces)


def attn_bwd_kernel(
    own_ref,
    *refs,
):
    items, refs = refs[:8], refs[8:]
    (
    cot_blk,
    res_ref,
    ctx_ref,
    qkv_ref,
    tok_ref,
    code_ref,
    w_ref,
    gain_ref,
    wr_ref,
    *gtok_refs,
    keep_ref,
    give_ref,
    acc,
    rows_acc,
    sums,
    n2_ref,
    gtok_ref,
    ) = refs
    cot_ref = cot_blk.at[0]
    own = own_ref[0]
    img = pl.program_id(0)
    seq_len, width = n2_ref.shape

    @pl.when(img == 0)
    def _():
        acc[...] = jnp.zeros_like(acc)
        rows_acc[...] = jnp.zeros_like(rows_acc)

    half = pl.num_programs(0) // 2
    for side in range(2):

        @pl.when((img >= side * half) & (img < (side + 1) * half))
        def _():
            d0, d1, d2, n2 = (items[2 * t + side] for t in range(4))
            sums[...] = d0[0].astype(F32) + d1[0].astype(F32) + d2[0].astype(F32)
            n2_ref[...] = n2[0]

    code = code_ref[:, 0].reshape(seq_len, 128)[:, 0:1].astype(F32)
    keep = (code.astype(jnp.int32) & 1) > 0
    total = sums[...]
    n2 = n2_ref[...]
    probs, chosen = router(own, n2, wr_ref[...], cot_ref[seq_len : seq_len + 1, :seq_len])
    gate_grad = chosen * total[width : width + 8]
    logit_grad = probs * (gate_grad - jnp.sum(probs * gate_grad, axis=0, keepdims=True))
    high = logit_grad.astype(BF)
    low = (logit_grad - high.astype(F32)).astype(BF)
    rows_acc[16:24] += dot(high, n2) + dot(low, n2)
    wr = wr_ref[...].astype(BF)
    dn2 = (total[:width] + dot(wr, high, TN) + dot(wr, low, TN)).T
    hat2, inv2 = norm(res_ref[0])
    rows_acc[1:2] += jnp.sum(dn2 * hat2, axis=0, keepdims=True)
    res_grad = cot_ref[:seq_len].astype(F32) + norm_back(dn2 * gain_ref[1:2], hat2, inv2)
    pg = jnp.where(keep, res_grad, 0.0).astype(BF)
    acc[:, 3 * width :] += dot(ctx_ref[0], pg, TN)
    dctx = dot(pg, w_ref[:, 3 * width : 4 * width], NT).astype(BF)
    dqs, dks, dvs = [], [], []
    for h in range(HEADS):
        q = qkv_ref[0, :, h * HEAD : (h + 1) * HEAD]
        k = qkv_ref[0, :, width + h * HEAD : width + (h + 1) * HEAD]
        v = qkv_ref[0, :, 2 * width + h * HEAD : 2 * width + (h + 1) * HEAD]
        do = dctx[:, h * HEAD : (h + 1) * HEAD]
        s = jnp.where(keep, dot(k, q, NT) * 0.125, -1e30)
        e = jnp.exp(s - jnp.max(s, axis=0, keepdims=True))
        p = e * (1.0 / jnp.sum(e, axis=0, keepdims=True))
        dvs.append(dot(p.astype(BF), do))
        wg = dot(v, do, NT)
        sg = (p * (wg - jnp.sum(p * wg, axis=0, keepdims=True))).astype(BF)
        dqs.append(dot(sg, k, TN) * 0.125)
        dks.append(dot(sg, q) * 0.125)
    dqkv = jnp.concatenate(dqs + dks + dvs, axis=1).astype(BF)
    hat, inv = norm(tok_ref[:, 0].reshape(seq_len, width).astype(F32))
    n1 = (hat * gain_ref[0:1]).astype(BF)
    acc[:, : 3 * width] += dot(n1, dqkv, TN)
    dn1 = dot(dqkv, w_ref[:, : 3 * width], NT)
    rows_acc[0:1] += jnp.sum(dn1 * hat, axis=0, keepdims=True)
    gtok = res_grad + norm_back(dn1 * gain_ref[0:1], hat, inv)
    gtok = jnp.where(keep, gtok, 0.0).astype(BF)
    gtok_ref[...] = gtok.reshape(gtok_ref.shape)
    for r, ref in enumerate(gtok_refs):
        ref[0] = gtok_ref[own ^ r]

    @pl.when(img == pl.num_programs(0) - 1)
    def _():
        for r in range(4):
            rows_acc[pl.ds(8 + (own ^ r), 1)] = rows_acc[16 + r : 17 + r]
        tail = rows_acc[...].T.astype(BF)
        mid = keep_ref.shape[1]
        for core, left, right in ((0, keep_ref, give_ref), (1, give_ref, keep_ref)):

            @pl.when((own & 1) == core)
            def _():
                left[...] = acc[:, :mid].astype(BF)
                right[:, : 4 * width - mid] = acc[:, mid:].astype(BF)
                right[:, 4 * width - mid :] = tail


def attn_bwd(own, d0, d1, d2, n2, cot, res, ctx, qkv, tok, code, w, gains, wr):
    images, seq_len, width = res.shape
    parts, _, seg, _ = tok.shape
    half = images // 2
    item = lambda a: pl.BlockSpec((1,) + a.shape[1:], lambda i, *_: (i, 0, 0))
    whole = lambda a: pl.BlockSpec(a.shape, lambda i, *_: (0, 0))
    cols = 4 * width + SMALL

    def side(a, k):
        return pl.BlockSpec(
            (1,) + a.shape[1:], lambda i, *_: (jnp.clip(i - k * half, 0, half - 1), 0, 0)
        )

    halves = [*d0, *d1, *d2, *n2]
    return pl.pallas_call(
        attn_bwd_kernel,
        grid_spec=pltpu.PrefetchScalarGridSpec(
            num_scalar_prefetch=1,
            grid=(images,),
            in_specs=[side(a, k % 2) for k, a in enumerate(halves)]
            + [item(a) for a in (cot, res, ctx, qkv)]
            + [
                pl.BlockSpec((parts, 1, seg, width), lambda i, *_: (0, i, 0, 0)),
                pl.BlockSpec((parts, 1, seg, 128), lambda i, *_: (0, i, 0, 0)),
            ]
            + [whole(a) for a in (w, gains, wr)],
            out_specs=[
                *[pl.BlockSpec((1, seg, width), lambda i, *_: (i, 0, 0))] * 4,
                pl.BlockSpec((width, cols // 2), lambda i, *_: (0, 0)),
                pl.BlockSpec((width, cols // 2), lambda i, *_: (0, 0)),
            ],
            scratch_shapes=[
                pltpu.VMEM((width, 4 * width), F32),
                pltpu.VMEM((SMALL, width), F32),
                pltpu.VMEM(d0[0].shape[1:], F32),
                pltpu.VMEM((seq_len, width), BF),
                pltpu.VMEM((parts, seg, width), BF),
            ],
        ),
        out_shape=[
            *[jax.ShapeDtypeStruct((images, seg, width), BF)] * 4,
            jax.ShapeDtypeStruct((width, cols // 2), BF),
            jax.ShapeDtypeStruct((width, cols // 2), BF),
        ],
        compiler_params=pltpu.CompilerParams(vmem_limit_bytes=30 * MIB),
        cost_estimate=cost(17),
    )(own, *halves, cot, res, ctx, qkv, tok, code, w, gains, wr)


def result_kernel(own_ref, *refs):
    outs, res_ref, code_ref, out_refs, sums, parts = refs[:5], refs[5], refs[6], refs[7:11], *refs[11:]
    img = pl.program_id(0)
    half = pl.num_programs(0) // 2
    seq_len, width = res_ref.shape[1:]
    for side in range(2):

        @pl.when((img >= side * half) & (img < (side + 1) * half))
        def _():
            one, two = outs[1 + side], outs[3 + side]
            sums[...] = outs[0][0].astype(F32) + one[0].astype(F32) + two[0].astype(F32)

    code = code_ref[:, 0].reshape(seq_len, 128)[:, 0:1].astype(F32)
    keep = (code.astype(jnp.int32) & 1) > 0
    out = (res_ref[0] + jnp.where(keep, sums[...].T, 0.0)).astype(BF)
    parts[...] = out.reshape(parts.shape)
    for r, ref in enumerate(out_refs):
        ref[0] = parts[own_ref[0] ^ r]


def result(own, outs, o1, o2, res, code):
    images, seq_len, width = res.shape
    parts, _, seg, _ = code.shape
    half = images // 2

    def side(k):
        return pl.BlockSpec(
            (1, width, seq_len), lambda i: (jnp.clip(i - k * half, 0, half - 1), 0, 0)
        )

    return pl.pallas_call(
        result_kernel,
        grid=(images,),
        in_specs=[
            pl.BlockSpec(memory_space=pltpu.SMEM),
            pl.BlockSpec((1, width, seq_len), lambda i: (i, 0, 0)),
            side(0),
            side(1),
            side(0),
            side(1),
            pl.BlockSpec((1, seq_len, width), lambda i: (i, 0, 0)),
            pl.BlockSpec((parts, 1, seg, 128), lambda i: (0, i, 0, 0)),
        ],
        out_specs=[pl.BlockSpec((1, seg, width), lambda i: (i, 0, 0))] * 4,
        out_shape=[jax.ShapeDtypeStruct((images, seg, width), BF)] * 4,
        scratch_shapes=[
            pltpu.VMEM((width, seq_len), F32),
            pltpu.VMEM((parts, seg, width), BF),
        ],
        compiler_params=pltpu.CompilerParams(vmem_limit_bytes=12 * MIB),
        cost_estimate=cost(2),
    )(own, outs, *o1, *o2, res, code)


def gather_images_kernel(own_ref, p0, p1, p2, p3, out_ref):
    for r, piece in enumerate((p0, p1, p2, p3)):
        out_ref[own_ref[0] ^ r] = piece[...].astype(out_ref.dtype)


def gather_images(own, pieces, dtype):
    whole = pl.BlockSpec(memory_space=pltpu.VMEM)
    shape = pieces[0].shape
    out = pl.pallas_call(
        gather_images_kernel,
        in_specs=[pl.BlockSpec(memory_space=pltpu.SMEM)] + [whole] * 4,
        out_specs=whole,
        out_shape=jax.ShapeDtypeStruct((4,) + shape, dtype),
        compiler_params=pltpu.CompilerParams(vmem_limit_bytes=8 * MIB),
        cost_estimate=cost(1),
    )(own, *pieces)
    return out.reshape((4 * shape[0],) + shape[1:])


def finish_kernel(own_ref, mine_ref, other_ref, qkv_ref, proj_ref, small_ref):
    mid = mine_ref.shape[1]
    rest = qkv_ref.shape[1] - mid
    width = proj_ref.shape[1]
    for core, left, right in ((0, mine_ref, other_ref), (1, other_ref, mine_ref)):

        @pl.when((own_ref[0] & 1) == core)
        def _():
            qkv_ref[:, :mid] = left[...].astype(F32)
            qkv_ref[:, mid:] = right[:, :rest].astype(F32)
            proj_ref[...] = right[:, rest : rest + width].astype(F32)
            small_ref[...] = right[:, rest + width : rest + width + 128].astype(F32)


def finish(own, mine, other, width):
    rows = mine.shape[0]
    whole = pl.BlockSpec(memory_space=pltpu.VMEM)
    shape = lambda w: jax.ShapeDtypeStruct((rows, w), F32)
    return pl.pallas_call(
        finish_kernel,
        in_specs=[pl.BlockSpec(memory_space=pltpu.SMEM), whole, whole],
        out_specs=[whole] * 3,
        out_shape=[shape(3 * width), shape(width), shape(128)],
        compiler_params=pltpu.CompilerParams(vmem_limit_bytes=8 * MIB),
        cost_estimate=cost(1),
    )(own, mine, other)


def ring_gather(x, m, fw, bw, cut):
    ahead, behind = [], []
    a = b = x
    for _ in range(m // 2 - 1):
        a, b = send(a, "fsdp", fw), send(b, "fsdp", bw)
        ahead.append(a)
        behind.append(b)
    return ahead, behind, send(cut(a)[0], "fsdp", fw), send(cut(b)[1], "fsdp", bw)


def halves_gather(parts, m, fw, bw, last=lambda a: a):
    ahead, behind = [], []
    f, b = list(parts), list(parts)
    for _ in range(m // 2 - 1):
        first, second = send(f[0], "fsdp", fw), send(b[1], "fsdp", bw)
        f, b = [first, send(f[1], "fsdp", fw)], [send(b[0], "fsdp", bw), second]
        ahead.append(f)
        behind.append(b)
    return ahead, behind, send(last(f[0]), "fsdp", fw), send(last(b[1]), "fsdp", bw)


def halves_scatter(ahead, behind, far, fw, bw, wait=lambda a: a, seen=None):
    out = []
    for terms, pairs, whole in ((ahead, fw, 0), (behind, bw, 1)):
        got = [None, None]
        for half in (whole, 1 - whole):
            acc = far[half] if half == whole else None
            for term in reversed(terms):
                acc = term[half] if acc is None else add_low(term[half], wait(send(acc, "fsdp", pairs)))
                if seen is not None and half == whole:
                    seen.append(acc)
            got[half] = send(acc, "fsdp", pairs)
        out.append(got)
    return out


def ring_scatter(ahead, behind, top, bottom, fw, bw, put):
    a, b = send(top, "fsdp", fw), send(bottom, "fsdp", bw)
    for step, (to_fw, to_bw) in enumerate(zip(reversed(ahead), reversed(behind))):
        if step == 0:
            a, b = put(to_fw, a, 0), put(to_bw, b, 1)
        else:
            a, b = add_low(jnp.concatenate(to_fw), a), add_low(jnp.concatenate(to_bw), b)
        a, b = send(a, "fsdp", fw), send(b, "fsdp", bw)
    return a, b


def after(x, *done):
    return lax.optimization_barrier((x,) + done)[0]


def per_device(
    tokens, pad_mask, routes, ln1_gain, w_qkv, w_proj, ln2_gain, w_router, exp_in, exp_out, cotangent
):
    n = lax.axis_size("fsdp")
    per_device_images, seg, width = tokens.shape
    seq_idx = lax.axis_index("seq")
    own = seq_idx.astype(jnp.int32).reshape(1)
    idx = lax.axis_index("fsdp")
    m = n // 2
    fw8, bw8 = ring_pairs([ring_order(n)])
    low_ring = ring_order(m)
    fw4, bw4 = ring_pairs([low_ring, [m + i for i in low_ring]])
    pair = [(i, (i + m) % n) for i in range(n)]
    by_core = [(i, i ^ 1) for i in range(4)]
    by_half = [(i, i ^ 2) for i in range(4)]

    rows = w_qkv.shape[0]
    small = jnp.concatenate([ln1_gain[:, None], ln2_gain[:, None]], axis=1)
    small = jnp.pad(small, ((0, 0), (0, SMALL - 2))) + jnp.pad(
        w_router, ((0, 0), (8, SMALL - 12))
    )
    block = block_of(own, w_qkv, w_proj, small)
    mid = block.shape[1]

    fr = exp_in.shape[0]
    pick = lambda a: lax.dynamic_index_in_dim(a, seq_idx, 1, False)
    mine = jnp.stack([pick(exp_in), pick(exp_out)]).astype(BF)
    part = lambda k: mine[:, k * fr // 2 : (k + 1) * fr // 2]

    keep = pad_mask.astype(BF)[..., None]
    code = pad_mask + 2 * routes[..., 0] + 8 * routes[..., 1]
    code = jnp.pad(code.astype(BF)[..., None], ((0, 0), (0, 0), (0, 127)))
    fused = jnp.concatenate([tokens * keep, cotangent * keep, code], axis=2)
    images = per_device_images // 4
    half_img = images // 2
    fused = fused.reshape(4, images, seg, 2 * width + 128)
    by_seq = [[(i, i ^ r) for i in range(4)] for r in range(4)]
    pieces = [lax.dynamic_index_in_dim(fused, seq_idx ^ r, 0, False) for r in range(4)]
    swap = lambda parts: [parts[0]] + [send(parts[r], "seq", by_seq[r]) for r in (3, 2, 1)][::-1]
    tok, codes, cot = unpack(own, swap(pieces), width)

    base = jnp.where(idx < m, 0, m)
    spot = idx - base
    place = jnp.where(spot % 2 == 0, spot // 2, m - 1 - spot // 2)

    def member(p):
        p = p % m
        return jnp.where(p < m // 2, 2 * p, 2 * (m - 1 - p) + 1)

    chunk = jnp.stack([block, send(block, "fsdp", pair)])
    ahead, behind, top, bottom = ring_gather(
        chunk, m, fw4, bw4, lambda a: after((a[:1], a[1:]), tok)
    )
    q0 = send(after(mine, chunk), "fsdp", pair)

    pieces, offs = [chunk], [idx, (idx + m) % n]
    for d in range(1, m // 2):
        for got, i in ((ahead, member(place - d + m)), (behind, member(place + d))):
            pieces.append(got[d - 1])
            offs += [base + i, m - base + i]
    far_member = member(place + m // 2)
    pieces += [top, bottom]
    offs += [base + far_member, m - base + far_member]
    offs = jnp.stack(offs).astype(jnp.int32) * rows
    w_mine = gather_rows(pieces, offs, (n * rows, mid))
    w_other = send(w_mine, "seq", by_core)

    late_in, late_out = after((exp_in, exp_out), top, bottom)
    win = late_in.transpose(1, 0, 2).astype(BF)
    wout = late_out.transpose(1, 0, 2).astype(BF)
    *n2, res, qkv, ctx, w, gains, wr = attn_fwd(own, tok, codes, w_mine, w_other)
    g_ahead, g_behind, g_top, g_bottom = ring_gather(
        after(cot, top, bottom),
        m,
        fw4,
        bw4,
        lambda a: after((a[:half_img], a[half_img:]), *n2),
    )
    q2 = send(q0, "seq", by_half)
    quarters = [q0, send(q0, "seq", by_core), q2, send(q2, "seq", by_core)]

    win, wout, wint, woutt = weights(own, win, wout, quarters)
    units = images * m
    bufs, at = None, 0

    def experts(xs, gs):
        nonlocal at, bufs
        *dd, b0, b1, b2, b3 = moe_call(
            xs, gs, own, wr, win, wout, wint, at, units, bufs
        )
        bufs = [b0, b1, b2, b3]
        at += images
        return dd

    d_own = experts(n2, [(cot, 0), (cot, half_img)])
    x_ahead, x_behind, x_top, x_bottom = halves_gather(
        n2, m, fw4, bw4, lambda a: after(a, *d_own)
    )
    dx_ahead, dx_behind, where = [], [], []
    for d in range(m // 2 - 1):
        (xa, xb), (ga, gb) = (x_ahead[d], x_behind[d]), (g_ahead[d], g_behind[d])
        where.append(at)
        back0, on1 = experts([xa[0], xb[1]], [(ga, 0), (gb, half_img)])
        back1, on0 = experts([xa[1], xb[0]], [(ga, half_img), (gb, 0)])
        dx_ahead.append([on0, on1])
        dx_behind.append([back0, back1])
    far_at = at
    far = experts([x_top, x_bottom], [(g_top, 0), (g_bottom, 0)])
    ga, hg, xb, gb = bufs

    grad3 = moe_grad(ga, hg, xb, gb, 3)
    grad2 = moe_grad(after(ga, grad3), hg, xb, gb, 2)
    grad1 = moe_grad(after(ga, grad2), hg, xb, gb, 1)
    seen = []
    d1, d2 = halves_scatter(
        dx_ahead, dx_behind, far, fw4, bw4, lambda a: after(a, grad1), seen
    )
    kept2 = add_low(grad2, send(grad3, "seq", by_core))
    grad0 = moe_grad(after(ga, kept2, *seen), hg, xb, gb, 0)
    kept0 = add_low(grad0, send(grad1, "seq", by_core))
    outs = moe_out(woutt, after(ga, grad0))
    first_half = send(kept2[1], "seq", by_half)
    d_own = [after(d_own[0], grad0), d_own[1]]

    *gtok, dw_keep, dw_give = attn_bwd(
        own, d_own, d1, d2, n2, cot, res, ctx, qkv, tok, codes, w, gains, wr
    )

    outs = after(outs, *d1, *d2)
    out_at = lambda k: outs[k : k + half_img]
    o_ahead = [[out_at(k + 3 * half_img), out_at(k + half_img)] for k in where]
    o_behind = [[out_at(k), out_at(k + 2 * half_img)] for k in where]
    firsts = []

    def hold(a):
        firsts.append(a)
        return after(a, dw_keep)

    o1, o2 = halves_scatter(
        o_ahead, o_behind, (out_at(far_at), out_at(far_at + half_img)), fw4, bw4, hold
    )
    kept_pair = add_low(kept0[1], after(first_half, dw_keep))
    from_pair = send(kept_pair, "fsdp", pair)

    dw_give = after(dw_give, first_half, *firsts[: 2 if m == 4 else 0])
    dw = add_low(dw_keep, send(dw_give, "seq", by_core))

    def term(i):
        cut = lambda k: lax.dynamic_slice_in_dim(dw, k * rows, rows, 0)[None]
        return [cut(base + i), cut(m - base + i)]

    def put_part(t, part, side):
        t = list(t)
        t[side] = add_low(t[side], part)
        return jnp.concatenate(t)

    last = term(far_member)
    s1, s2 = ring_scatter(
        [term(member(place + d)) for d in range(1, m // 2)],
        [term(member(place - d + m)) for d in range(1, m // 2)],
        last[0],
        last[1],
        fw4,
        bw4,
        put_part,
    )
    low = lambda a: a.astype(F32)
    mine_t, pair_t = term(spot)
    for_pair = (low(pair_t) + low(s1[1:]) + low(s2[1:])).astype(BF)
    dense = (low(mine_t) + low(s1[:1]) + low(s2[:1]) + low(send(for_pair, "fsdp", pair)))[0].astype(BF)
    dense = add_low(dense, send(dense, "seq", by_half))
    g_qkv, g_proj, g_small = finish(own, dense, send(dense, "seq", by_core), width)

    grad_tokens = gather_images(own, swap(gtok), F32)
    block_out = gather_images(own, swap(result(own, outs, o1, o2, res, codes)), BF)

    from_half = after(send(kept2[0], "seq", by_half), dw_keep)
    quarter = add_low(add_low(kept0[0], from_half), from_pair)
    from_half = send(quarter, "seq", by_half)
    grad_in, grad_out = pack(
        own,
        [quarter, send(quarter, "seq", by_core), from_half, send(from_half, "seq", by_core)],
    )

    return (
        block_out,
        grad_tokens,
        g_small[:, 0],
        g_qkv,
        g_proj,
        g_small[:, 1],
        g_small[:, 8:12],
        grad_in,
        grad_out,
    )


def solution(mesh):
    row = P("fsdp", None)
    cube = P("fsdp", None, None)
    split = P("fsdp", "seq", None)
    return jax.shard_map(
        per_device,
        mesh=mesh,
        in_specs=(
            split,
            P("fsdp", "seq"),
            split,
            P("fsdp"),
            row,
            row,
            P("fsdp"),
            row,
            cube,
            cube,
            split,
        ),
        out_specs=(split, split, P("fsdp"), row, row, P("fsdp"), row, cube, cube),
        check_vma=False,
    )
```

```python
import jax
import jax.numpy as jnp
from jax import lax
from jax.experimental import pallas as pl
from jax.experimental.pallas import tpu as pltpu
from jax.sharding import PartitionSpec as P

BF = jnp.bfloat16
F32 = jnp.float32
HEADS = 8
HEAD = 64
EPS = 1e-06
SQRT_HALF = 0.7071067811865476
INV_ROOT_TWO_PI = 0.3989422804014327
SMALL = 256
CODE_ROWS = 16
NT = (((1,), (1,)), ((), ()))
TN = (((0,), (0,)), ((), ()))
MIB = 1 << 20
PACE = 0.0001


def cost(us):
    return pl.CostEstimate(
        flops=int(us * 1.15e9 * PACE) + 1, bytes_accessed=int(us * 1e5 * PACE) + 1, transcendentals=0
    )


def dot(a, b, dims=(((1,), (0,)), ((), ()))):
    return lax.dot_general(a, b, dims, preferred_element_type=F32)


def ring_order(n):
    return [2 * i for i in range(n // 2)] + [2 * i + 1 for i in reversed(range(n // 2))]


def ring_pairs(orders):
    fw = []
    for order in orders:
        n = len(order)
        fw += [(order[i], order[(i + 1) % n]) for i in range(n)]
    return fw, [(b, a) for a, b in fw]


def send(x, axis, pairs):
    return lax.ppermute(x, axis, pairs)


def add_low(a, b):
    return (a.astype(F32) + b.astype(F32)).astype(BF)


def norm(v):
    c = v - jnp.mean(v, axis=-1, keepdims=True)
    inv = lax.rsqrt(jnp.mean(c * c, axis=-1, keepdims=True) + EPS)
    return c * inv, inv


def norm_back(u, hat, inv):
    return inv * (
        u
        - jnp.mean(u, axis=-1, keepdims=True)
        - hat * jnp.mean(u * hat, axis=-1, keepdims=True)
    )


def block_kernel(own_ref, qkv_ref, proj_ref, small_ref, out_ref):
    mid = out_ref.shape[1]
    rest = qkv_ref.shape[1] - mid
    width = proj_ref.shape[1]

    @pl.when((own_ref[0] & 1) == 0)
    def _():
        out_ref[...] = qkv_ref[:, :mid].astype(BF)

    @pl.when((own_ref[0] & 1) == 1)
    def _():
        out_ref[:, :rest] = qkv_ref[:, mid:].astype(BF)
        out_ref[:, rest : rest + width] = proj_ref[...].astype(BF)
        out_ref[:, rest + width :] = small_ref[...].astype(BF)


def block_of(own, w_qkv, w_proj, small):
    rows = w_qkv.shape[0]
    mid = (w_qkv.shape[1] + w_proj.shape[1] + SMALL) // 2
    whole = pl.BlockSpec(memory_space=pltpu.VMEM)
    return pl.pallas_call(
        block_kernel,
        in_specs=[pl.BlockSpec(memory_space=pltpu.SMEM)] + [whole] * 3,
        out_specs=whole,
        out_shape=jax.ShapeDtypeStruct((rows, mid), BF),
        compiler_params=pltpu.CompilerParams(vmem_limit_bytes=8 * MIB),
        cost_estimate=cost(1),
    )(own, w_qkv, w_proj, small)


def unpack_kernel(own_ref, p0, p1, p2, p3, tok_ref, code_ref, cot_ref):
    own = own_ref[0]
    seg, width = tok_ref.shape[2:]
    for r, piece in enumerate((p0, p1, p2, p3)):
        at = own ^ r
        tok_ref[at, 0] = piece[0, :, :width]
        code_ref[at, 0] = piece[0, :, 2 * width :]
        cot_ref[0, pl.ds(pl.multiple_of(at * seg, seg), seg)] = piece[0, :, width : 2 * width]

    seq_len = 4 * seg
    code = code_ref[:, 0].astype(F32).reshape(seq_len, 128).T
    cot_ref[0, seq_len:, :seq_len] = code[:CODE_ROWS].astype(BF)
    cot_ref[0, seq_len:, seq_len:] = jnp.zeros((CODE_ROWS, width - seq_len), BF)


def unpack(own, pieces, width):
    images, seg, cols = pieces[0].shape
    rows = 4 * seg + CODE_ROWS
    piece = pl.BlockSpec((1, seg, cols), lambda i: (i, 0, 0))
    nat = lambda w: pl.BlockSpec((4, 1, seg, w), lambda i: (0, i, 0, 0))
    shape = lambda *d: jax.ShapeDtypeStruct(d, BF)
    return pl.pallas_call(
        unpack_kernel,
        grid=(images,),
        in_specs=[pl.BlockSpec(memory_space=pltpu.SMEM)] + [piece] * 4,
        out_specs=[nat(width), nat(128), pl.BlockSpec((1, rows, width), lambda i: (i, 0, 0))],
        out_shape=[
            shape(4, images, seg, width),
            shape(4, images, seg, 128),
            shape(images, rows, width),
        ],
        compiler_params=pltpu.CompilerParams(vmem_limit_bytes=8 * MIB),
        cost_estimate=cost(1.5),
    )(own, *pieces)


def gather_kernel(n_pieces, offs, *refs):
    pieces, out_ref, sems = refs[:n_pieces], refs[n_pieces], refs[n_pieces + 1]
    copies, k = [], 0
    for piece in pieces:
        for part in range(piece.shape[0]):
            rows = piece.shape[1]
            off = pl.multiple_of(offs[k], rows)
            copies.append(
                pltpu.make_async_copy(piece.at[part], out_ref.at[pl.ds(off, rows)], sems.at[k])
            )
            k += 1
    for copy in copies:
        copy.start()
    for copy in copies:
        copy.wait()


def gather_rows(pieces, offs, shape):
    n = len(pieces)
    anywhere = pl.BlockSpec(memory_space=pl.ANY)
    return pl.pallas_call(
        lambda *a: gather_kernel(n, *a),
        in_specs=[pl.BlockSpec(memory_space=pltpu.SMEM)] + [anywhere] * n,
        out_specs=pl.BlockSpec(memory_space=pltpu.VMEM),
        out_shape=jax.ShapeDtypeStruct(shape, BF),
        scratch_shapes=[pltpu.SemaphoreType.DMA((sum(p.shape[0] for p in pieces),))],
        compiler_params=pltpu.CompilerParams(vmem_limit_bytes=8 * MIB),
        cost_estimate=cost(2),
    )(offs, *pieces)


def attn_fwd_kernel(own_ref, tok_ref, code_ref, mine_ref, other_ref, *refs):
    n2a_ref, n2b_ref, res_ref, qkv_ref, ctx_ref, w_ref, gain_ref, wr_ref = refs
    img = pl.program_id(0)
    seq_len, width = res_ref.shape[1:]
    mid = mine_ref.shape[1]
    own = own_ref[0]

    @pl.when(img == 0)
    def _():
        for core, left, right in ((0, mine_ref, other_ref), (1, other_ref, mine_ref)):

            @pl.when((own & 1) == core)
            def _():
                w_ref[:, :mid] = left[...]
                w_ref[:, mid:] = right[...]

        small = w_ref[:, 4 * width : 4 * width + 128].astype(F32).T
        gain_ref[...] = small[0:16]
        for r in range(4):
            wr_ref[r : r + 1] = gain_ref[pl.ds(8 + (own ^ r), 1)]
        wr_ref[4:8] = jnp.zeros((4, width), F32)

    code = code_ref[:, 0].reshape(seq_len, 128).astype(F32)
    keep = (code[:, 0:1].astype(jnp.int32) & 1) > 0
    key_ok = (code.T[0:1].astype(jnp.int32) & 1) > 0
    x = tok_ref[:, 0].reshape(seq_len, width).astype(F32)
    hat, _ = norm(x)
    n1 = (hat * gain_ref[0:1]).astype(BF)
    qkv_ref[0] = dot(n1, w_ref[:, : 3 * width]).astype(BF)
    parts = []
    for h in range(HEADS):
        q = qkv_ref[0, :, h * HEAD : (h + 1) * HEAD]
        k = qkv_ref[0, :, width + h * HEAD : width + (h + 1) * HEAD]
        v = qkv_ref[0, :, 2 * width + h * HEAD : 2 * width + (h + 1) * HEAD]
        s = jnp.where(key_ok, dot(q, k, NT) * 0.125, -1e30)
        e = jnp.exp(s - jnp.max(s, axis=-1, keepdims=True))
        p = (e * (1.0 / jnp.sum(e, axis=-1, keepdims=True))).astype(BF)
        parts.append(dot(p, v))
    ctx = jnp.concatenate(parts, axis=1).astype(BF)
    ctx_ref[0] = ctx
    res = x + jnp.where(keep, dot(ctx, w_ref[:, 3 * width : 4 * width]), 0.0)
    res_ref[0] = res
    hat2, _ = norm(res)
    n2 = (hat2 * gain_ref[1:2]).astype(BF)
    half = pl.num_programs(0) // 2
    for k, ref in ((0, n2a_ref), (1, n2b_ref)):

        @pl.when((img >= k * half) & (img < (k + 1) * half))
        def _():
            ref[0] = n2


def attn_fwd(own, tok, code, mine, other):
    parts, images, seg, width = tok.shape
    seq_len, half = parts * seg, images // 2
    row = lambda w: pl.BlockSpec((1, seq_len, w), lambda i, *_: (i, 0, 0))
    whole = lambda s: pl.BlockSpec(s, lambda i, *_: (0,) * len(s))
    side = lambda k: pl.BlockSpec(
        (1, seq_len, width), lambda i, *_: (jnp.clip(i - k * half, 0, half - 1), 0, 0)
    )
    cols = 4 * width + SMALL
    return pl.pallas_call(
        attn_fwd_kernel,
        grid_spec=pltpu.PrefetchScalarGridSpec(
            num_scalar_prefetch=1,
            grid=(images,),
            in_specs=[
                pl.BlockSpec((parts, 1, seg, width), lambda i, *_: (0, i, 0, 0)),
                pl.BlockSpec((parts, 1, seg, 128), lambda i, *_: (0, i, 0, 0)),
                whole(mine.shape),
                whole(other.shape),
            ],
            out_specs=[
                side(0),
                side(1),
                row(width),
                row(3 * width),
                row(width),
                whole((width, cols)),
                whole((16, width)),
                whole((8, width)),
            ],
        ),
        out_shape=[
            jax.ShapeDtypeStruct((half, seq_len, width), BF),
            jax.ShapeDtypeStruct((half, seq_len, width), BF),
            jax.ShapeDtypeStruct((images, seq_len, width), F32),
            jax.ShapeDtypeStruct((images, seq_len, 3 * width), BF),
            jax.ShapeDtypeStruct((images, seq_len, width), BF),
            jax.ShapeDtypeStruct((width, cols), BF),
            jax.ShapeDtypeStruct((16, width), F32),
            jax.ShapeDtypeStruct((8, width), F32),
        ],
        compiler_params=pltpu.CompilerParams(vmem_limit_bytes=20 * MIB),
        cost_estimate=cost(8),
    )(own, tok, code, mine, other)


def router(own, n2, wr, code):
    ids = lax.broadcasted_iota(jnp.int32, (8, n2.shape[0]), 0)
    logits = jnp.where(ids < 4, dot(wr.astype(BF), n2, NT), -1e30)
    e = jnp.exp(logits - jnp.max(logits, axis=0, keepdims=True))
    probs = e * (1.0 / jnp.sum(e, axis=0, keepdims=True))
    route = code.astype(F32).astype(jnp.int32)
    first = (route >> 1) & 3
    second = route >> 3
    ids = ids ^ own
    chosen = ((ids == first) | (ids == second)).astype(F32)
    return probs, chosen


def weights_kernel(own_ref, *refs):
    win_ref, wout_ref = refs[:2]
    pieces = refs[2:-4]
    parts = len(pieces) // 4
    all_in, all_out, in_t, out_t = refs[-4:]
    own = own_ref[0]
    rows = win_ref.shape[1]
    for b in range(8):
        sl = slice(b * rows, (b + 1) * rows)
        if b < 4:
            a, c = win_ref[own ^ b], wout_ref[own ^ b]
        else:
            mine = pieces[(b - 4) * parts : (b - 3) * parts]
            a, c = (jnp.concatenate([p[k] for p in mine], axis=0) for k in range(2))
        all_in[sl] = a
        all_out[sl] = c
        in_t[:, sl] = a.T
        out_t[:, sl] = c.T


def weights(own, win, wout, pieces):
    rows, width = win.shape[1:]
    whole = pl.BlockSpec(memory_space=pltpu.VMEM)
    flat = jax.ShapeDtypeStruct((8 * rows, width), BF)
    turned = jax.ShapeDtypeStruct((width, 8 * rows), BF)
    return pl.pallas_call(
        weights_kernel,
        in_specs=[pl.BlockSpec(memory_space=pltpu.SMEM)] + [whole] * (2 + len(pieces)),
        out_specs=[whole] * 4,
        out_shape=[flat, flat, turned, turned],
        compiler_params=pltpu.CompilerParams(vmem_limit_bytes=16 * MIB),
        cost_estimate=cost(3),
    )(own, win, wout, *pieces)


def moe_kernel(starts, n_aliased, own_ref, wr_ref, win_ref, wout_ref, wint_ref, *refs):
    n = len(starts)
    xs, gs = refs[:n], refs[n : 2 * n]
    refs = refs[2 * n + n_aliased :]
    dx_refs = refs[:n]
    ga_ref, hg_ref, xo_ref, go_ref = refs[n:]
    step = pl.program_id(0)
    seq_len, width = xo_ref.shape[1:]
    rows = win_ref.shape[0] // 8
    within = []
    for j in range(n):
        low, high = starts[j], starts[j + 1] if j + 1 < n else None
        within.append((step >= low) if high is None else ((step >= low) & (step < high)))

        @pl.when(within[j])
        def _():
            xo_ref[0] = xs[j][0]
            go_ref[0] = gs[j][0]

    x = xo_ref[0]
    g = go_ref[0, :seq_len]
    probs, chosen = router(own_ref[0], x, wr_ref[...], go_ref[0, seq_len : seq_len + 1, :seq_len])
    gate = probs * chosen
    sums = [None] * 4
    for b in range(8):
        e = b % 4
        sl = slice(b * rows, (b + 1) * rows)
        h = dot(win_ref[sl], x, NT)
        u = dot(wout_ref[sl], g, NT)
        cumul = 0.5 * (1.0 + lax.erf(h * SQRT_HALF))
        slope = cumul + h * (INV_ROOT_TWO_PI * jnp.exp(-0.5 * h * h))
        act = h * cumul
        row = gate[e : e + 1]
        ga_ref[0, sl] = (act * row).astype(BF)
        hg_ref[0, sl] = (u * row * slope).astype(BF)
        part = jnp.sum(act * u, axis=0, keepdims=True)
        sums[e] = part if sums[e] is None else sums[e] + part
    dx = dot(wint_ref[...], hg_ref[0]).astype(BF)
    pad = jnp.zeros((CODE_ROWS - 4, seq_len), F32)
    tail = jnp.concatenate(sums + [pad], axis=0).astype(BF)
    for j in range(n):

        @pl.when(within[j])
        def _():
            dx_refs[j][0, :width] = dx
            dx_refs[j][0, width:] = tail


def moe_call(xs, gs, own, wr, win, wout, wint, first, units, bufs):
    n = len(xs)
    counts = [x.shape[0] for x in xs]
    starts = [sum(counts[:j]) for j in range(n)]
    total = sum(counts)
    seq_len, width = xs[0].shape[1:]
    f = win.shape[0]
    g_rows = gs[0][0].shape[1]

    def item(rows, j, at=0):
        lo, c = starts[j], counts[j]
        return pl.BlockSpec(
            (1, rows, width), lambda i: (at + jnp.clip(i - lo, 0, c - 1), 0, 0)
        )

    def out_item(j):
        lo, c = starts[j], counts[j]
        return pl.BlockSpec(
            (1, width + CODE_ROWS, seq_len), lambda i: (jnp.clip(i - lo, 0, c - 1), 0, 0)
        )

    whole = lambda s: pl.BlockSpec(s, lambda i: (0, 0), pipeline_mode=pl.Buffered(1))
    buf = lambda r, w: pl.BlockSpec((1, r, w), lambda i: (first + i, 0, 0))
    aliased = [] if bufs is None else list(bufs)
    base = 5 + 2 * n
    return pl.pallas_call(
        lambda *a: moe_kernel(starts, len(aliased), *a),
        grid=(total,),
        in_specs=[pl.BlockSpec(memory_space=pltpu.SMEM)]
        + [whole(wr.shape), whole(win.shape), whole(wout.shape), whole(wint.shape)]
        + [item(seq_len, j) for j in range(n)]
        + [item(g_rows, j, gs[j][1]) for j in range(n)]
        + [pl.BlockSpec(memory_space=pl.ANY)] * len(aliased),
        out_specs=[out_item(j) for j in range(n)]
        + [
            buf(f, seq_len),
            buf(f, seq_len),
            buf(seq_len, width),
            buf(g_rows, width),
        ],
        out_shape=[
            jax.ShapeDtypeStruct((c, width + CODE_ROWS, seq_len), BF) for c in counts
        ]
        + [
            jax.ShapeDtypeStruct((units, f, seq_len), BF),
            jax.ShapeDtypeStruct((units, f, seq_len), BF),
            jax.ShapeDtypeStruct((units, seq_len, width), BF),
            jax.ShapeDtypeStruct((units, g_rows, width), BF),
        ],
        input_output_aliases={base + k: n + k for k in range(len(aliased))},
        compiler_params=pltpu.CompilerParams(vmem_limit_bytes=16 * MIB),
        cost_estimate=cost(2.6 * total),
    )(own, wr, win, wout, wint, *xs, *[g for g, _ in gs], *aliased)


def moe_out_kernel(woutt_ref, ga_ref, out_ref):
    out_ref[0] = dot(woutt_ref[...], ga_ref[0]).astype(BF)


def moe_out(woutt, ga):
    units, f, seq_len = ga.shape
    width = woutt.shape[0]
    return pl.pallas_call(
        moe_out_kernel,
        grid=(units,),
        in_specs=[
            pl.BlockSpec((width, f), lambda i: (0, 0), pipeline_mode=pl.Buffered(1)),
            pl.BlockSpec((1, f, seq_len), lambda i: (i, 0, 0)),
        ],
        out_specs=pl.BlockSpec((1, width, seq_len), lambda i: (i, 0, 0)),
        out_shape=jax.ShapeDtypeStruct((units, width, seq_len), BF),
        compiler_params=pltpu.CompilerParams(vmem_limit_bytes=8 * MIB),
        cost_estimate=cost(0.7 * units),
    )(woutt, ga)


def moe_grad_kernel(groups, ga_ref, hg_ref, x_ref, g_ref, out_ref, acc_in, acc_out):
    seq_len = x_ref.shape[1]
    part = pl.program_id(1)
    a_in = a_out = None
    for u in range(x_ref.shape[0]):
        t_in = dot(hg_ref[u], x_ref[u])
        t_out = dot(ga_ref[u], g_ref[u, :seq_len])
        a_in = t_in if a_in is None else a_in + t_in
        a_out = t_out if a_out is None else a_out + t_out
    if groups == 1:
        out_ref[0, 0] = a_in.astype(BF)
        out_ref[0, 1] = a_out.astype(BF)
        return

    @pl.when(part == 0)
    def _():
        acc_in[...] = jnp.zeros_like(acc_in)
        acc_out[...] = jnp.zeros_like(acc_out)

    acc_in[...] += a_in
    acc_out[...] += a_out

    @pl.when(part == groups - 1)
    def _():
        out_ref[0, 0] = acc_in[...].astype(BF)
        out_ref[0, 1] = acc_out[...].astype(BF)


def moe_grad(ga, hg, xb, gb, r):
    units, f, seq_len = ga.shape
    width = xb.shape[2]
    rows = f // 8
    per = min(units, 8)
    groups = units // per
    act = pl.BlockSpec((per, rows, seq_len), lambda b, p: (p, 4 * b + r, 0))
    return pl.pallas_call(
        lambda *a: moe_grad_kernel(groups, *a),
        grid=(2, groups),
        in_specs=[
            act,
            act,
            pl.BlockSpec((per, seq_len, width), lambda b, p: (p, 0, 0)),
            pl.BlockSpec((per, gb.shape[1], width), lambda b, p: (p, 0, 0)),
        ],
        out_specs=pl.BlockSpec((1, 2, rows, width), lambda b, p: (b, 0, 0, 0)),
        out_shape=jax.ShapeDtypeStruct((2, 2, rows, width), BF),
        scratch_shapes=[pltpu.VMEM((rows, width), F32)] * 2,
        compiler_params=pltpu.CompilerParams(vmem_limit_bytes=18 * MIB),
        cost_estimate=cost(0.47 * units),
    )(ga, hg, xb, gb)


def pack_kernel(own_ref, *refs):
    pieces = refs[:4]
    in_ref, out_ref = refs[4:]
    own = own_ref[0]
    for k in range(4):

        @pl.when(own == k)
        def _():
            for e in range(4):
                in_ref[:, e, :] = pieces[k ^ e][0].astype(F32)
                out_ref[:, e, :] = pieces[k ^ e][1].astype(F32)


def pack(own, pieces):
    rows, width = pieces[0].shape[1:]
    tile = min(rows, 64)
    piece = pl.BlockSpec((2, tile, width), lambda i: (0, i, 0))
    out = pl.BlockSpec((tile, 4, width), lambda i: (i, 0, 0))
    shape = jax.ShapeDtypeStruct((rows, 4, width), F32)
    return pl.pallas_call(
        pack_kernel,
        grid=(rows // tile,),
        in_specs=[pl.BlockSpec(memory_space=pltpu.SMEM)] + [piece] * 4,
        out_specs=[out, out],
        out_shape=[shape, shape],
        compiler_params=pltpu.CompilerParams(vmem_limit_bytes=24 * MIB),
        cost_estimate=cost(3),
    )(own, *pieces)


def attn_bwd_kernel(
    own_ref,
    *refs,
):
    items, refs = refs[:8], refs[8:]
    (
    cot_blk,
    res_ref,
    ctx_ref,
    qkv_ref,
    tok_ref,
    code_ref,
    w_ref,
    gain_ref,
    wr_ref,
    *gtok_refs,
    keep_ref,
    give_ref,
    acc,
    rows_acc,
    sums,
    n2_ref,
    gtok_ref,
    ) = refs
    cot_ref = cot_blk.at[0]
    own = own_ref[0]
    img = pl.program_id(0)
    seq_len, width = n2_ref.shape

    @pl.when(img == 0)
    def _():
        acc[...] = jnp.zeros_like(acc)
        rows_acc[...] = jnp.zeros_like(rows_acc)

    half = pl.num_programs(0) // 2
    for side in range(2):

        @pl.when((img >= side * half) & (img < (side + 1) * half))
        def _():
            d0, d1, d2, n2 = (items[2 * t + side] for t in range(4))
            sums[...] = d0[0].astype(F32) + d1[0].astype(F32) + d2[0].astype(F32)
            n2_ref[...] = n2[0]

    code = code_ref[:, 0].reshape(seq_len, 128)[:, 0:1].astype(F32)
    keep = (code.astype(jnp.int32) & 1) > 0
    total = sums[...]
    n2 = n2_ref[...]
    probs, chosen = router(own, n2, wr_ref[...], cot_ref[seq_len : seq_len + 1, :seq_len])
    gate_grad = chosen * total[width : width + 8]
    logit_grad = probs * (gate_grad - jnp.sum(probs * gate_grad, axis=0, keepdims=True))
    high = logit_grad.astype(BF)
    low = (logit_grad - high.astype(F32)).astype(BF)
    rows_acc[16:24] += dot(high, n2) + dot(low, n2)
    wr = wr_ref[...].astype(BF)
    dn2 = (total[:width] + dot(wr, high, TN) + dot(wr, low, TN)).T
    hat2, inv2 = norm(res_ref[0])
    rows_acc[1:2] += jnp.sum(dn2 * hat2, axis=0, keepdims=True)
    res_grad = cot_ref[:seq_len].astype(F32) + norm_back(dn2 * gain_ref[1:2], hat2, inv2)
    pg = jnp.where(keep, res_grad, 0.0).astype(BF)
    acc[:, 3 * width :] += dot(ctx_ref[0], pg, TN)
    dctx = dot(pg, w_ref[:, 3 * width : 4 * width], NT).astype(BF)
    dqs, dks, dvs = [], [], []
    for h in range(HEADS):
        q = qkv_ref[0, :, h * HEAD : (h + 1) * HEAD]
        k = qkv_ref[0, :, width + h * HEAD : width + (h + 1) * HEAD]
        v = qkv_ref[0, :, 2 * width + h * HEAD : 2 * width + (h + 1) * HEAD]
        do = dctx[:, h * HEAD : (h + 1) * HEAD]
        s = jnp.where(keep, dot(k, q, NT) * 0.125, -1e30)
        e = jnp.exp(s - jnp.max(s, axis=0, keepdims=True))
        p = e * (1.0 / jnp.sum(e, axis=0, keepdims=True))
        dvs.append(dot(p.astype(BF), do))
        wg = dot(v, do, NT)
        sg = (p * (wg - jnp.sum(p * wg, axis=0, keepdims=True))).astype(BF)
        dqs.append(dot(sg, k, TN) * 0.125)
        dks.append(dot(sg, q) * 0.125)
    dqkv = jnp.concatenate(dqs + dks + dvs, axis=1).astype(BF)
    hat, inv = norm(tok_ref[:, 0].reshape(seq_len, width).astype(F32))
    n1 = (hat * gain_ref[0:1]).astype(BF)
    acc[:, : 3 * width] += dot(n1, dqkv, TN)
    dn1 = dot(dqkv, w_ref[:, : 3 * width], NT)
    rows_acc[0:1] += jnp.sum(dn1 * hat, axis=0, keepdims=True)
    gtok = res_grad + norm_back(dn1 * gain_ref[0:1], hat, inv)
    gtok = jnp.where(keep, gtok, 0.0).astype(BF)
    gtok_ref[...] = gtok.reshape(gtok_ref.shape)
    for r, ref in enumerate(gtok_refs):
        ref[0] = gtok_ref[own ^ r]

    @pl.when(img == pl.num_programs(0) - 1)
    def _():
        for r in range(4):
            rows_acc[pl.ds(8 + (own ^ r), 1)] = rows_acc[16 + r : 17 + r]
        tail = rows_acc[...].T.astype(BF)
        mid = keep_ref.shape[1]
        for core, left, right in ((0, keep_ref, give_ref), (1, give_ref, keep_ref)):

            @pl.when((own & 1) == core)
            def _():
                left[...] = acc[:, :mid].astype(BF)
                right[:, : 4 * width - mid] = acc[:, mid:].astype(BF)
                right[:, 4 * width - mid :] = tail


def attn_bwd(own, d0, d1, d2, n2, cot, res, ctx, qkv, tok, code, w, gains, wr):
    images, seq_len, width = res.shape
    parts, _, seg, _ = tok.shape
    half = images // 2
    item = lambda a: pl.BlockSpec((1,) + a.shape[1:], lambda i, *_: (i, 0, 0))
    whole = lambda a: pl.BlockSpec(a.shape, lambda i, *_: (0, 0))
    cols = 4 * width + SMALL

    def side(a, k):
        return pl.BlockSpec(
            (1,) + a.shape[1:], lambda i, *_: (jnp.clip(i - k * half, 0, half - 1), 0, 0)
        )

    halves = [*d0, *d1, *d2, *n2]
    return pl.pallas_call(
        attn_bwd_kernel,
        grid_spec=pltpu.PrefetchScalarGridSpec(
            num_scalar_prefetch=1,
            grid=(images,),
            in_specs=[side(a, k % 2) for k, a in enumerate(halves)]
            + [item(a) for a in (cot, res, ctx, qkv)]
            + [
                pl.BlockSpec((parts, 1, seg, width), lambda i, *_: (0, i, 0, 0)),
                pl.BlockSpec((parts, 1, seg, 128), lambda i, *_: (0, i, 0, 0)),
            ]
            + [whole(a) for a in (w, gains, wr)],
            out_specs=[
                *[pl.BlockSpec((1, seg, width), lambda i, *_: (i, 0, 0))] * 4,
                pl.BlockSpec((width, cols // 2), lambda i, *_: (0, 0)),
                pl.BlockSpec((width, cols // 2), lambda i, *_: (0, 0)),
            ],
            scratch_shapes=[
                pltpu.VMEM((width, 4 * width), F32),
                pltpu.VMEM((SMALL, width), F32),
                pltpu.VMEM(d0[0].shape[1:], F32),
                pltpu.VMEM((seq_len, width), BF),
                pltpu.VMEM((parts, seg, width), BF),
            ],
        ),
        out_shape=[
            *[jax.ShapeDtypeStruct((images, seg, width), BF)] * 4,
            jax.ShapeDtypeStruct((width, cols // 2), BF),
            jax.ShapeDtypeStruct((width, cols // 2), BF),
        ],
        compiler_params=pltpu.CompilerParams(vmem_limit_bytes=30 * MIB),
        cost_estimate=cost(17),
    )(own, *halves, cot, res, ctx, qkv, tok, code, w, gains, wr)


def result_kernel(own_ref, *refs):
    outs, res_ref, code_ref, out_refs, sums, parts = refs[:5], refs[5], refs[6], refs[7:11], *refs[11:]
    img = pl.program_id(0)
    half = pl.num_programs(0) // 2
    seq_len, width = res_ref.shape[1:]
    for side in range(2):

        @pl.when((img >= side * half) & (img < (side + 1) * half))
        def _():
            one, two = outs[1 + side], outs[3 + side]
            sums[...] = outs[0][0].astype(F32) + one[0].astype(F32) + two[0].astype(F32)

    code = code_ref[:, 0].reshape(seq_len, 128)[:, 0:1].astype(F32)
    keep = (code.astype(jnp.int32) & 1) > 0
    out = (res_ref[0] + jnp.where(keep, sums[...].T, 0.0)).astype(BF)
    parts[...] = out.reshape(parts.shape)
    for r, ref in enumerate(out_refs):
        ref[0] = parts[own_ref[0] ^ r]


def result(own, outs, o1, o2, res, code):
    images, seq_len, width = res.shape
    parts, _, seg, _ = code.shape
    half = images // 2

    def side(k):
        return pl.BlockSpec(
            (1, width, seq_len), lambda i: (jnp.clip(i - k * half, 0, half - 1), 0, 0)
        )

    return pl.pallas_call(
        result_kernel,
        grid=(images,),
        in_specs=[
            pl.BlockSpec(memory_space=pltpu.SMEM),
            pl.BlockSpec((1, width, seq_len), lambda i: (i, 0, 0)),
            side(0),
            side(1),
            side(0),
            side(1),
            pl.BlockSpec((1, seq_len, width), lambda i: (i, 0, 0)),
            pl.BlockSpec((parts, 1, seg, 128), lambda i: (0, i, 0, 0)),
        ],
        out_specs=[pl.BlockSpec((1, seg, width), lambda i: (i, 0, 0))] * 4,
        out_shape=[jax.ShapeDtypeStruct((images, seg, width), BF)] * 4,
        scratch_shapes=[
            pltpu.VMEM((width, seq_len), F32),
            pltpu.VMEM((parts, seg, width), BF),
        ],
        compiler_params=pltpu.CompilerParams(vmem_limit_bytes=12 * MIB),
        cost_estimate=cost(2),
    )(own, outs, *o1, *o2, res, code)


def gather_images_kernel(own_ref, p0, p1, p2, p3, out_ref):
    for r, piece in enumerate((p0, p1, p2, p3)):
        out_ref[own_ref[0] ^ r] = piece[...].astype(out_ref.dtype)


def gather_images(own, pieces, dtype):
    whole = pl.BlockSpec(memory_space=pltpu.VMEM)
    shape = pieces[0].shape
    out = pl.pallas_call(
        gather_images_kernel,
        in_specs=[pl.BlockSpec(memory_space=pltpu.SMEM)] + [whole] * 4,
        out_specs=whole,
        out_shape=jax.ShapeDtypeStruct((4,) + shape, dtype),
        compiler_params=pltpu.CompilerParams(vmem_limit_bytes=8 * MIB),
        cost_estimate=cost(1),
    )(own, *pieces)
    return out.reshape((4 * shape[0],) + shape[1:])


def finish_kernel(own_ref, mine_ref, other_ref, qkv_ref, proj_ref, small_ref):
    mid = mine_ref.shape[1]
    rest = qkv_ref.shape[1] - mid
    width = proj_ref.shape[1]
    for core, left, right in ((0, mine_ref, other_ref), (1, other_ref, mine_ref)):

        @pl.when((own_ref[0] & 1) == core)
        def _():
            qkv_ref[:, :mid] = left[...].astype(F32)
            qkv_ref[:, mid:] = right[:, :rest].astype(F32)
            proj_ref[...] = right[:, rest : rest + width].astype(F32)
            small_ref[...] = right[:, rest + width : rest + width + 128].astype(F32)


def finish(own, mine, other, width):
    rows = mine.shape[0]
    whole = pl.BlockSpec(memory_space=pltpu.VMEM)
    shape = lambda w: jax.ShapeDtypeStruct((rows, w), F32)
    return pl.pallas_call(
        finish_kernel,
        in_specs=[pl.BlockSpec(memory_space=pltpu.SMEM), whole, whole],
        out_specs=[whole] * 3,
        out_shape=[shape(3 * width), shape(width), shape(128)],
        compiler_params=pltpu.CompilerParams(vmem_limit_bytes=8 * MIB),
        cost_estimate=cost(1),
    )(own, mine, other)


def ring_gather(x, m, fw, bw, cut):
    ahead, behind = [], []
    a = b = x
    for _ in range(m // 2 - 1):
        a, b = send(a, "fsdp", fw), send(b, "fsdp", bw)
        ahead.append(a)
        behind.append(b)
    return ahead, behind, send(cut(a)[0], "fsdp", fw), send(cut(b)[1], "fsdp", bw)


def halves_gather(parts, m, fw, bw, last=lambda a: a):
    ahead, behind = [], []
    f, b = list(parts), list(parts)
    for _ in range(m // 2 - 1):
        first, second = send(f[0], "fsdp", fw), send(b[1], "fsdp", bw)
        f, b = [first, send(f[1], "fsdp", fw)], [send(b[0], "fsdp", bw), second]
        ahead.append(f)
        behind.append(b)
    return ahead, behind, send(last(f[0]), "fsdp", fw), send(last(b[1]), "fsdp", bw)


def halves_scatter(ahead, behind, far, fw, bw, wait=lambda a: a, seen=None):
    out = []
    for terms, pairs, whole in ((ahead, fw, 0), (behind, bw, 1)):
        got = [None, None]
        for half in (whole, 1 - whole):
            acc = far[half] if half == whole else None
            for term in reversed(terms):
                acc = term[half] if acc is None else add_low(term[half], wait(send(acc, "fsdp", pairs)))
                if seen is not None and half == whole:
                    seen.append(acc)
            got[half] = send(acc, "fsdp", pairs)
        out.append(got)
    return out


def ring_scatter(ahead, behind, top, bottom, fw, bw, put):
    a, b = send(top, "fsdp", fw), send(bottom, "fsdp", bw)
    for step, (to_fw, to_bw) in enumerate(zip(reversed(ahead), reversed(behind))):
        if step == 0:
            a, b = put(to_fw, a, 0), put(to_bw, b, 1)
        else:
            a, b = add_low(jnp.concatenate(to_fw), a), add_low(jnp.concatenate(to_bw), b)
        a, b = send(a, "fsdp", fw), send(b, "fsdp", bw)
    return a, b


def after(x, *done):
    return lax.optimization_barrier((x,) + done)[0]


def per_device(
    tokens, pad_mask, routes, ln1_gain, w_qkv, w_proj, ln2_gain, w_router, exp_in, exp_out, cotangent
):
    n = lax.axis_size("fsdp")
    per_device_images, seg, width = tokens.shape
    seq_idx = lax.axis_index("seq")
    own = seq_idx.astype(jnp.int32).reshape(1)
    idx = lax.axis_index("fsdp")
    m = n // 2
    fw8, bw8 = ring_pairs([ring_order(n)])
    low_ring = ring_order(m)
    fw4, bw4 = ring_pairs([low_ring, [m + i for i in low_ring]])
    pair = [(i, (i + m) % n) for i in range(n)]
    by_core = [(i, i ^ 1) for i in range(4)]
    by_half = [(i, i ^ 2) for i in range(4)]

    rows = w_qkv.shape[0]
    small = jnp.concatenate([ln1_gain[:, None], ln2_gain[:, None]], axis=1)
    small = jnp.pad(small, ((0, 0), (0, SMALL - 2))) + jnp.pad(
        w_router, ((0, 0), (8, SMALL - 12))
    )
    block = block_of(own, w_qkv, w_proj, small)
    mid = block.shape[1]

    fr = exp_in.shape[0]
    pick = lambda a: lax.dynamic_index_in_dim(a, seq_idx, 1, False)
    mine = jnp.stack([pick(exp_in), pick(exp_out)]).astype(BF)
    part = lambda k: mine[:, k * fr // 2 : (k + 1) * fr // 2]

    keep = pad_mask.astype(BF)[..., None]
    code = pad_mask + 2 * routes[..., 0] + 8 * routes[..., 1]
    code = jnp.pad(code.astype(BF)[..., None], ((0, 0), (0, 0), (0, 127)))
    fused = jnp.concatenate([tokens * keep, cotangent * keep, code], axis=2)
    images = per_device_images // 4
    half_img = images // 2
    fused = fused.reshape(4, images, seg, 2 * width + 128)
    by_seq = [[(i, i ^ r) for i in range(4)] for r in range(4)]
    pieces = [lax.dynamic_index_in_dim(fused, seq_idx ^ r, 0, False) for r in range(4)]
    swap = lambda parts: [parts[0]] + [send(parts[r], "seq", by_seq[r]) for r in (3, 2, 1)][::-1]
    tok, codes, cot = unpack(own, swap(pieces), width)

    base = jnp.where(idx < m, 0, m)
    spot = idx - base
    place = jnp.where(spot % 2 == 0, spot // 2, m - 1 - spot // 2)

    def member(p):
        p = p % m
        return jnp.where(p < m // 2, 2 * p, 2 * (m - 1 - p) + 1)

    chunk = jnp.stack([block, send(block, "fsdp", pair)])
    ahead, behind, top, bottom = ring_gather(
        chunk, m, fw4, bw4, lambda a: after((a[:1], a[1:]), tok)
    )
    q0 = send(after(mine, chunk), "fsdp", pair)

    pieces, offs = [chunk], [idx, (idx + m) % n]
    for d in range(1, m // 2):
        for got, i in ((ahead, member(place - d + m)), (behind, member(place + d))):
            pieces.append(got[d - 1])
            offs += [base + i, m - base + i]
    far_member = member(place + m // 2)
    pieces += [top, bottom]
    offs += [base + far_member, m - base + far_member]
    offs = jnp.stack(offs).astype(jnp.int32) * rows
    w_mine = gather_rows(pieces, offs, (n * rows, mid))
    w_other = send(w_mine, "seq", by_core)

    late_in, late_out = after((exp_in, exp_out), q0)
    win = late_in.transpose(1, 0, 2).astype(BF)
    wout = late_out.transpose(1, 0, 2).astype(BF)
    *n2, res, qkv, ctx, w, gains, wr = attn_fwd(own, tok, codes, w_mine, w_other)
    g_ahead, g_behind, g_top, g_bottom = ring_gather(
        after(cot, top, bottom),
        m,
        fw4,
        bw4,
        lambda a: after((a[:half_img], a[half_img:]), *n2),
    )
    q2 = send(q0, "seq", by_half)
    quarters = [q0, send(q0, "seq", by_core), q2, send(q2, "seq", by_core)]

    win, wout, wint, woutt = weights(own, win, wout, quarters)
    units = images * m
    bufs, at = None, 0

    def experts(xs, gs):
        nonlocal at, bufs
        *dd, b0, b1, b2, b3 = moe_call(
            xs, gs, own, wr, win, wout, wint, at, units, bufs
        )
        bufs = [b0, b1, b2, b3]
        at += images
        return dd

    d_own = experts(n2, [(cot, 0), (cot, half_img)])
    x_ahead, x_behind, x_top, x_bottom = halves_gather(
        n2, m, fw4, bw4, lambda a: after(a, *d_own)
    )
    dx_ahead, dx_behind, where = [], [], []
    for d in range(m // 2 - 1):
        (xa, xb), (ga, gb) = (x_ahead[d], x_behind[d]), (g_ahead[d], g_behind[d])
        where.append(at)
        back0, on1 = experts([xa[0], xb[1]], [(ga, 0), (gb, half_img)])
        back1, on0 = experts([xa[1], xb[0]], [(ga, half_img), (gb, 0)])
        dx_ahead.append([on0, on1])
        dx_behind.append([back0, back1])
    far_at = at
    far = experts([x_top, x_bottom], [(g_top, 0), (g_bottom, 0)])
    ga, hg, xb, gb = bufs

    grad3 = moe_grad(ga, hg, xb, gb, 3)
    grad2 = moe_grad(after(ga, grad3), hg, xb, gb, 2)
    grad1 = moe_grad(after(ga, grad2), hg, xb, gb, 1)
    seen = []
    d1, d2 = halves_scatter(
        dx_ahead, dx_behind, far, fw4, bw4, lambda a: after(a, grad1), seen
    )
    kept2 = add_low(grad2, send(grad3, "seq", by_core))
    grad0 = moe_grad(after(ga, kept2, *seen), hg, xb, gb, 0)
    kept0 = add_low(grad0, send(grad1, "seq", by_core))
    outs = moe_out(woutt, after(ga, grad0))
    first_half = send(kept2[1], "seq", by_half)
    d_own = [after(d_own[0], grad0), d_own[1]]

    *gtok, dw_keep, dw_give = attn_bwd(
        own, d_own, d1, d2, n2, cot, res, ctx, qkv, tok, codes, w, gains, wr
    )

    outs = after(outs, *d1, *d2)
    out_at = lambda k: outs[k : k + half_img]
    o_ahead = [[out_at(k + 3 * half_img), out_at(k + half_img)] for k in where]
    o_behind = [[out_at(k), out_at(k + 2 * half_img)] for k in where]
    firsts = []

    def hold(a):
        firsts.append(a)
        return after(a, dw_keep)

    o1, o2 = halves_scatter(
        o_ahead, o_behind, (out_at(far_at), out_at(far_at + half_img)), fw4, bw4, hold
    )
    kept_pair = add_low(kept0[1], after(first_half, dw_keep))
    from_pair = send(kept_pair, "fsdp", pair)

    dw_give = after(dw_give, first_half, *firsts[: 2 if m == 4 else 0])
    dw = add_low(dw_keep, send(dw_give, "seq", by_core))

    def term(i):
        cut = lambda k: lax.dynamic_slice_in_dim(dw, k * rows, rows, 0)[None]
        return [cut(base + i), cut(m - base + i)]

    def put_part(t, part, side):
        t = list(t)
        t[side] = add_low(t[side], part)
        return jnp.concatenate(t)

    last = term(far_member)
    s1, s2 = ring_scatter(
        [term(member(place + d)) for d in range(1, m // 2)],
        [term(member(place - d + m)) for d in range(1, m // 2)],
        last[0],
        last[1],
        fw4,
        bw4,
        put_part,
    )
    low = lambda a: a.astype(F32)
    mine_t, pair_t = term(spot)
    for_pair = (low(pair_t) + low(s1[1:]) + low(s2[1:])).astype(BF)
    dense = (low(mine_t) + low(s1[:1]) + low(s2[:1]) + low(send(for_pair, "fsdp", pair)))[0].astype(BF)
    dense = add_low(dense, send(dense, "seq", by_half))
    g_qkv, g_proj, g_small = finish(own, dense, send(dense, "seq", by_core), width)

    grad_tokens = gather_images(own, swap([after(g, s1) for g in gtok]), F32)
    block_out = gather_images(own, swap(result(own, outs, o1, o2, res, codes)), BF)

    from_half = after(send(kept2[0], "seq", by_half), dw_keep)
    quarter = add_low(add_low(kept0[0], from_half), from_pair)
    from_half = send(quarter, "seq", by_half)
    grad_in, grad_out = pack(
        own,
        [quarter, send(quarter, "seq", by_core), from_half, send(from_half, "seq", by_core)],
    )

    return (
        block_out,
        grad_tokens,
        g_small[:, 0],
        g_qkv,
        g_proj,
        g_small[:, 1],
        g_small[:, 8:12],
        grad_in,
        grad_out,
    )


def solution(mesh):
    row = P("fsdp", None)
    cube = P("fsdp", None, None)
    split = P("fsdp", "seq", None)
    return jax.shard_map(
        per_device,
        mesh=mesh,
        in_specs=(
            split,
            P("fsdp", "seq"),
            split,
            P("fsdp"),
            row,
            row,
            P("fsdp"),
            row,
            cube,
            cube,
            split,
        ),
        out_specs=(split, split, P("fsdp"), row, row, P("fsdp"), row, cube, cube),
        check_vma=False,
    )
```

```python
import jax
import jax.numpy as jnp
from jax import lax
from jax.experimental import pallas as pl
from jax.experimental.pallas import tpu as pltpu
from jax.sharding import PartitionSpec as P

BF = jnp.bfloat16
F32 = jnp.float32
HEADS = 8
HEAD = 64
EPS = 1e-06
SQRT_HALF = 0.7071067811865476
INV_ROOT_TWO_PI = 0.3989422804014327
SMALL = 256
CODE_ROWS = 16
NT = (((1,), (1,)), ((), ()))
TN = (((0,), (0,)), ((), ()))
MIB = 1 << 20
PACE = 0.0001


def cost(us):
    return pl.CostEstimate(
        flops=int(us * 1.15e9 * PACE) + 1, bytes_accessed=int(us * 1e5 * PACE) + 1, transcendentals=0
    )


def dot(a, b, dims=(((1,), (0,)), ((), ()))):
    return lax.dot_general(a, b, dims, preferred_element_type=F32)


def ring_order(n):
    return [2 * i for i in range(n // 2)] + [2 * i + 1 for i in reversed(range(n // 2))]


def ring_pairs(orders):
    fw = []
    for order in orders:
        n = len(order)
        fw += [(order[i], order[(i + 1) % n]) for i in range(n)]
    return fw, [(b, a) for a, b in fw]


def send(x, axis, pairs):
    return lax.ppermute(x, axis, pairs)


def add_low(a, b):
    return (a.astype(F32) + b.astype(F32)).astype(BF)


def norm(v):
    c = v - jnp.mean(v, axis=-1, keepdims=True)
    inv = lax.rsqrt(jnp.mean(c * c, axis=-1, keepdims=True) + EPS)
    return c * inv, inv


def norm_back(u, hat, inv):
    return inv * (
        u
        - jnp.mean(u, axis=-1, keepdims=True)
        - hat * jnp.mean(u * hat, axis=-1, keepdims=True)
    )


def block_kernel(own_ref, qkv_ref, proj_ref, small_ref, out_ref):
    mid = out_ref.shape[1]
    rest = qkv_ref.shape[1] - mid
    width = proj_ref.shape[1]

    @pl.when((own_ref[0] & 1) == 0)
    def _():
        out_ref[...] = qkv_ref[:, :mid].astype(BF)

    @pl.when((own_ref[0] & 1) == 1)
    def _():
        out_ref[:, :rest] = qkv_ref[:, mid:].astype(BF)
        out_ref[:, rest : rest + width] = proj_ref[...].astype(BF)
        out_ref[:, rest + width :] = small_ref[...].astype(BF)


def block_of(own, w_qkv, w_proj, small):
    rows = w_qkv.shape[0]
    mid = (w_qkv.shape[1] + w_proj.shape[1] + SMALL) // 2
    whole = pl.BlockSpec(memory_space=pltpu.VMEM)
    return pl.pallas_call(
        block_kernel,
        in_specs=[pl.BlockSpec(memory_space=pltpu.SMEM)] + [whole] * 3,
        out_specs=whole,
        out_shape=jax.ShapeDtypeStruct((rows, mid), BF),
        compiler_params=pltpu.CompilerParams(vmem_limit_bytes=8 * MIB),
        cost_estimate=cost(1),
    )(own, w_qkv, w_proj, small)


def unpack_kernel(own_ref, p0, p1, p2, p3, tok_ref, code_ref, cot_ref):
    own = own_ref[0]
    seg, width = tok_ref.shape[2:]
    for r, piece in enumerate((p0, p1, p2, p3)):
        at = own ^ r
        tok_ref[at, 0] = piece[0, :, :width]
        code_ref[at, 0] = piece[0, :, 2 * width :]
        cot_ref[0, pl.ds(pl.multiple_of(at * seg, seg), seg)] = piece[0, :, width : 2 * width]

    seq_len = 4 * seg
    code = code_ref[:, 0].astype(F32).reshape(seq_len, 128).T
    cot_ref[0, seq_len:, :seq_len] = code[:CODE_ROWS].astype(BF)
    cot_ref[0, seq_len:, seq_len:] = jnp.zeros((CODE_ROWS, width - seq_len), BF)


def unpack(own, pieces, width):
    images, seg, cols = pieces[0].shape
    rows = 4 * seg + CODE_ROWS
    piece = pl.BlockSpec((1, seg, cols), lambda i: (i, 0, 0))
    nat = lambda w: pl.BlockSpec((4, 1, seg, w), lambda i: (0, i, 0, 0))
    shape = lambda *d: jax.ShapeDtypeStruct(d, BF)
    return pl.pallas_call(
        unpack_kernel,
        grid=(images,),
        in_specs=[pl.BlockSpec(memory_space=pltpu.SMEM)] + [piece] * 4,
        out_specs=[nat(width), nat(128), pl.BlockSpec((1, rows, width), lambda i: (i, 0, 0))],
        out_shape=[
            shape(4, images, seg, width),
            shape(4, images, seg, 128),
            shape(images, rows, width),
        ],
        compiler_params=pltpu.CompilerParams(vmem_limit_bytes=8 * MIB),
        cost_estimate=cost(1.5),
    )(own, *pieces)


def gather_kernel(n_pieces, offs, *refs):
    pieces, out_ref, sems = refs[:n_pieces], refs[n_pieces], refs[n_pieces + 1]
    copies, k = [], 0
    for piece in pieces:
        for part in range(piece.shape[0]):
            rows = piece.shape[1]
            off = pl.multiple_of(offs[k], rows)
            copies.append(
                pltpu.make_async_copy(piece.at[part], out_ref.at[pl.ds(off, rows)], sems.at[k])
            )
            k += 1
    for copy in copies:
        copy.start()
    for copy in copies:
        copy.wait()


def gather_rows(pieces, offs, shape):
    n = len(pieces)
    anywhere = pl.BlockSpec(memory_space=pl.ANY)
    return pl.pallas_call(
        lambda *a: gather_kernel(n, *a),
        in_specs=[pl.BlockSpec(memory_space=pltpu.SMEM)] + [anywhere] * n,
        out_specs=pl.BlockSpec(memory_space=pltpu.VMEM),
        out_shape=jax.ShapeDtypeStruct(shape, BF),
        scratch_shapes=[pltpu.SemaphoreType.DMA((sum(p.shape[0] for p in pieces),))],
        compiler_params=pltpu.CompilerParams(vmem_limit_bytes=8 * MIB),
        cost_estimate=cost(2),
    )(offs, *pieces)


def attn_fwd_kernel(own_ref, tok_ref, code_ref, mine_ref, other_ref, *refs):
    n2a_ref, n2b_ref, res_ref, qkv_ref, ctx_ref, w_ref, gain_ref, wr_ref = refs
    img = pl.program_id(0)
    seq_len, width = res_ref.shape[1:]
    mid = mine_ref.shape[1]
    own = own_ref[0]

    @pl.when(img == 0)
    def _():
        for core, left, right in ((0, mine_ref, other_ref), (1, other_ref, mine_ref)):

            @pl.when((own & 1) == core)
            def _():
                w_ref[:, :mid] = left[...]
                w_ref[:, mid:] = right[...]

        small = w_ref[:, 4 * width : 4 * width + 128].astype(F32).T
        gain_ref[...] = small[0:16]
        for r in range(4):
            wr_ref[r : r + 1] = gain_ref[pl.ds(8 + (own ^ r), 1)]
        wr_ref[4:8] = jnp.zeros((4, width), F32)

    code = code_ref[:, 0].reshape(seq_len, 128).astype(F32)
    keep = (code[:, 0:1].astype(jnp.int32) & 1) > 0
    key_ok = (code.T[0:1].astype(jnp.int32) & 1) > 0
    x = tok_ref[:, 0].reshape(seq_len, width).astype(F32)
    hat, _ = norm(x)
    n1 = (hat * gain_ref[0:1]).astype(BF)
    qkv_ref[0] = dot(n1, w_ref[:, : 3 * width]).astype(BF)
    parts = []
    for h in range(HEADS):
        q = qkv_ref[0, :, h * HEAD : (h + 1) * HEAD]
        k = qkv_ref[0, :, width + h * HEAD : width + (h + 1) * HEAD]
        v = qkv_ref[0, :, 2 * width + h * HEAD : 2 * width + (h + 1) * HEAD]
        s = jnp.where(key_ok, dot(q, k, NT) * 0.125, -1e30)
        e = jnp.exp(s - jnp.max(s, axis=-1, keepdims=True))
        p = (e * (1.0 / jnp.sum(e, axis=-1, keepdims=True))).astype(BF)
        parts.append(dot(p, v))
    ctx = jnp.concatenate(parts, axis=1).astype(BF)
    ctx_ref[0] = ctx
    res = x + jnp.where(keep, dot(ctx, w_ref[:, 3 * width : 4 * width]), 0.0)
    res_ref[0] = res
    hat2, _ = norm(res)
    n2 = (hat2 * gain_ref[1:2]).astype(BF)
    half = pl.num_programs(0) // 2
    for k, ref in ((0, n2a_ref), (1, n2b_ref)):

        @pl.when((img >= k * half) & (img < (k + 1) * half))
        def _():
            ref[0] = n2


def attn_fwd(own, tok, code, mine, other):
    parts, images, seg, width = tok.shape
    seq_len, half = parts * seg, images // 2
    row = lambda w: pl.BlockSpec((1, seq_len, w), lambda i, *_: (i, 0, 0))
    whole = lambda s: pl.BlockSpec(s, lambda i, *_: (0,) * len(s))
    side = lambda k: pl.BlockSpec(
        (1, seq_len, width), lambda i, *_: (jnp.clip(i - k * half, 0, half - 1), 0, 0)
    )
    cols = 4 * width + SMALL
    return pl.pallas_call(
        attn_fwd_kernel,
        grid_spec=pltpu.PrefetchScalarGridSpec(
            num_scalar_prefetch=1,
            grid=(images,),
            in_specs=[
                pl.BlockSpec((parts, 1, seg, width), lambda i, *_: (0, i, 0, 0)),
                pl.BlockSpec((parts, 1, seg, 128), lambda i, *_: (0, i, 0, 0)),
                whole(mine.shape),
                whole(other.shape),
            ],
            out_specs=[
                side(0),
                side(1),
                row(width),
                row(3 * width),
                row(width),
                whole((width, cols)),
                whole((16, width)),
                whole((8, width)),
            ],
        ),
        out_shape=[
            jax.ShapeDtypeStruct((half, seq_len, width), BF),
            jax.ShapeDtypeStruct((half, seq_len, width), BF),
            jax.ShapeDtypeStruct((images, seq_len, width), F32),
            jax.ShapeDtypeStruct((images, seq_len, 3 * width), BF),
            jax.ShapeDtypeStruct((images, seq_len, width), BF),
            jax.ShapeDtypeStruct((width, cols), BF),
            jax.ShapeDtypeStruct((16, width), F32),
            jax.ShapeDtypeStruct((8, width), F32),
        ],
        compiler_params=pltpu.CompilerParams(vmem_limit_bytes=20 * MIB),
        cost_estimate=cost(8),
    )(own, tok, code, mine, other)


def router(own, n2, wr, code):
    ids = lax.broadcasted_iota(jnp.int32, (8, n2.shape[0]), 0)
    logits = jnp.where(ids < 4, dot(wr.astype(BF), n2, NT), -1e30)
    e = jnp.exp(logits - jnp.max(logits, axis=0, keepdims=True))
    probs = e * (1.0 / jnp.sum(e, axis=0, keepdims=True))
    route = code.astype(F32).astype(jnp.int32)
    first = (route >> 1) & 3
    second = route >> 3
    ids = ids ^ own
    chosen = ((ids == first) | (ids == second)).astype(F32)
    return probs, chosen


def weights_kernel(own_ref, *refs):
    win_ref, wout_ref = refs[:2]
    pieces = refs[2:-4]
    parts = len(pieces) // 4
    all_in, all_out, in_t, out_t = refs[-4:]
    own = own_ref[0]
    rows = win_ref.shape[1]
    for b in range(8):
        sl = slice(b * rows, (b + 1) * rows)
        if b < 4:
            a, c = win_ref[own ^ b], wout_ref[own ^ b]
        else:
            mine = pieces[(b - 4) * parts : (b - 3) * parts]
            a, c = (jnp.concatenate([p[k] for p in mine], axis=0) for k in range(2))
        all_in[sl] = a
        all_out[sl] = c
        in_t[:, sl] = a.T
        out_t[:, sl] = c.T


def weights(own, win, wout, pieces):
    rows, width = win.shape[1:]
    whole = pl.BlockSpec(memory_space=pltpu.VMEM)
    flat = jax.ShapeDtypeStruct((8 * rows, width), BF)
    turned = jax.ShapeDtypeStruct((width, 8 * rows), BF)
    return pl.pallas_call(
        weights_kernel,
        in_specs=[pl.BlockSpec(memory_space=pltpu.SMEM)] + [whole] * (2 + len(pieces)),
        out_specs=[whole] * 4,
        out_shape=[flat, flat, turned, turned],
        compiler_params=pltpu.CompilerParams(vmem_limit_bytes=16 * MIB),
        cost_estimate=cost(3),
    )(own, win, wout, *pieces)


def moe_kernel(starts, n_aliased, own_ref, wr_ref, win_ref, wout_ref, wint_ref, *refs):
    n = len(starts)
    xs, gs = refs[:n], refs[n : 2 * n]
    refs = refs[2 * n + n_aliased :]
    dx_refs = refs[:n]
    ga_ref, hg_ref, xo_ref, go_ref = refs[n:]
    step = pl.program_id(0)
    seq_len, width = xo_ref.shape[1:]
    rows = win_ref.shape[0] // 8
    within = []
    for j in range(n):
        low, high = starts[j], starts[j + 1] if j + 1 < n else None
        within.append((step >= low) if high is None else ((step >= low) & (step < high)))

        @pl.when(within[j])
        def _():
            xo_ref[0] = xs[j][0]
            go_ref[0] = gs[j][0]

    x = xo_ref[0]
    g = go_ref[0, :seq_len]
    probs, chosen = router(own_ref[0], x, wr_ref[...], go_ref[0, seq_len : seq_len + 1, :seq_len])
    gate = probs * chosen
    sums = [None] * 4
    for b in range(8):
        e = b % 4
        sl = slice(b * rows, (b + 1) * rows)
        h = dot(win_ref[sl], x, NT)
        u = dot(wout_ref[sl], g, NT)
        cumul = 0.5 * (1.0 + lax.erf(h * SQRT_HALF))
        slope = cumul + h * (INV_ROOT_TWO_PI * jnp.exp(-0.5 * h * h))
        act = h * cumul
        row = gate[e : e + 1]
        ga_ref[0, sl] = (act * row).astype(BF)
        hg_ref[0, sl] = (u * row * slope).astype(BF)
        part = jnp.sum(act * u, axis=0, keepdims=True)
        sums[e] = part if sums[e] is None else sums[e] + part
    dx = dot(wint_ref[...], hg_ref[0]).astype(BF)
    pad = jnp.zeros((CODE_ROWS - 4, seq_len), F32)
    tail = jnp.concatenate(sums + [pad], axis=0).astype(BF)
    for j in range(n):

        @pl.when(within[j])
        def _():
            dx_refs[j][0, :width] = dx
            dx_refs[j][0, width:] = tail


def moe_call(xs, gs, own, wr, win, wout, wint, first, units, bufs):
    n = len(xs)
    counts = [x.shape[0] for x in xs]
    starts = [sum(counts[:j]) for j in range(n)]
    total = sum(counts)
    seq_len, width = xs[0].shape[1:]
    f = win.shape[0]
    g_rows = gs[0][0].shape[1]

    def item(rows, j, at=0):
        lo, c = starts[j], counts[j]
        return pl.BlockSpec(
            (1, rows, width), lambda i: (at + jnp.clip(i - lo, 0, c - 1), 0, 0)
        )

    def out_item(j):
        lo, c = starts[j], counts[j]
        return pl.BlockSpec(
            (1, width + CODE_ROWS, seq_len), lambda i: (jnp.clip(i - lo, 0, c - 1), 0, 0)
        )

    whole = lambda s: pl.BlockSpec(s, lambda i: (0, 0), pipeline_mode=pl.Buffered(1))
    buf = lambda r, w: pl.BlockSpec((1, r, w), lambda i: (first + i, 0, 0))
    aliased = [] if bufs is None else list(bufs)
    base = 5 + 2 * n
    return pl.pallas_call(
        lambda *a: moe_kernel(starts, len(aliased), *a),
        grid=(total,),
        in_specs=[pl.BlockSpec(memory_space=pltpu.SMEM)]
        + [whole(wr.shape), whole(win.shape), whole(wout.shape), whole(wint.shape)]
        + [item(seq_len, j) for j in range(n)]
        + [item(g_rows, j, gs[j][1]) for j in range(n)]
        + [pl.BlockSpec(memory_space=pl.ANY)] * len(aliased),
        out_specs=[out_item(j) for j in range(n)]
        + [
            buf(f, seq_len),
            buf(f, seq_len),
            buf(seq_len, width),
            buf(g_rows, width),
        ],
        out_shape=[
            jax.ShapeDtypeStruct((c, width + CODE_ROWS, seq_len), BF) for c in counts
        ]
        + [
            jax.ShapeDtypeStruct((units, f, seq_len), BF),
            jax.ShapeDtypeStruct((units, f, seq_len), BF),
            jax.ShapeDtypeStruct((units, seq_len, width), BF),
            jax.ShapeDtypeStruct((units, g_rows, width), BF),
        ],
        input_output_aliases={base + k: n + k for k in range(len(aliased))},
        compiler_params=pltpu.CompilerParams(vmem_limit_bytes=16 * MIB),
        cost_estimate=cost(2.6 * total),
    )(own, wr, win, wout, wint, *xs, *[g for g, _ in gs], *aliased)


def moe_out_kernel(woutt_ref, ga_ref, out_ref):
    out_ref[0] = dot(woutt_ref[...], ga_ref[0]).astype(BF)


def moe_out(woutt, ga):
    units, f, seq_len = ga.shape
    width = woutt.shape[0]
    return pl.pallas_call(
        moe_out_kernel,
        grid=(units,),
        in_specs=[
            pl.BlockSpec((width, f), lambda i: (0, 0), pipeline_mode=pl.Buffered(1)),
            pl.BlockSpec((1, f, seq_len), lambda i: (i, 0, 0)),
        ],
        out_specs=pl.BlockSpec((1, width, seq_len), lambda i: (i, 0, 0)),
        out_shape=jax.ShapeDtypeStruct((units, width, seq_len), BF),
        compiler_params=pltpu.CompilerParams(vmem_limit_bytes=8 * MIB),
        cost_estimate=cost(0.7 * units),
    )(woutt, ga)


def moe_grad_kernel(groups, ga_ref, hg_ref, x_ref, g_ref, out_ref, acc_in, acc_out):
    seq_len = x_ref.shape[1]
    part = pl.program_id(1)
    a_in = a_out = None
    for u in range(x_ref.shape[0]):
        t_in = dot(hg_ref[u], x_ref[u])
        t_out = dot(ga_ref[u], g_ref[u, :seq_len])
        a_in = t_in if a_in is None else a_in + t_in
        a_out = t_out if a_out is None else a_out + t_out
    if groups == 1:
        out_ref[0, 0] = a_in.astype(BF)
        out_ref[0, 1] = a_out.astype(BF)
        return

    @pl.when(part == 0)
    def _():
        acc_in[...] = jnp.zeros_like(acc_in)
        acc_out[...] = jnp.zeros_like(acc_out)

    acc_in[...] += a_in
    acc_out[...] += a_out

    @pl.when(part == groups - 1)
    def _():
        out_ref[0, 0] = acc_in[...].astype(BF)
        out_ref[0, 1] = acc_out[...].astype(BF)


def moe_grad(ga, hg, xb, gb, r):
    units, f, seq_len = ga.shape
    width = xb.shape[2]
    rows = f // 8
    per = min(units, 8)
    groups = units // per
    act = pl.BlockSpec((per, rows, seq_len), lambda b, p: (p, 4 * b + r, 0))
    return pl.pallas_call(
        lambda *a: moe_grad_kernel(groups, *a),
        grid=(2, groups),
        in_specs=[
            act,
            act,
            pl.BlockSpec((per, seq_len, width), lambda b, p: (p, 0, 0)),
            pl.BlockSpec((per, gb.shape[1], width), lambda b, p: (p, 0, 0)),
        ],
        out_specs=pl.BlockSpec((1, 2, rows, width), lambda b, p: (b, 0, 0, 0)),
        out_shape=jax.ShapeDtypeStruct((2, 2, rows, width), BF),
        scratch_shapes=[pltpu.VMEM((rows, width), F32)] * 2,
        compiler_params=pltpu.CompilerParams(vmem_limit_bytes=15 * MIB),
        cost_estimate=cost(0.47 * units),
    )(ga, hg, xb, gb)


def pack_kernel(own_ref, *refs):
    pieces = refs[:4]
    in_ref, out_ref, held = refs[4:]
    for r in range(4):
        held[own_ref[0] ^ r] = pieces[r][...]
    for e in range(4):
        in_ref[:, e, :] = held[e, 0].astype(F32)
        out_ref[:, e, :] = held[e, 1].astype(F32)


def pack(own, pieces):
    rows, width = pieces[0].shape[1:]
    tile = min(rows, 64)
    piece = pl.BlockSpec((2, tile, width), lambda i: (0, i, 0))
    out = pl.BlockSpec((tile, 4, width), lambda i: (i, 0, 0))
    shape = jax.ShapeDtypeStruct((rows, 4, width), F32)
    return pl.pallas_call(
        pack_kernel,
        grid=(rows // tile,),
        in_specs=[pl.BlockSpec(memory_space=pltpu.SMEM)] + [piece] * 4,
        out_specs=[out, out],
        out_shape=[shape, shape],
        scratch_shapes=[pltpu.VMEM((4, 2, tile, width), BF)],
        compiler_params=pltpu.CompilerParams(vmem_limit_bytes=16 * MIB),
        cost_estimate=cost(3),
    )(own, *pieces)


def attn_bwd_kernel(
    own_ref,
    *refs,
):
    items, refs = refs[:8], refs[8:]
    (
    cot_blk,
    res_ref,
    ctx_ref,
    qkv_ref,
    tok_ref,
    code_ref,
    w_ref,
    gain_ref,
    wr_ref,
    *gtok_refs,
    keep_ref,
    give_ref,
    acc,
    rows_acc,
    sums,
    n2_ref,
    gtok_ref,
    ) = refs
    cot_ref = cot_blk.at[0]
    own = own_ref[0]
    img = pl.program_id(0)
    seq_len, width = n2_ref.shape

    @pl.when(img == 0)
    def _():
        acc[...] = jnp.zeros_like(acc)
        rows_acc[...] = jnp.zeros_like(rows_acc)

    half = pl.num_programs(0) // 2
    for side in range(2):

        @pl.when((img >= side * half) & (img < (side + 1) * half))
        def _():
            d0, d1, d2, n2 = (items[2 * t + side] for t in range(4))
            sums[...] = d0[0].astype(F32) + d1[0].astype(F32) + d2[0].astype(F32)
            n2_ref[...] = n2[0]

    code = code_ref[:, 0].reshape(seq_len, 128)[:, 0:1].astype(F32)
    keep = (code.astype(jnp.int32) & 1) > 0
    total = sums[...]
    n2 = n2_ref[...]
    probs, chosen = router(own, n2, wr_ref[...], cot_ref[seq_len : seq_len + 1, :seq_len])
    gate_grad = chosen * total[width : width + 8]
    logit_grad = probs * (gate_grad - jnp.sum(probs * gate_grad, axis=0, keepdims=True))
    high = logit_grad.astype(BF)
    low = (logit_grad - high.astype(F32)).astype(BF)
    rows_acc[16:24] += dot(high, n2) + dot(low, n2)
    wr = wr_ref[...].astype(BF)
    dn2 = (total[:width] + dot(wr, high, TN) + dot(wr, low, TN)).T
    hat2, inv2 = norm(res_ref[0])
    rows_acc[1:2] += jnp.sum(dn2 * hat2, axis=0, keepdims=True)
    res_grad = cot_ref[:seq_len].astype(F32) + norm_back(dn2 * gain_ref[1:2], hat2, inv2)
    pg = jnp.where(keep, res_grad, 0.0).astype(BF)
    acc[:, 3 * width :] += dot(ctx_ref[0], pg, TN)
    dctx = dot(pg, w_ref[:, 3 * width : 4 * width], NT).astype(BF)
    dqs, dks, dvs = [], [], []
    for h in range(HEADS):
        q = qkv_ref[0, :, h * HEAD : (h + 1) * HEAD]
        k = qkv_ref[0, :, width + h * HEAD : width + (h + 1) * HEAD]
        v = qkv_ref[0, :, 2 * width + h * HEAD : 2 * width + (h + 1) * HEAD]
        do = dctx[:, h * HEAD : (h + 1) * HEAD]
        s = jnp.where(keep, dot(k, q, NT) * 0.125, -1e30)
        e = jnp.exp(s - jnp.max(s, axis=0, keepdims=True))
        p = e * (1.0 / jnp.sum(e, axis=0, keepdims=True))
        dvs.append(dot(p.astype(BF), do))
        wg = dot(v, do, NT)
        sg = (p * (wg - jnp.sum(p * wg, axis=0, keepdims=True))).astype(BF)
        dqs.append(dot(sg, k, TN) * 0.125)
        dks.append(dot(sg, q) * 0.125)
    dqkv = jnp.concatenate(dqs + dks + dvs, axis=1).astype(BF)
    hat, inv = norm(tok_ref[:, 0].reshape(seq_len, width).astype(F32))
    n1 = (hat * gain_ref[0:1]).astype(BF)
    acc[:, : 3 * width] += dot(n1, dqkv, TN)
    dn1 = dot(dqkv, w_ref[:, : 3 * width], NT)
    rows_acc[0:1] += jnp.sum(dn1 * hat, axis=0, keepdims=True)
    gtok = res_grad + norm_back(dn1 * gain_ref[0:1], hat, inv)
    gtok = jnp.where(keep, gtok, 0.0).astype(BF)
    gtok_ref[...] = gtok.reshape(gtok_ref.shape)
    for r, ref in enumerate(gtok_refs):
        ref[0] = gtok_ref[own ^ r]

    @pl.when(img == pl.num_programs(0) - 1)
    def _():
        for r in range(4):
            rows_acc[pl.ds(8 + (own ^ r), 1)] = rows_acc[16 + r : 17 + r]
        tail = rows_acc[...].T.astype(BF)
        mid = keep_ref.shape[1]
        for core, left, right in ((0, keep_ref, give_ref), (1, give_ref, keep_ref)):

            @pl.when((own & 1) == core)
            def _():
                left[...] = acc[:, :mid].astype(BF)
                right[:, : 4 * width - mid] = acc[:, mid:].astype(BF)
                right[:, 4 * width - mid :] = tail


def attn_bwd(own, d0, d1, d2, n2, cot, res, ctx, qkv, tok, code, w, gains, wr):
    images, seq_len, width = res.shape
    parts, _, seg, _ = tok.shape
    half = images // 2
    item = lambda a: pl.BlockSpec((1,) + a.shape[1:], lambda i, *_: (i, 0, 0))
    whole = lambda a: pl.BlockSpec(a.shape, lambda i, *_: (0, 0))
    cols = 4 * width + SMALL

    def side(a, k):
        return pl.BlockSpec(
            (1,) + a.shape[1:], lambda i, *_: (jnp.clip(i - k * half, 0, half - 1), 0, 0)
        )

    halves = [*d0, *d1, *d2, *n2]
    return pl.pallas_call(
        attn_bwd_kernel,
        grid_spec=pltpu.PrefetchScalarGridSpec(
            num_scalar_prefetch=1,
            grid=(images,),
            in_specs=[side(a, k % 2) for k, a in enumerate(halves)]
            + [item(a) for a in (cot, res, ctx, qkv)]
            + [
                pl.BlockSpec((parts, 1, seg, width), lambda i, *_: (0, i, 0, 0)),
                pl.BlockSpec((parts, 1, seg, 128), lambda i, *_: (0, i, 0, 0)),
            ]
            + [whole(a) for a in (w, gains, wr)],
            out_specs=[
                *[pl.BlockSpec((1, seg, width), lambda i, *_: (i, 0, 0))] * 4,
                pl.BlockSpec((width, cols // 2), lambda i, *_: (0, 0)),
                pl.BlockSpec((width, cols // 2), lambda i, *_: (0, 0)),
            ],
            scratch_shapes=[
                pltpu.VMEM((width, 4 * width), F32),
                pltpu.VMEM((SMALL, width), F32),
                pltpu.VMEM(d0[0].shape[1:], F32),
                pltpu.VMEM((seq_len, width), BF),
                pltpu.VMEM((parts, seg, width), BF),
            ],
        ),
        out_shape=[
            *[jax.ShapeDtypeStruct((images, seg, width), BF)] * 4,
            jax.ShapeDtypeStruct((width, cols // 2), BF),
            jax.ShapeDtypeStruct((width, cols // 2), BF),
        ],
        compiler_params=pltpu.CompilerParams(vmem_limit_bytes=30 * MIB),
        cost_estimate=cost(17),
    )(own, *halves, cot, res, ctx, qkv, tok, code, w, gains, wr)


def result_kernel(own_ref, *refs):
    outs, res_ref, code_ref, out_refs, sums, parts = refs[:5], refs[5], refs[6], refs[7:11], *refs[11:]
    img = pl.program_id(0)
    half = pl.num_programs(0) // 2
    seq_len, width = res_ref.shape[1:]
    for side in range(2):

        @pl.when((img >= side * half) & (img < (side + 1) * half))
        def _():
            one, two = outs[1 + side], outs[3 + side]
            sums[...] = outs[0][0].astype(F32) + one[0].astype(F32) + two[0].astype(F32)

    code = code_ref[:, 0].reshape(seq_len, 128)[:, 0:1].astype(F32)
    keep = (code.astype(jnp.int32) & 1) > 0
    out = (res_ref[0] + jnp.where(keep, sums[...].T, 0.0)).astype(BF)
    parts[...] = out.reshape(parts.shape)
    for r, ref in enumerate(out_refs):
        ref[0] = parts[own_ref[0] ^ r]


def result(own, outs, o1, o2, res, code):
    images, seq_len, width = res.shape
    parts, _, seg, _ = code.shape
    half = images // 2

    def side(k):
        return pl.BlockSpec(
            (1, width, seq_len), lambda i: (jnp.clip(i - k * half, 0, half - 1), 0, 0)
        )

    return pl.pallas_call(
        result_kernel,
        grid=(images,),
        in_specs=[
            pl.BlockSpec(memory_space=pltpu.SMEM),
            pl.BlockSpec((1, width, seq_len), lambda i: (i, 0, 0)),
            side(0),
            side(1),
            side(0),
            side(1),
            pl.BlockSpec((1, seq_len, width), lambda i: (i, 0, 0)),
            pl.BlockSpec((parts, 1, seg, 128), lambda i: (0, i, 0, 0)),
        ],
        out_specs=[pl.BlockSpec((1, seg, width), lambda i: (i, 0, 0))] * 4,
        out_shape=[jax.ShapeDtypeStruct((images, seg, width), BF)] * 4,
        scratch_shapes=[
            pltpu.VMEM((width, seq_len), F32),
            pltpu.VMEM((parts, seg, width), BF),
        ],
        compiler_params=pltpu.CompilerParams(vmem_limit_bytes=12 * MIB),
        cost_estimate=cost(2),
    )(own, outs, *o1, *o2, res, code)


def gather_images_kernel(own_ref, p0, p1, p2, p3, out_ref):
    for r, piece in enumerate((p0, p1, p2, p3)):
        out_ref[own_ref[0] ^ r] = piece[...].astype(out_ref.dtype)


def gather_images(own, pieces, dtype):
    whole = pl.BlockSpec(memory_space=pltpu.VMEM)
    shape = pieces[0].shape
    out = pl.pallas_call(
        gather_images_kernel,
        in_specs=[pl.BlockSpec(memory_space=pltpu.SMEM)] + [whole] * 4,
        out_specs=whole,
        out_shape=jax.ShapeDtypeStruct((4,) + shape, dtype),
        compiler_params=pltpu.CompilerParams(vmem_limit_bytes=8 * MIB),
        cost_estimate=cost(1),
    )(own, *pieces)
    return out.reshape((4 * shape[0],) + shape[1:])


def finish_kernel(own_ref, mine_ref, other_ref, qkv_ref, proj_ref, small_ref):
    mid = mine_ref.shape[1]
    rest = qkv_ref.shape[1] - mid
    width = proj_ref.shape[1]
    for core, left, right in ((0, mine_ref, other_ref), (1, other_ref, mine_ref)):

        @pl.when((own_ref[0] & 1) == core)
        def _():
            qkv_ref[:, :mid] = left[...].astype(F32)
            qkv_ref[:, mid:] = right[:, :rest].astype(F32)
            proj_ref[...] = right[:, rest : rest + width].astype(F32)
            small_ref[...] = right[:, rest + width : rest + width + 128].astype(F32)


def finish(own, mine, other, width):
    rows = mine.shape[0]
    whole = pl.BlockSpec(memory_space=pltpu.VMEM)
    shape = lambda w: jax.ShapeDtypeStruct((rows, w), F32)
    return pl.pallas_call(
        finish_kernel,
        in_specs=[pl.BlockSpec(memory_space=pltpu.SMEM), whole, whole],
        out_specs=[whole] * 3,
        out_shape=[shape(3 * width), shape(width), shape(128)],
        compiler_params=pltpu.CompilerParams(vmem_limit_bytes=8 * MIB),
        cost_estimate=cost(1),
    )(own, mine, other)


def ring_gather(x, m, fw, bw, cut):
    ahead, behind = [], []
    a = b = x
    for _ in range(m // 2 - 1):
        a, b = send(a, "fsdp", fw), send(b, "fsdp", bw)
        ahead.append(a)
        behind.append(b)
    return ahead, behind, send(cut(a)[0], "fsdp", fw), send(cut(b)[1], "fsdp", bw)


def halves_gather(parts, m, fw, bw, last=lambda a: a):
    ahead, behind = [], []
    f, b = list(parts), list(parts)
    for _ in range(m // 2 - 1):
        first, second = send(f[0], "fsdp", fw), send(b[1], "fsdp", bw)
        f, b = [first, send(f[1], "fsdp", fw)], [send(b[0], "fsdp", bw), second]
        ahead.append(f)
        behind.append(b)
    return ahead, behind, send(last(f[0]), "fsdp", fw), send(last(b[1]), "fsdp", bw)


def halves_scatter(ahead, behind, far, fw, bw, wait=lambda a: a, seen=None):
    out = []
    for terms, pairs, whole in ((ahead, fw, 0), (behind, bw, 1)):
        got = [None, None]
        for half in (whole, 1 - whole):
            acc = far[half] if half == whole else None
            for term in reversed(terms):
                acc = term[half] if acc is None else add_low(term[half], wait(send(acc, "fsdp", pairs)))
                if seen is not None and half == whole:
                    seen.append(acc)
            got[half] = send(acc, "fsdp", pairs)
        out.append(got)
    return out


def ring_scatter(ahead, behind, top, bottom, fw, bw, put):
    a, b = send(top, "fsdp", fw), send(bottom, "fsdp", bw)
    for step, (to_fw, to_bw) in enumerate(zip(reversed(ahead), reversed(behind))):
        if step == 0:
            a, b = put(to_fw, a, 0), put(to_bw, b, 1)
        else:
            a, b = add_low(jnp.concatenate(to_fw), a), add_low(jnp.concatenate(to_bw), b)
        a, b = send(a, "fsdp", fw), send(b, "fsdp", bw)
    return a, b


def after(x, *done):
    return lax.optimization_barrier((x,) + done)[0]


def per_device(
    tokens, pad_mask, routes, ln1_gain, w_qkv, w_proj, ln2_gain, w_router, exp_in, exp_out, cotangent
):
    n = lax.axis_size("fsdp")
    per_device_images, seg, width = tokens.shape
    seq_idx = lax.axis_index("seq")
    own = seq_idx.astype(jnp.int32).reshape(1)
    idx = lax.axis_index("fsdp")
    m = n // 2
    fw8, bw8 = ring_pairs([ring_order(n)])
    low_ring = ring_order(m)
    fw4, bw4 = ring_pairs([low_ring, [m + i for i in low_ring]])
    pair = [(i, (i + m) % n) for i in range(n)]
    by_core = [(i, i ^ 1) for i in range(4)]
    by_half = [(i, i ^ 2) for i in range(4)]

    rows = w_qkv.shape[0]
    small = jnp.concatenate([ln1_gain[:, None], ln2_gain[:, None]], axis=1)
    small = jnp.pad(small, ((0, 0), (0, SMALL - 2))) + jnp.pad(
        w_router, ((0, 0), (8, SMALL - 12))
    )
    block = block_of(own, w_qkv, w_proj, small)
    mid = block.shape[1]

    fr = exp_in.shape[0]
    pick = lambda a: lax.dynamic_index_in_dim(a, seq_idx, 1, False)
    mine = jnp.stack([pick(exp_in), pick(exp_out)]).astype(BF)
    part = lambda k: mine[:, k * fr // 2 : (k + 1) * fr // 2]

    keep = pad_mask.astype(BF)[..., None]
    code = pad_mask + 2 * routes[..., 0] + 8 * routes[..., 1]
    code = jnp.pad(code.astype(BF)[..., None], ((0, 0), (0, 0), (0, 127)))
    fused = jnp.concatenate([tokens * keep, cotangent * keep, code], axis=2)
    images = per_device_images // 4
    half_img = images // 2
    fused = fused.reshape(4, images, seg, 2 * width + 128)
    by_seq = [[(i, i ^ r) for i in range(4)] for r in range(4)]
    pieces = [lax.dynamic_index_in_dim(fused, seq_idx ^ r, 0, False) for r in range(4)]
    swap = lambda parts: [parts[0]] + [send(parts[r], "seq", by_seq[r]) for r in (3, 2, 1)][::-1]
    tok, codes, cot = unpack(own, swap(pieces), width)

    base = jnp.where(idx < m, 0, m)
    spot = idx - base
    place = jnp.where(spot % 2 == 0, spot // 2, m - 1 - spot // 2)

    def member(p):
        p = p % m
        return jnp.where(p < m // 2, 2 * p, 2 * (m - 1 - p) + 1)

    chunk = jnp.stack([block, send(block, "fsdp", pair)])
    ahead, behind, top, bottom = ring_gather(
        chunk, m, fw4, bw4, lambda a: after((a[:1], a[1:]), tok)
    )
    q0 = send(after(mine, chunk), "fsdp", pair)

    pieces, offs = [chunk], [idx, (idx + m) % n]
    for d in range(1, m // 2):
        for got, i in ((ahead, member(place - d + m)), (behind, member(place + d))):
            pieces.append(got[d - 1])
            offs += [base + i, m - base + i]
    far_member = member(place + m // 2)
    pieces += [top, bottom]
    offs += [base + far_member, m - base + far_member]
    offs = jnp.stack(offs).astype(jnp.int32) * rows
    w_mine = gather_rows(pieces, offs, (n * rows, mid))
    w_other = send(w_mine, "seq", by_core)

    late_in, late_out = after((exp_in, exp_out), q0)
    win = late_in.transpose(1, 0, 2).astype(BF)
    wout = late_out.transpose(1, 0, 2).astype(BF)
    *n2, res, qkv, ctx, w, gains, wr = attn_fwd(own, tok, codes, w_mine, w_other)
    g_ahead, g_behind, g_top, g_bottom = ring_gather(
        after(cot, top, bottom),
        m,
        fw4,
        bw4,
        lambda a: after((a[:half_img], a[half_img:]), *n2),
    )
    q2 = send(q0, "seq", by_half)
    quarters = [q0, send(q0, "seq", by_core), q2, send(q2, "seq", by_core)]

    win, wout, wint, woutt = weights(own, win, wout, quarters)
    units = images * m
    bufs, at = None, 0

    def experts(xs, gs):
        nonlocal at, bufs
        *dd, b0, b1, b2, b3 = moe_call(
            xs, gs, own, wr, win, wout, wint, at, units, bufs
        )
        bufs = [b0, b1, b2, b3]
        at += images
        return dd

    d_own = experts(n2, [(cot, 0), (cot, half_img)])
    x_ahead, x_behind, x_top, x_bottom = halves_gather(
        n2, m, fw4, bw4, lambda a: after(a, *d_own)
    )
    dx_ahead, dx_behind, where = [], [], []
    for d in range(m // 2 - 1):
        (xa, xb), (ga, gb) = (x_ahead[d], x_behind[d]), (g_ahead[d], g_behind[d])
        where.append(at)
        back0, on1 = experts([xa[0], xb[1]], [(ga, 0), (gb, half_img)])
        back1, on0 = experts([xa[1], xb[0]], [(ga, half_img), (gb, 0)])
        dx_ahead.append([on0, on1])
        dx_behind.append([back0, back1])
    far_at = at
    far = experts([x_top, x_bottom], [(g_top, 0), (g_bottom, 0)])
    ga, hg, xb, gb = bufs

    grad3 = moe_grad(ga, hg, xb, gb, 3)
    grad2 = moe_grad(after(ga, grad3), hg, xb, gb, 2)
    grad1 = moe_grad(after(ga, grad2), hg, xb, gb, 1)
    seen = []
    d1, d2 = halves_scatter(
        dx_ahead, dx_behind, far, fw4, bw4, lambda a: after(a, grad1), seen
    )
    kept2 = add_low(grad2, send(grad3, "seq", by_core))
    grad0 = moe_grad(after(ga, kept2, *seen), hg, xb, gb, 0)
    kept0 = add_low(grad0, send(grad1, "seq", by_core))
    outs = moe_out(woutt, after(ga, grad0))
    first_half = send(kept2[1], "seq", by_half)
    d_own = [after(d_own[0], grad0), d_own[1]]

    *gtok, dw_keep, dw_give = attn_bwd(
        own, d_own, d1, d2, n2, cot, res, ctx, qkv, tok, codes, w, gains, wr
    )

    outs = after(outs, *d1, *d2)
    out_at = lambda k: outs[k : k + half_img]
    o_ahead = [[out_at(k + 3 * half_img), out_at(k + half_img)] for k in where]
    o_behind = [[out_at(k), out_at(k + 2 * half_img)] for k in where]
    firsts = []

    def hold(a):
        firsts.append(a)
        return after(a, dw_keep)

    o1, o2 = halves_scatter(
        o_ahead, o_behind, (out_at(far_at), out_at(far_at + half_img)), fw4, bw4, hold
    )
    kept_pair = add_low(kept0[1], after(first_half, dw_keep))
    from_pair = send(kept_pair, "fsdp", pair)

    dw_give = after(dw_give, first_half, *firsts[: 2 if m == 4 else 0])
    dw = add_low(dw_keep, send(dw_give, "seq", by_core))

    def term(i):
        cut = lambda k: lax.dynamic_slice_in_dim(dw, k * rows, rows, 0)[None]
        return [cut(base + i), cut(m - base + i)]

    def put_part(t, part, side):
        t = list(t)
        t[side] = add_low(t[side], part)
        return jnp.concatenate(t)

    last = term(far_member)
    s1, s2 = ring_scatter(
        [term(member(place + d)) for d in range(1, m // 2)],
        [term(member(place - d + m)) for d in range(1, m // 2)],
        last[0],
        last[1],
        fw4,
        bw4,
        put_part,
    )
    low = lambda a: a.astype(F32)
    mine_t, pair_t = term(spot)
    for_pair = (low(pair_t) + low(s1[1:]) + low(s2[1:])).astype(BF)
    dense = (low(mine_t) + low(s1[:1]) + low(s2[:1]) + low(send(for_pair, "fsdp", pair)))[0].astype(BF)
    dense = add_low(dense, send(dense, "seq", by_half))
    g_qkv, g_proj, g_small = finish(own, dense, send(dense, "seq", by_core), width)

    grad_tokens = gather_images(own, swap([after(g, s1) for g in gtok]), F32)
    block_out = gather_images(own, swap(result(own, outs, o1, o2, res, codes)), BF)

    from_half = after(send(kept2[0], "seq", by_half), dw_keep)
    quarter = add_low(add_low(kept0[0], from_half), from_pair)
    from_half = send(quarter, "seq", by_half)
    grad_in, grad_out = pack(
        own,
        [quarter, send(quarter, "seq", by_core), from_half, send(from_half, "seq", by_core)],
    )

    return (
        block_out,
        grad_tokens,
        g_small[:, 0],
        g_qkv,
        g_proj,
        g_small[:, 1],
        g_small[:, 8:12],
        grad_in,
        grad_out,
    )


def solution(mesh):
    row = P("fsdp", None)
    cube = P("fsdp", None, None)
    split = P("fsdp", "seq", None)
    return jax.shard_map(
        per_device,
        mesh=mesh,
        in_specs=(
            split,
            P("fsdp", "seq"),
            split,
            P("fsdp"),
            row,
            row,
            P("fsdp"),
            row,
            cube,
            cube,
            split,
        ),
        out_specs=(split, split, P("fsdp"), row, row, P("fsdp"), row, cube, cube),
        check_vma=False,
    )
```

```python
import jax
import jax.numpy as jnp
from jax import lax
from jax.experimental import pallas as pl
from jax.experimental.pallas import tpu as pltpu
from jax.sharding import PartitionSpec as P

BF = jnp.bfloat16
F32 = jnp.float32
HEADS = 8
HEAD = 64
EPS = 1e-06
SQRT_HALF = 0.7071067811865476
INV_ROOT_TWO_PI = 0.3989422804014327
SMALL = 256
CODE_ROWS = 16
NT = (((1,), (1,)), ((), ()))
TN = (((0,), (0,)), ((), ()))
MIB = 1 << 20
PACE = 0.0001


def cost(us):
    return pl.CostEstimate(
        flops=int(us * 1.15e9 * PACE) + 1, bytes_accessed=int(us * 1e5 * PACE) + 1, transcendentals=0
    )


def dot(a, b, dims=(((1,), (0,)), ((), ()))):
    return lax.dot_general(a, b, dims, preferred_element_type=F32)


def ring_order(n):
    return [2 * i for i in range(n // 2)] + [2 * i + 1 for i in reversed(range(n // 2))]


def ring_pairs(orders):
    fw = []
    for order in orders:
        n = len(order)
        fw += [(order[i], order[(i + 1) % n]) for i in range(n)]
    return fw, [(b, a) for a, b in fw]


def send(x, axis, pairs):
    return lax.ppermute(x, axis, pairs)


def add_low(a, b):
    return (a.astype(F32) + b.astype(F32)).astype(BF)


def norm(v):
    c = v - jnp.mean(v, axis=-1, keepdims=True)
    inv = lax.rsqrt(jnp.mean(c * c, axis=-1, keepdims=True) + EPS)
    return c * inv, inv


def norm_back(u, hat, inv):
    return inv * (
        u
        - jnp.mean(u, axis=-1, keepdims=True)
        - hat * jnp.mean(u * hat, axis=-1, keepdims=True)
    )


def block_kernel(own_ref, qkv_ref, proj_ref, small_ref, out_ref):
    mid = out_ref.shape[1]
    rest = qkv_ref.shape[1] - mid
    width = proj_ref.shape[1]

    @pl.when((own_ref[0] & 1) == 0)
    def _():
        out_ref[...] = qkv_ref[:, :mid].astype(BF)

    @pl.when((own_ref[0] & 1) == 1)
    def _():
        out_ref[:, :rest] = qkv_ref[:, mid:].astype(BF)
        out_ref[:, rest : rest + width] = proj_ref[...].astype(BF)
        out_ref[:, rest + width :] = small_ref[...].astype(BF)


def block_of(own, w_qkv, w_proj, small):
    rows = w_qkv.shape[0]
    mid = (w_qkv.shape[1] + w_proj.shape[1] + SMALL) // 2
    whole = pl.BlockSpec(memory_space=pltpu.VMEM)
    return pl.pallas_call(
        block_kernel,
        in_specs=[pl.BlockSpec(memory_space=pltpu.SMEM)] + [whole] * 3,
        out_specs=whole,
        out_shape=jax.ShapeDtypeStruct((rows, mid), BF),
        compiler_params=pltpu.CompilerParams(vmem_limit_bytes=8 * MIB),
        cost_estimate=cost(1),
    )(own, w_qkv, w_proj, small)


def unpack_kernel(own_ref, p0, p1, p2, p3, tok_ref, code_ref, cot_ref):
    own = own_ref[0]
    seg, width = tok_ref.shape[2:]
    for r, piece in enumerate((p0, p1, p2, p3)):
        at = own ^ r
        tok_ref[at, 0] = piece[0, :, :width]
        code_ref[at, 0] = piece[0, :, 2 * width :]
        cot_ref[0, pl.ds(pl.multiple_of(at * seg, seg), seg)] = piece[0, :, width : 2 * width]

    seq_len = 4 * seg
    code = code_ref[:, 0].astype(F32).reshape(seq_len, 128).T
    cot_ref[0, seq_len:, :seq_len] = code[:CODE_ROWS].astype(BF)
    cot_ref[0, seq_len:, seq_len:] = jnp.zeros((CODE_ROWS, width - seq_len), BF)


def unpack(own, pieces, width):
    images, seg, cols = pieces[0].shape
    rows = 4 * seg + CODE_ROWS
    piece = pl.BlockSpec((1, seg, cols), lambda i: (i, 0, 0))
    nat = lambda w: pl.BlockSpec((4, 1, seg, w), lambda i: (0, i, 0, 0))
    shape = lambda *d: jax.ShapeDtypeStruct(d, BF)
    return pl.pallas_call(
        unpack_kernel,
        grid=(images,),
        in_specs=[pl.BlockSpec(memory_space=pltpu.SMEM)] + [piece] * 4,
        out_specs=[nat(width), nat(128), pl.BlockSpec((1, rows, width), lambda i: (i, 0, 0))],
        out_shape=[
            shape(4, images, seg, width),
            shape(4, images, seg, 128),
            shape(images, rows, width),
        ],
        compiler_params=pltpu.CompilerParams(vmem_limit_bytes=8 * MIB),
        cost_estimate=cost(1.5),
    )(own, *pieces)


def gather_kernel(n_pieces, offs, *refs):
    pieces, out_ref, sems = refs[:n_pieces], refs[n_pieces], refs[n_pieces + 1]
    copies, k = [], 0
    for piece in pieces:
        for part in range(piece.shape[0]):
            rows = piece.shape[1]
            off = pl.multiple_of(offs[k], rows)
            copies.append(
                pltpu.make_async_copy(piece.at[part], out_ref.at[pl.ds(off, rows)], sems.at[k])
            )
            k += 1
    for copy in copies:
        copy.start()
    for copy in copies:
        copy.wait()


def gather_rows(pieces, offs, shape):
    n = len(pieces)
    anywhere = pl.BlockSpec(memory_space=pl.ANY)
    return pl.pallas_call(
        lambda *a: gather_kernel(n, *a),
        in_specs=[pl.BlockSpec(memory_space=pltpu.SMEM)] + [anywhere] * n,
        out_specs=pl.BlockSpec(memory_space=pltpu.VMEM),
        out_shape=jax.ShapeDtypeStruct(shape, BF),
        scratch_shapes=[pltpu.SemaphoreType.DMA((sum(p.shape[0] for p in pieces),))],
        compiler_params=pltpu.CompilerParams(vmem_limit_bytes=8 * MIB),
        cost_estimate=cost(2),
    )(offs, *pieces)


def attn_fwd_kernel(own_ref, tok_ref, code_ref, mine_ref, other_ref, *refs):
    n2a_ref, n2b_ref, res_ref, qkv_ref, ctx_ref, w_ref, gain_ref, wr_ref = refs
    img = pl.program_id(0)
    seq_len, width = res_ref.shape[1:]
    mid = mine_ref.shape[1]
    own = own_ref[0]

    @pl.when(img == 0)
    def _():
        for core, left, right in ((0, mine_ref, other_ref), (1, other_ref, mine_ref)):

            @pl.when((own & 1) == core)
            def _():
                w_ref[:, :mid] = left[...]
                w_ref[:, mid:] = right[...]

        small = w_ref[:, 4 * width : 4 * width + 128].astype(F32).T
        gain_ref[...] = small[0:16]
        for r in range(4):
            wr_ref[r : r + 1] = gain_ref[pl.ds(8 + (own ^ r), 1)]
        wr_ref[4:8] = jnp.zeros((4, width), F32)

    code = code_ref[:, 0].reshape(seq_len, 128).astype(F32)
    keep = (code[:, 0:1].astype(jnp.int32) & 1) > 0
    key_ok = (code.T[0:1].astype(jnp.int32) & 1) > 0
    x = tok_ref[:, 0].reshape(seq_len, width).astype(F32)
    hat, _ = norm(x)
    n1 = (hat * gain_ref[0:1]).astype(BF)
    qkv_ref[0] = dot(n1, w_ref[:, : 3 * width]).astype(BF)
    parts = []
    for h in range(HEADS):
        q = qkv_ref[0, :, h * HEAD : (h + 1) * HEAD]
        k = qkv_ref[0, :, width + h * HEAD : width + (h + 1) * HEAD]
        v = qkv_ref[0, :, 2 * width + h * HEAD : 2 * width + (h + 1) * HEAD]
        s = jnp.where(key_ok, dot(q, k, NT) * 0.125, -1e30)
        e = jnp.exp(s - jnp.max(s, axis=-1, keepdims=True))
        p = (e * (1.0 / jnp.sum(e, axis=-1, keepdims=True))).astype(BF)
        parts.append(dot(p, v))
    ctx = jnp.concatenate(parts, axis=1).astype(BF)
    ctx_ref[0] = ctx
    res = x + jnp.where(keep, dot(ctx, w_ref[:, 3 * width : 4 * width]), 0.0)
    res_ref[0] = res
    hat2, _ = norm(res)
    n2 = (hat2 * gain_ref[1:2]).astype(BF)
    half = pl.num_programs(0) // 2
    for k, ref in ((0, n2a_ref), (1, n2b_ref)):

        @pl.when((img >= k * half) & (img < (k + 1) * half))
        def _():
            ref[0] = n2


def attn_fwd(own, tok, code, mine, other):
    parts, images, seg, width = tok.shape
    seq_len, half = parts * seg, images // 2
    row = lambda w: pl.BlockSpec((1, seq_len, w), lambda i, *_: (i, 0, 0))
    whole = lambda s: pl.BlockSpec(s, lambda i, *_: (0,) * len(s))
    side = lambda k: pl.BlockSpec(
        (1, seq_len, width), lambda i, *_: (jnp.clip(i - k * half, 0, half - 1), 0, 0)
    )
    cols = 4 * width + SMALL
    return pl.pallas_call(
        attn_fwd_kernel,
        grid_spec=pltpu.PrefetchScalarGridSpec(
            num_scalar_prefetch=1,
            grid=(images,),
            in_specs=[
                pl.BlockSpec((parts, 1, seg, width), lambda i, *_: (0, i, 0, 0)),
                pl.BlockSpec((parts, 1, seg, 128), lambda i, *_: (0, i, 0, 0)),
                whole(mine.shape),
                whole(other.shape),
            ],
            out_specs=[
                side(0),
                side(1),
                row(width),
                row(3 * width),
                row(width),
                whole((width, cols)),
                whole((16, width)),
                whole((8, width)),
            ],
        ),
        out_shape=[
            jax.ShapeDtypeStruct((half, seq_len, width), BF),
            jax.ShapeDtypeStruct((half, seq_len, width), BF),
            jax.ShapeDtypeStruct((images, seq_len, width), F32),
            jax.ShapeDtypeStruct((images, seq_len, 3 * width), BF),
            jax.ShapeDtypeStruct((images, seq_len, width), BF),
            jax.ShapeDtypeStruct((width, cols), BF),
            jax.ShapeDtypeStruct((16, width), F32),
            jax.ShapeDtypeStruct((8, width), F32),
        ],
        compiler_params=pltpu.CompilerParams(vmem_limit_bytes=20 * MIB),
        cost_estimate=cost(8),
    )(own, tok, code, mine, other)


def router(own, n2, wr, code):
    ids = lax.broadcasted_iota(jnp.int32, (8, n2.shape[0]), 0)
    logits = jnp.where(ids < 4, dot(wr.astype(BF), n2, NT), -1e30)
    e = jnp.exp(logits - jnp.max(logits, axis=0, keepdims=True))
    probs = e * (1.0 / jnp.sum(e, axis=0, keepdims=True))
    route = code.astype(F32).astype(jnp.int32)
    first = (route >> 1) & 3
    second = route >> 3
    ids = ids ^ own
    chosen = ((ids == first) | (ids == second)).astype(F32)
    return probs, chosen


def weights_kernel(own_ref, *refs):
    win_ref, wout_ref = refs[:2]
    pieces = refs[2:-4]
    parts = len(pieces) // 4
    all_in, all_out, in_t, out_t = refs[-4:]
    own = own_ref[0]
    rows = win_ref.shape[1]
    for b in range(8):
        sl = slice(b * rows, (b + 1) * rows)
        if b < 4:
            a, c = win_ref[own ^ b], wout_ref[own ^ b]
        else:
            mine = pieces[(b - 4) * parts : (b - 3) * parts]
            a, c = (jnp.concatenate([p[k] for p in mine], axis=0) for k in range(2))
        all_in[sl] = a
        all_out[sl] = c
        in_t[:, sl] = a.T
        out_t[:, sl] = c.T


def weights(own, win, wout, pieces):
    rows, width = win.shape[1:]
    whole = pl.BlockSpec(memory_space=pltpu.VMEM)
    flat = jax.ShapeDtypeStruct((8 * rows, width), BF)
    turned = jax.ShapeDtypeStruct((width, 8 * rows), BF)
    return pl.pallas_call(
        weights_kernel,
        in_specs=[pl.BlockSpec(memory_space=pltpu.SMEM)] + [whole] * (2 + len(pieces)),
        out_specs=[whole] * 4,
        out_shape=[flat, flat, turned, turned],
        compiler_params=pltpu.CompilerParams(vmem_limit_bytes=16 * MIB),
        cost_estimate=cost(3),
    )(own, win, wout, *pieces)


def moe_kernel(starts, n_aliased, own_ref, wr_ref, win_ref, wout_ref, wint_ref, *refs):
    n = len(starts)
    xs, gs = refs[:n], refs[n : 2 * n]
    refs = refs[2 * n + n_aliased :]
    dx_refs = refs[:n]
    ga_ref, hg_ref, xo_ref, go_ref = refs[n:]
    step = pl.program_id(0)
    seq_len, width = xo_ref.shape[1:]
    rows = win_ref.shape[0] // 8
    within = []
    for j in range(n):
        low, high = starts[j], starts[j + 1] if j + 1 < n else None
        within.append((step >= low) if high is None else ((step >= low) & (step < high)))

        @pl.when(within[j])
        def _():
            xo_ref[0] = xs[j][0]
            go_ref[0] = gs[j][0]

    x = xo_ref[0]
    g = go_ref[0, :seq_len]
    probs, chosen = router(own_ref[0], x, wr_ref[...], go_ref[0, seq_len : seq_len + 1, :seq_len])
    gate = probs * chosen
    sums = [None] * 4
    for b in range(8):
        e = b % 4
        sl = slice(b * rows, (b + 1) * rows)
        h = dot(win_ref[sl], x, NT)
        u = dot(wout_ref[sl], g, NT)
        cumul = 0.5 * (1.0 + lax.erf(h * SQRT_HALF))
        slope = cumul + h * (INV_ROOT_TWO_PI * jnp.exp(-0.5 * h * h))
        act = h * cumul
        row = gate[e : e + 1]
        ga_ref[0, sl] = (act * row).astype(BF)
        hg_ref[0, sl] = (u * row * slope).astype(BF)
        part = jnp.sum(act * u, axis=0, keepdims=True)
        sums[e] = part if sums[e] is None else sums[e] + part
    dx = dot(wint_ref[...], hg_ref[0]).astype(BF)
    pad = jnp.zeros((CODE_ROWS - 4, seq_len), F32)
    tail = jnp.concatenate(sums + [pad], axis=0).astype(BF)
    for j in range(n):

        @pl.when(within[j])
        def _():
            dx_refs[j][0, :width] = dx
            dx_refs[j][0, width:] = tail


def moe_call(xs, gs, own, wr, win, wout, wint, first, units, bufs):
    n = len(xs)
    counts = [x.shape[0] for x in xs]
    starts = [sum(counts[:j]) for j in range(n)]
    total = sum(counts)
    seq_len, width = xs[0].shape[1:]
    f = win.shape[0]
    g_rows = gs[0][0].shape[1]

    def item(rows, j, at=0):
        lo, c = starts[j], counts[j]
        return pl.BlockSpec(
            (1, rows, width), lambda i: (at + jnp.clip(i - lo, 0, c - 1), 0, 0)
        )

    def out_item(j):
        lo, c = starts[j], counts[j]
        return pl.BlockSpec(
            (1, width + CODE_ROWS, seq_len), lambda i: (jnp.clip(i - lo, 0, c - 1), 0, 0)
        )

    whole = lambda s: pl.BlockSpec(s, lambda i: (0, 0), pipeline_mode=pl.Buffered(1))
    buf = lambda r, w: pl.BlockSpec((1, r, w), lambda i: (first + i, 0, 0))
    aliased = [] if bufs is None else list(bufs)
    base = 5 + 2 * n
    return pl.pallas_call(
        lambda *a: moe_kernel(starts, len(aliased), *a),
        grid=(total,),
        in_specs=[pl.BlockSpec(memory_space=pltpu.SMEM)]
        + [whole(wr.shape), whole(win.shape), whole(wout.shape), whole(wint.shape)]
        + [item(seq_len, j) for j in range(n)]
        + [item(g_rows, j, gs[j][1]) for j in range(n)]
        + [pl.BlockSpec(memory_space=pl.ANY)] * len(aliased),
        out_specs=[out_item(j) for j in range(n)]
        + [
            buf(f, seq_len),
            buf(f, seq_len),
            buf(seq_len, width),
            buf(g_rows, width),
        ],
        out_shape=[
            jax.ShapeDtypeStruct((c, width + CODE_ROWS, seq_len), BF) for c in counts
        ]
        + [
            jax.ShapeDtypeStruct((units, f, seq_len), BF),
            jax.ShapeDtypeStruct((units, f, seq_len), BF),
            jax.ShapeDtypeStruct((units, seq_len, width), BF),
            jax.ShapeDtypeStruct((units, g_rows, width), BF),
        ],
        input_output_aliases={base + k: n + k for k in range(len(aliased))},
        compiler_params=pltpu.CompilerParams(vmem_limit_bytes=16 * MIB),
        cost_estimate=cost(2.6 * total),
    )(own, wr, win, wout, wint, *xs, *[g for g, _ in gs], *aliased)


def moe_out_kernel(woutt_ref, ga_ref, out_ref):
    out_ref[0] = dot(woutt_ref[...], ga_ref[0]).astype(BF)


def moe_out(woutt, ga):
    units, f, seq_len = ga.shape
    width = woutt.shape[0]
    return pl.pallas_call(
        moe_out_kernel,
        grid=(units,),
        in_specs=[
            pl.BlockSpec((width, f), lambda i: (0, 0), pipeline_mode=pl.Buffered(1)),
            pl.BlockSpec((1, f, seq_len), lambda i: (i, 0, 0)),
        ],
        out_specs=pl.BlockSpec((1, width, seq_len), lambda i: (i, 0, 0)),
        out_shape=jax.ShapeDtypeStruct((units, width, seq_len), BF),
        compiler_params=pltpu.CompilerParams(vmem_limit_bytes=8 * MIB),
        cost_estimate=cost(0.7 * units),
    )(woutt, ga)


def moe_grad_kernel(groups, ga_ref, hg_ref, x_ref, g_ref, out_ref, acc_in, acc_out):
    seq_len = x_ref.shape[1]
    part = pl.program_id(1)
    a_in = a_out = None
    for u in range(x_ref.shape[0]):
        t_in = dot(hg_ref[u], x_ref[u])
        t_out = dot(ga_ref[u], g_ref[u, :seq_len])
        a_in = t_in if a_in is None else a_in + t_in
        a_out = t_out if a_out is None else a_out + t_out
    if groups == 1:
        out_ref[0, 0] = a_in.astype(BF)
        out_ref[0, 1] = a_out.astype(BF)
        return

    @pl.when(part == 0)
    def _():
        acc_in[...] = jnp.zeros_like(acc_in)
        acc_out[...] = jnp.zeros_like(acc_out)

    acc_in[...] += a_in
    acc_out[...] += a_out

    @pl.when(part == groups - 1)
    def _():
        out_ref[0, 0] = acc_in[...].astype(BF)
        out_ref[0, 1] = acc_out[...].astype(BF)


def moe_grad(ga, hg, xb, gb, r):
    units, f, seq_len = ga.shape
    width = xb.shape[2]
    rows = f // 8
    per = min(units, 8)
    groups = units // per
    act = pl.BlockSpec((per, rows, seq_len), lambda b, p: (p, 4 * b + r, 0))
    return pl.pallas_call(
        lambda *a: moe_grad_kernel(groups, *a),
        grid=(2, groups),
        in_specs=[
            act,
            act,
            pl.BlockSpec((per, seq_len, width), lambda b, p: (p, 0, 0)),
            pl.BlockSpec((per, gb.shape[1], width), lambda b, p: (p, 0, 0)),
        ],
        out_specs=pl.BlockSpec((1, 2, rows, width), lambda b, p: (b, 0, 0, 0)),
        out_shape=jax.ShapeDtypeStruct((2, 2, rows, width), BF),
        scratch_shapes=[pltpu.VMEM((rows, width), F32)] * 2,
        compiler_params=pltpu.CompilerParams(vmem_limit_bytes=15 * MIB),
        cost_estimate=cost(0.47 * units),
    )(ga, hg, xb, gb)


def pack_kernel(own_ref, *refs):
    pieces = refs[:4]
    in_ref, out_ref, held = refs[4:]
    for r in range(4):
        held[own_ref[0] ^ r] = pieces[r][...]
    for e in range(4):
        in_ref[:, e, :] = held[e, 0].astype(F32)
        out_ref[:, e, :] = held[e, 1].astype(F32)


def pack(own, pieces):
    rows, width = pieces[0].shape[1:]
    tile = min(rows, 64)
    piece = pl.BlockSpec((2, tile, width), lambda i: (0, i, 0))
    out = pl.BlockSpec((tile, 4, width), lambda i: (i, 0, 0))
    shape = jax.ShapeDtypeStruct((rows, 4, width), F32)
    return pl.pallas_call(
        pack_kernel,
        grid=(rows // tile,),
        in_specs=[pl.BlockSpec(memory_space=pltpu.SMEM)] + [piece] * 4,
        out_specs=[out, out],
        out_shape=[shape, shape],
        scratch_shapes=[pltpu.VMEM((4, 2, tile, width), BF)],
        compiler_params=pltpu.CompilerParams(vmem_limit_bytes=16 * MIB),
        cost_estimate=cost(3),
    )(own, *pieces)


def attn_bwd_kernel(
    own_ref,
    *refs,
):
    items, refs = refs[:8], refs[8:]
    (
    cot_blk,
    res_ref,
    ctx_ref,
    qkv_ref,
    tok_ref,
    code_ref,
    w_ref,
    gain_ref,
    wr_ref,
    *gtok_refs,
    keep_ref,
    give_ref,
    acc,
    rows_acc,
    sums,
    n2_ref,
    gtok_ref,
    ) = refs
    cot_ref = cot_blk.at[0]
    own = own_ref[0]
    img = pl.program_id(0)
    seq_len, width = n2_ref.shape

    @pl.when(img == 0)
    def _():
        acc[...] = jnp.zeros_like(acc)
        rows_acc[...] = jnp.zeros_like(rows_acc)

    half = pl.num_programs(0) // 2
    for side in range(2):

        @pl.when((img >= side * half) & (img < (side + 1) * half))
        def _():
            d0, d1, d2, n2 = (items[2 * t + side] for t in range(4))
            sums[...] = d0[0].astype(F32) + d1[0].astype(F32) + d2[0].astype(F32)
            n2_ref[...] = n2[0]

    code = code_ref[:, 0].reshape(seq_len, 128)[:, 0:1].astype(F32)
    keep = (code.astype(jnp.int32) & 1) > 0
    total = sums[...]
    n2 = n2_ref[...]
    probs, chosen = router(own, n2, wr_ref[...], cot_ref[seq_len : seq_len + 1, :seq_len])
    gate_grad = chosen * total[width : width + 8]
    logit_grad = probs * (gate_grad - jnp.sum(probs * gate_grad, axis=0, keepdims=True))
    high = logit_grad.astype(BF)
    low = (logit_grad - high.astype(F32)).astype(BF)
    rows_acc[16:24] += dot(high, n2) + dot(low, n2)
    wr = wr_ref[...].astype(BF)
    dn2 = (total[:width] + dot(wr, high, TN) + dot(wr, low, TN)).T
    hat2, inv2 = norm(res_ref[0])
    rows_acc[1:2] += jnp.sum(dn2 * hat2, axis=0, keepdims=True)
    res_grad = cot_ref[:seq_len].astype(F32) + norm_back(dn2 * gain_ref[1:2], hat2, inv2)
    pg = jnp.where(keep, res_grad, 0.0).astype(BF)
    acc[:, 3 * width :] += dot(ctx_ref[0], pg, TN)
    dctx = dot(pg, w_ref[:, 3 * width : 4 * width], NT).astype(BF)
    dqs, dks, dvs = [], [], []
    for h in range(HEADS):
        q = qkv_ref[0, :, h * HEAD : (h + 1) * HEAD]
        k = qkv_ref[0, :, width + h * HEAD : width + (h + 1) * HEAD]
        v = qkv_ref[0, :, 2 * width + h * HEAD : 2 * width + (h + 1) * HEAD]
        do = dctx[:, h * HEAD : (h + 1) * HEAD]
        s = jnp.where(keep, dot(k, q, NT) * 0.125, -1e30)
        e = jnp.exp(s - jnp.max(s, axis=0, keepdims=True))
        p = e * (1.0 / jnp.sum(e, axis=0, keepdims=True))
        dvs.append(dot(p.astype(BF), do))
        wg = dot(v, do, NT)
        sg = (p * (wg - jnp.sum(p * wg, axis=0, keepdims=True))).astype(BF)
        dqs.append(dot(sg, k, TN) * 0.125)
        dks.append(dot(sg, q) * 0.125)
    dqkv = jnp.concatenate(dqs + dks + dvs, axis=1).astype(BF)
    hat, inv = norm(tok_ref[:, 0].reshape(seq_len, width).astype(F32))
    n1 = (hat * gain_ref[0:1]).astype(BF)
    acc[:, : 3 * width] += dot(n1, dqkv, TN)
    dn1 = dot(dqkv, w_ref[:, : 3 * width], NT)
    rows_acc[0:1] += jnp.sum(dn1 * hat, axis=0, keepdims=True)
    gtok = res_grad + norm_back(dn1 * gain_ref[0:1], hat, inv)
    gtok = jnp.where(keep, gtok, 0.0).astype(BF)
    gtok_ref[...] = gtok.reshape(gtok_ref.shape)
    for r, ref in enumerate(gtok_refs):
        ref[0] = gtok_ref[own ^ r]

    @pl.when(img == pl.num_programs(0) - 1)
    def _():
        for r in range(4):
            rows_acc[pl.ds(8 + (own ^ r), 1)] = rows_acc[16 + r : 17 + r]
        tail = rows_acc[...].T.astype(BF)
        mid = keep_ref.shape[1]
        for core, left, right in ((0, keep_ref, give_ref), (1, give_ref, keep_ref)):

            @pl.when((own & 1) == core)
            def _():
                left[...] = acc[:, :mid].astype(BF)
                right[:, : 4 * width - mid] = acc[:, mid:].astype(BF)
                right[:, 4 * width - mid :] = tail


def attn_bwd(own, d0, d1, d2, n2, cot, res, ctx, qkv, tok, code, w, gains, wr):
    images, seq_len, width = res.shape
    parts, _, seg, _ = tok.shape
    half = images // 2
    item = lambda a: pl.BlockSpec((1,) + a.shape[1:], lambda i, *_: (i, 0, 0))
    whole = lambda a: pl.BlockSpec(a.shape, lambda i, *_: (0, 0))
    cols = 4 * width + SMALL

    def side(a, k):
        return pl.BlockSpec(
            (1,) + a.shape[1:], lambda i, *_: (jnp.clip(i - k * half, 0, half - 1), 0, 0)
        )

    halves = [*d0, *d1, *d2, *n2]
    return pl.pallas_call(
        attn_bwd_kernel,
        grid_spec=pltpu.PrefetchScalarGridSpec(
            num_scalar_prefetch=1,
            grid=(images,),
            in_specs=[side(a, k % 2) for k, a in enumerate(halves)]
            + [item(a) for a in (cot, res, ctx, qkv)]
            + [
                pl.BlockSpec((parts, 1, seg, width), lambda i, *_: (0, i, 0, 0)),
                pl.BlockSpec((parts, 1, seg, 128), lambda i, *_: (0, i, 0, 0)),
            ]
            + [whole(a) for a in (w, gains, wr)],
            out_specs=[
                *[pl.BlockSpec((1, seg, width), lambda i, *_: (i, 0, 0))] * 4,
                pl.BlockSpec((width, cols // 2), lambda i, *_: (0, 0)),
                pl.BlockSpec((width, cols // 2), lambda i, *_: (0, 0)),
            ],
            scratch_shapes=[
                pltpu.VMEM((width, 4 * width), F32),
                pltpu.VMEM((SMALL, width), F32),
                pltpu.VMEM(d0[0].shape[1:], F32),
                pltpu.VMEM((seq_len, width), BF),
                pltpu.VMEM((parts, seg, width), BF),
            ],
        ),
        out_shape=[
            *[jax.ShapeDtypeStruct((images, seg, width), BF)] * 4,
            jax.ShapeDtypeStruct((width, cols // 2), BF),
            jax.ShapeDtypeStruct((width, cols // 2), BF),
        ],
        compiler_params=pltpu.CompilerParams(vmem_limit_bytes=30 * MIB),
        cost_estimate=cost(17),
    )(own, *halves, cot, res, ctx, qkv, tok, code, w, gains, wr)


def result_kernel(own_ref, *refs):
    outs, res_ref, code_ref, out_refs, sums, parts = refs[:5], refs[5], refs[6], refs[7:11], *refs[11:]
    img = pl.program_id(0)
    half = pl.num_programs(0) // 2
    seq_len, width = res_ref.shape[1:]
    for side in range(2):

        @pl.when((img >= side * half) & (img < (side + 1) * half))
        def _():
            one, two = outs[1 + side], outs[3 + side]
            sums[...] = outs[0][0].astype(F32) + one[0].astype(F32) + two[0].astype(F32)

    code = code_ref[:, 0].reshape(seq_len, 128)[:, 0:1].astype(F32)
    keep = (code.astype(jnp.int32) & 1) > 0
    out = (res_ref[0] + jnp.where(keep, sums[...].T, 0.0)).astype(BF)
    parts[...] = out.reshape(parts.shape)
    for r, ref in enumerate(out_refs):
        ref[0] = parts[own_ref[0] ^ r]


def result(own, outs, o1, o2, res, code):
    images, seq_len, width = res.shape
    parts, _, seg, _ = code.shape
    half = images // 2

    def side(k):
        return pl.BlockSpec(
            (1, width, seq_len), lambda i: (jnp.clip(i - k * half, 0, half - 1), 0, 0)
        )

    return pl.pallas_call(
        result_kernel,
        grid=(images,),
        in_specs=[
            pl.BlockSpec(memory_space=pltpu.SMEM),
            pl.BlockSpec((1, width, seq_len), lambda i: (i, 0, 0)),
            side(0),
            side(1),
            side(0),
            side(1),
            pl.BlockSpec((1, seq_len, width), lambda i: (i, 0, 0)),
            pl.BlockSpec((parts, 1, seg, 128), lambda i: (0, i, 0, 0)),
        ],
        out_specs=[pl.BlockSpec((1, seg, width), lambda i: (i, 0, 0))] * 4,
        out_shape=[jax.ShapeDtypeStruct((images, seg, width), BF)] * 4,
        scratch_shapes=[
            pltpu.VMEM((width, seq_len), F32),
            pltpu.VMEM((parts, seg, width), BF),
        ],
        compiler_params=pltpu.CompilerParams(vmem_limit_bytes=12 * MIB),
        cost_estimate=cost(2),
    )(own, outs, *o1, *o2, res, code)


def gather_images_kernel(own_ref, p0, p1, p2, p3, out_ref):
    for r, piece in enumerate((p0, p1, p2, p3)):
        out_ref[own_ref[0] ^ r] = piece[...].astype(out_ref.dtype)


def gather_images(own, pieces, dtype):
    whole = pl.BlockSpec(memory_space=pltpu.VMEM)
    shape = pieces[0].shape
    out = pl.pallas_call(
        gather_images_kernel,
        in_specs=[pl.BlockSpec(memory_space=pltpu.SMEM)] + [whole] * 4,
        out_specs=whole,
        out_shape=jax.ShapeDtypeStruct((4,) + shape, dtype),
        compiler_params=pltpu.CompilerParams(vmem_limit_bytes=8 * MIB),
        cost_estimate=cost(1),
    )(own, *pieces)
    return out.reshape((4 * shape[0],) + shape[1:])


def finish_kernel(own_ref, mine_ref, other_ref, qkv_ref, proj_ref, small_ref):
    mid = mine_ref.shape[1]
    rest = qkv_ref.shape[1] - mid
    width = proj_ref.shape[1]
    for core, left, right in ((0, mine_ref, other_ref), (1, other_ref, mine_ref)):

        @pl.when((own_ref[0] & 1) == core)
        def _():
            qkv_ref[:, :mid] = left[...].astype(F32)
            qkv_ref[:, mid:] = right[:, :rest].astype(F32)
            proj_ref[...] = right[:, rest : rest + width].astype(F32)
            small_ref[...] = right[:, rest + width : rest + width + 128].astype(F32)


def finish(own, mine, other, width):
    rows = mine.shape[0]
    whole = pl.BlockSpec(memory_space=pltpu.VMEM)
    shape = lambda w: jax.ShapeDtypeStruct((rows, w), F32)
    return pl.pallas_call(
        finish_kernel,
        in_specs=[pl.BlockSpec(memory_space=pltpu.SMEM), whole, whole],
        out_specs=[whole] * 3,
        out_shape=[shape(3 * width), shape(width), shape(128)],
        compiler_params=pltpu.CompilerParams(vmem_limit_bytes=8 * MIB),
        cost_estimate=cost(1),
    )(own, mine, other)


def ring_gather(x, m, fw, bw, cut):
    ahead, behind = [], []
    a = b = x
    for _ in range(m // 2 - 1):
        a, b = send(a, "fsdp", fw), send(b, "fsdp", bw)
        ahead.append(a)
        behind.append(b)
    return ahead, behind, send(cut(a)[0], "fsdp", fw), send(cut(b)[1], "fsdp", bw)


def halves_gather(parts, m, fw, bw, last=lambda a: a):
    ahead, behind = [], []
    f, b = list(parts), list(parts)
    for _ in range(m // 2 - 1):
        first, second = send(f[0], "fsdp", fw), send(b[1], "fsdp", bw)
        f, b = [first, send(f[1], "fsdp", fw)], [send(b[0], "fsdp", bw), second]
        ahead.append(f)
        behind.append(b)
    return ahead, behind, send(last(f[0]), "fsdp", fw), send(last(b[1]), "fsdp", bw)


def halves_scatter(ahead, behind, far, fw, bw, wait=lambda a: a, seen=None):
    out = []
    for terms, pairs, whole in ((ahead, fw, 0), (behind, bw, 1)):
        got = [None, None]
        for half in (whole, 1 - whole):
            acc = far[half] if half == whole else None
            for term in reversed(terms):
                acc = term[half] if acc is None else add_low(term[half], wait(send(acc, "fsdp", pairs)))
                if seen is not None and half == whole:
                    seen.append(acc)
            got[half] = send(acc, "fsdp", pairs)
        out.append(got)
    return out


def ring_scatter(ahead, behind, top, bottom, fw, bw, put):
    a, b = send(top, "fsdp", fw), send(bottom, "fsdp", bw)
    for step, (to_fw, to_bw) in enumerate(zip(reversed(ahead), reversed(behind))):
        if step == 0:
            a, b = put(to_fw, a, 0), put(to_bw, b, 1)
        else:
            a, b = add_low(jnp.concatenate(to_fw), a), add_low(jnp.concatenate(to_bw), b)
        a, b = send(a, "fsdp", fw), send(b, "fsdp", bw)
    return a, b


def after(x, *done):
    return lax.optimization_barrier((x,) + done)[0]


def per_device(
    tokens, pad_mask, routes, ln1_gain, w_qkv, w_proj, ln2_gain, w_router, exp_in, exp_out, cotangent
):
    n = lax.axis_size("fsdp")
    per_device_images, seg, width = tokens.shape
    seq_idx = lax.axis_index("seq")
    own = seq_idx.astype(jnp.int32).reshape(1)
    idx = lax.axis_index("fsdp")
    m = n // 2
    fw8, bw8 = ring_pairs([ring_order(n)])
    low_ring = ring_order(m)
    fw4, bw4 = ring_pairs([low_ring, [m + i for i in low_ring]])
    pair = [(i, (i + m) % n) for i in range(n)]
    by_core = [(i, i ^ 1) for i in range(4)]
    by_half = [(i, i ^ 2) for i in range(4)]

    rows = w_qkv.shape[0]
    small = jnp.concatenate([ln1_gain[:, None], ln2_gain[:, None]], axis=1)
    small = jnp.pad(small, ((0, 0), (0, SMALL - 2))) + jnp.pad(
        w_router, ((0, 0), (8, SMALL - 12))
    )
    block = block_of(own, w_qkv, w_proj, small)
    mid = block.shape[1]

    fr = exp_in.shape[0]
    pick = lambda a: lax.dynamic_index_in_dim(a, seq_idx, 1, False)
    mine = jnp.stack([pick(exp_in), pick(exp_out)]).astype(BF)
    part = lambda k: mine[:, k * fr // 2 : (k + 1) * fr // 2]

    keep = pad_mask.astype(BF)[..., None]
    code = pad_mask + 2 * routes[..., 0] + 8 * routes[..., 1]
    code = jnp.pad(code.astype(BF)[..., None], ((0, 0), (0, 0), (0, 127)))
    fused = jnp.concatenate([tokens * keep, cotangent * keep, code], axis=2)
    images = per_device_images // 4
    half_img = images // 2
    fused = fused.reshape(4, images, seg, 2 * width + 128)
    by_seq = [[(i, i ^ r) for i in range(4)] for r in range(4)]
    pieces = [lax.dynamic_index_in_dim(fused, seq_idx ^ r, 0, False) for r in range(4)]
    swap = lambda parts: [parts[0]] + [send(parts[r], "seq", by_seq[r]) for r in (3, 2, 1)][::-1]
    tok, codes, cot = unpack(own, swap(pieces), width)

    base = jnp.where(idx < m, 0, m)
    spot = idx - base
    place = jnp.where(spot % 2 == 0, spot // 2, m - 1 - spot // 2)

    def member(p):
        p = p % m
        return jnp.where(p < m // 2, 2 * p, 2 * (m - 1 - p) + 1)

    chunk = jnp.stack([block, send(block, "fsdp", pair)])
    ahead, behind, top, bottom = ring_gather(
        chunk, m, fw4, bw4, lambda a: after((a[:1], a[1:]), tok)
    )
    q0 = send(after(mine, chunk), "fsdp", pair)

    pieces, offs = [chunk], [idx, (idx + m) % n]
    for d in range(1, m // 2):
        for got, i in ((ahead, member(place - d + m)), (behind, member(place + d))):
            pieces.append(got[d - 1])
            offs += [base + i, m - base + i]
    far_member = member(place + m // 2)
    pieces += [top, bottom]
    offs += [base + far_member, m - base + far_member]
    offs = jnp.stack(offs).astype(jnp.int32) * rows
    w_mine = gather_rows(pieces, offs, (n * rows, mid))
    w_other = send(w_mine, "seq", by_core)

    late_in, late_out = after((exp_in, exp_out), q0)
    win = late_in.transpose(1, 0, 2).astype(BF)
    wout = late_out.transpose(1, 0, 2).astype(BF)
    *n2, res, qkv, ctx, w, gains, wr = attn_fwd(own, tok, codes, w_mine, w_other)
    g_ahead, g_behind, g_top, g_bottom = ring_gather(
        after(cot, top, bottom),
        m,
        fw4,
        bw4,
        lambda a: after((a[:half_img], a[half_img:]), *n2),
    )
    q2 = send(q0, "seq", by_half)
    quarters = [q0, send(q0, "seq", by_core), q2, send(q2, "seq", by_core)]

    win, wout, wint, woutt = weights(own, win, wout, quarters)
    units = images * m
    bufs, at = None, 0

    def experts(xs, gs):
        nonlocal at, bufs
        *dd, b0, b1, b2, b3 = moe_call(
            xs, gs, own, wr, win, wout, wint, at, units, bufs
        )
        bufs = [b0, b1, b2, b3]
        at += images
        return dd

    d_own = experts(n2, [(cot, 0), (cot, half_img)])
    x_ahead, x_behind, x_top, x_bottom = halves_gather(
        n2, m, fw4, bw4, lambda a: after(a, *d_own)
    )
    dx_ahead, dx_behind, where = [], [], []
    for d in range(m // 2 - 1):
        (xa, xb), (ga, gb) = (x_ahead[d], x_behind[d]), (g_ahead[d], g_behind[d])
        where.append(at)
        back0, on1 = experts([xa[0], xb[1]], [(ga, 0), (gb, half_img)])
        back1, on0 = experts([xa[1], xb[0]], [(ga, half_img), (gb, 0)])
        dx_ahead.append([on0, on1])
        dx_behind.append([back0, back1])
    far_at = at
    far = experts([x_top, x_bottom], [(g_top, 0), (g_bottom, 0)])
    ga, hg, xb, gb = bufs

    grad3 = moe_grad(ga, hg, xb, gb, 3)
    grad2 = moe_grad(after(ga, grad3), hg, xb, gb, 2)
    grad1 = moe_grad(after(ga, grad2), hg, xb, gb, 1)
    seen = []
    d1, d2 = halves_scatter(
        dx_ahead, dx_behind, far, fw4, bw4, lambda a: after(a, grad1), seen
    )
    kept2 = add_low(grad2, send(grad3, "seq", by_core))
    grad0 = moe_grad(after(ga, *seen), hg, xb, gb, 0)
    kept0 = add_low(grad0, send(grad1, "seq", by_core))
    outs = moe_out(woutt, after(ga, grad0))
    first_half = send(kept2[1], "seq", by_half)
    d_own = [after(d_own[0], grad0), d_own[1]]

    *gtok, dw_keep, dw_give = attn_bwd(
        own, d_own, d1, d2, n2, cot, res, ctx, qkv, tok, codes, w, gains, wr
    )

    outs = after(outs, *d1, *d2)
    out_at = lambda k: outs[k : k + half_img]
    o_ahead = [[out_at(k + 3 * half_img), out_at(k + half_img)] for k in where]
    o_behind = [[out_at(k), out_at(k + 2 * half_img)] for k in where]
    firsts = []

    def hold(a):
        firsts.append(a)
        return after(a, dw_keep)

    o1, o2 = halves_scatter(
        o_ahead, o_behind, (out_at(far_at), out_at(far_at + half_img)), fw4, bw4, hold
    )
    kept_pair = add_low(kept0[1], after(first_half, dw_keep))
    from_pair = send(kept_pair, "fsdp", pair)

    dw_give = after(dw_give, first_half, *firsts[: 2 if m == 4 else 0])
    dw = add_low(dw_keep, send(dw_give, "seq", by_core))

    def term(i):
        cut = lambda k: lax.dynamic_slice_in_dim(dw, k * rows, rows, 0)[None]
        return [cut(base + i), cut(m - base + i)]

    def put_part(t, part, side):
        t = list(t)
        t[side] = add_low(t[side], part)
        return jnp.concatenate(t)

    last = term(far_member)
    s1, s2 = ring_scatter(
        [term(member(place + d)) for d in range(1, m // 2)],
        [term(member(place - d + m)) for d in range(1, m // 2)],
        last[0],
        last[1],
        fw4,
        bw4,
        put_part,
    )
    low = lambda a: a.astype(F32)
    mine_t, pair_t = term(spot)
    for_pair = (low(pair_t) + low(s1[1:]) + low(s2[1:])).astype(BF)
    dense = (low(mine_t) + low(s1[:1]) + low(s2[:1]) + low(send(for_pair, "fsdp", pair)))[0].astype(BF)
    dense = add_low(dense, send(dense, "seq", by_half))
    g_qkv, g_proj, g_small = finish(own, dense, send(dense, "seq", by_core), width)

    grad_tokens = gather_images(own, swap([after(g, s1) for g in gtok]), F32)
    block_out = gather_images(own, swap(result(own, outs, o1, o2, res, codes)), BF)

    from_half = after(send(kept2[0], "seq", by_half), dw_keep)
    quarter = add_low(add_low(kept0[0], from_half), from_pair)
    from_half = send(quarter, "seq", by_half)
    grad_in, grad_out = pack(
        own,
        [quarter, send(quarter, "seq", by_core), from_half, send(from_half, "seq", by_core)],
    )

    return (
        block_out,
        grad_tokens,
        g_small[:, 0],
        g_qkv,
        g_proj,
        g_small[:, 1],
        g_small[:, 8:12],
        grad_in,
        grad_out,
    )


def solution(mesh):
    row = P("fsdp", None)
    cube = P("fsdp", None, None)
    split = P("fsdp", "seq", None)
    return jax.shard_map(
        per_device,
        mesh=mesh,
        in_specs=(
            split,
            P("fsdp", "seq"),
            split,
            P("fsdp"),
            row,
            row,
            P("fsdp"),
            row,
            cube,
            cube,
            split,
        ),
        out_specs=(split, split, P("fsdp"), row, row, P("fsdp"), row, cube, cube),
        check_vma=False,
    )
```
